512 devices in a mesh: row: 16 (over z, core), col: 32 (over y, x).
Axes of the slice: x: 4, y: 8, z: 8, core: 2. Of those that a mesh axis runs over, the one named last changes fastest.
Arguments:
- tokens: bfloat16 [4096, 2560], P('row', 'col'), may hold values from -6 to 6
- w_down: bfloat16 [2560, 1056], P('col'), may hold values from -0.125 to 0.125
- q_gain: float32 [768], replicated, may hold values from 0.1 to 1.9
- kv_gain: float32 [256], replicated, may hold values from 0.1 to 1.9
- w_q_up: bfloat16 [768, 3072], P(None, 'col'), may hold values from -8.8767604 to 8.8767604
- w_kv_up: bfloat16 [256, 4096], replicated, may hold values from -0.375 to 0.375
- w_out: bfloat16 [2048, 2560], P('col'), may hold values from -0.75 to 0.75
- latent_cache: bfloat16 [16, 8192, 288], P('row', 'col'), may hold values from -6 to 6
- cache_len: int32 [16], replicated, may hold values from 1 to 8192, as said below
- new_len: int32 [16], replicated, may hold values from 1 to 256, as said below
- page_table: int32 [16, 128], replicated, may hold values from 0 to 127, each once within a row
- home_slot: int32 [16], replicated, may hold values from 0 to 15, each once
Outputs:
- output: bfloat16 [4096, 2560], P('row', 'col')
The draws below stay inside these ranges and needn't reach their ends.
Inputs may be any that keep to these rules, and one draw needn't show every extreme that they name: `cache_len`: some slot has exactly 8192 cached tokens; about half the slots hold at most 1024, the others at least 7168. `new_len`: some request has exactly 256 real new tokens.
All inputs are finite; a program needn't handle non-finite values.
Results may differ from the reference program's by a relative error of at most 0.023.
Values may be sent and summed in bfloat16 or wider, within the bound.
A program may use at most 64 MiB of HBM per device.

```python
import math
import jax
import jax.numpy as jnp
from jax import lax

D = 2560
QR = 768
KR = 256
NOPE = 64
ROPE = 32
VDIM = 64
GROUP = 256
PAGE = 64
HEADS = 32
R = 16
NPAGE = 128
MAXC = 8192
TOKENS = 4096


def draw_w_q_up(key, part):
    key_base = jax.random.fold_in(key, 11)
    base_draw = jnp.clip(jax.random.normal(key_base, (QR, HEADS * (NOPE + ROPE)), jnp.float32), -6.0, 6.0) * QR ** (-0.5)
    return base_draw.astype(jnp.bfloat16)


def draw_cache_len(key, part):
    key_short = jax.random.fold_in(key, 21)
    key_long = jax.random.fold_in(key, 22)
    key_pick = jax.random.fold_in(key, 23)
    key_fill = jax.random.fold_in(key, 24)
    shorter = jax.random.randint(key_short, (R,), 1, MAXC // 8 + 1)
    longer = MAXC - jax.random.randint(key_long, (R,), 0, MAXC // 8 + 1)
    picked = jax.random.randint(key_pick, (R,), 0, 2)
    lengths = jnp.where(picked == 1, longer, shorter)
    fullest = jax.random.randint(key_fill, (), 0, R)
    return jnp.where(jnp.arange(R) == fullest, MAXC, lengths).astype(jnp.int32)


def draw_new_len(key, part):
    key_length = jax.random.fold_in(key, 31)
    key_fill = jax.random.fold_in(key, 32)
    lengths = jax.random.randint(key_length, (R,), GROUP // 4 + 1, GROUP + 1)
    fullest = jax.random.randint(key_fill, (), 0, R)
    return jnp.where(jnp.arange(R) == fullest, GROUP, lengths).astype(jnp.int32)


def levels(rng, dims, split, least, largest):
    def one(axis_at, blocks):
        heights = jax.random.uniform(jax.random.fold_in(jax.random.fold_in(rng, 6), axis_at), (blocks,), jnp.float32, least / len(split), largest / len(split))
        return jnp.repeat(jnp.exp(heights), dims[axis_at] // blocks).reshape((-1,) + (1,) * (len(dims) - axis_at - 1))

    loudness = one(*split[0])
    for cut in split[1:]:
        loudness = loudness * one(*cut)
    return loudness


def normal_values(own_key, dims, deviation, reach, shards=(), held_as=jnp.bfloat16):
    level = levels(own_key, dims, shards, -0.22, 0.18) if shards else 1.0
    entries = jax.random.normal(own_key, dims, jnp.float32) * deviation * level
    return jnp.minimum(jnp.maximum(entries, -reach), reach).astype(held_as)


def setup_inputs(seed: int = 0) -> dict:
    seeds = jax.random.split(jax.random.key(seed), 13)
    return {
        "tokens": normal_values(seeds[0], (TOKENS, D), 1.0, 6.0, ((0, 16), (1, 32))),
        "w_down": normal_values(seeds[1], (D, QR + KR + ROPE), D ** -0.5, 0.125, ((0, 32),)),
        "q_gain": jnp.clip(1.0 + 0.18 * jax.random.normal(seeds[2], (QR,), jnp.float32), 0.1, 1.9),
        "kv_gain": jnp.clip(1.0 + 0.18 * jax.random.normal(seeds[3], (KR,), jnp.float32), 0.1, 1.9),
        "w_q_up": draw_w_q_up(jax.random.fold_in(seeds[12], 71), 0),
        "w_kv_up": normal_values(seeds[5], (KR, HEADS * (NOPE + VDIM)), KR ** -0.5, 0.375),
        "w_out": normal_values(seeds[6], (HEADS * VDIM, D), VDIM ** -0.5, 0.75, ((0, 32),)),
        "latent_cache": normal_values(seeds[7], (R, MAXC, KR + ROPE), 1.0, 6.0, ((0, 16), (1, 32))),
        "cache_len": draw_cache_len(jax.random.fold_in(seeds[12], 71), 0),
        "new_len": draw_new_len(jax.random.fold_in(seeds[12], 71), 0),
        "page_table": jax.vmap(lambda own: jax.random.permutation(own, NPAGE))(jax.random.split(seeds[10], R)).reshape((R, NPAGE)).astype(jnp.int32),
        "home_slot": jax.random.permutation(seeds[11], R).astype(jnp.int32),
    }


epsilon = 1e-05

def rms_scale(values, gain):
    return values * lax.rsqrt(lax.optimization_barrier(jnp.mean(values * values, axis=-1, keepdims=True)) + epsilon) * gain

def angle_tables(positions, width):
    half_dim = width // 2
    frequency = 10000.0 ** (-2.0 * jnp.arange(half_dim, dtype=jnp.float32) / width)
    angles = positions.astype(jnp.float32)[:, None] * frequency[None, :]
    return (jnp.cos(angles), jnp.sin(angles))

def rotary(values, cosine, sine_table):
    half_dim = values.shape[-1] // 2
    first_half = values[..., :half_dim]
    second_half = values[..., half_dim:]
    return jnp.concatenate([first_half * cosine - second_half * sine_table, second_half * cosine + first_half * sine_table], -1)

def reference(tokens, w_down, q_gain, kv_gain, w_q_up, w_kv_up, w_out, latent_cache, cache_len, new_len, page_table, home_slot):
    combined = jnp.dot(tokens, w_down, preferred_element_type=jnp.float32)
    block_of = jnp.arange(TOKENS, dtype=jnp.int32) // GROUP
    within = jnp.arange(TOKENS, dtype=jnp.int32) % GROUP
    position = cache_len[home_slot[block_of]] + within
    cosine, sine_table = angle_tables(position, ROPE)
    query_latent = rms_scale(combined[:, :QR], q_gain).astype(jnp.bfloat16)
    new_latent = rms_scale(combined[:, QR:QR + KR], kv_gain).astype(jnp.bfloat16)
    new_rope = rotary(combined[:, QR + KR:], cosine, sine_table).astype(jnp.bfloat16)
    projected = jnp.dot(query_latent, w_q_up, preferred_element_type=jnp.float32).reshape(TOKENS, HEADS, NOPE + ROPE)
    queries = jnp.concatenate([projected[..., :NOPE], rotary(projected[..., NOPE:], cosine[:, None, :], sine_table[:, None, :])], -1).astype(jnp.bfloat16)
    new_rows = jnp.concatenate([new_latent, new_rope], 1)
    score_scale = 1.0 / math.sqrt(NOPE + ROPE)
    key_count = MAXC + GROUP
    outputs = []
    for block_id in range(R):
        slot_index = home_slot[block_id]
        latents = jnp.concatenate([latent_cache[slot_index], new_rows[block_id * GROUP:(block_id + 1) * GROUP]], 0)
        lifted = jnp.dot(latents[:, :KR], w_kv_up, preferred_element_type=jnp.float32).astype(jnp.bfloat16).reshape(key_count, HEADS, NOPE + VDIM)
        key_rows = jnp.concatenate([lifted[..., :NOPE], jnp.broadcast_to(latents[:, None, KR:], (key_count, HEADS, ROPE))], -1)
        values = lifted[..., NOPE:]
        page_row = page_table[slot_index]
        page_ids = jnp.arange(NPAGE, dtype=jnp.int32)
        logical_page = lax.optimization_barrier(jnp.sum(page_ids[:, None] * (page_row[:, None] == page_ids[None, :]).astype(jnp.int32), 0))
        logical = (logical_page[:, None] * PAGE + jnp.arange(PAGE, dtype=jnp.int32)[None, :]).reshape(MAXC)
        cached_seen = logical < cache_len[slot_index]
        query_index = jnp.arange(GROUP, dtype=jnp.int32)[:, None]
        key_index = jnp.arange(GROUP, dtype=jnp.int32)[None, :]
        new_seen = (key_index <= query_index) & (key_index < new_len[block_id])
        visible = jnp.concatenate([jnp.broadcast_to(cached_seen[None, :], (GROUP, MAXC)), new_seen], 1)
        block_query = queries[block_id * GROUP:(block_id + 1) * GROUP].astype(jnp.float32)
        scores = jnp.einsum('qhd,khd->hqk', block_query, key_rows.astype(jnp.float32)) * score_scale
        scores = jnp.where(visible[None], scores, -jnp.inf)
        row_peak = lax.optimization_barrier(jnp.max(scores, -1, keepdims=True))
        exponent = jnp.exp(scores - row_peak)
        row_total = lax.optimization_barrier(jnp.sum(exponent, -1))
        weights = exponent.astype(jnp.bfloat16)
        summed = jnp.einsum('hqk,khd->qhd', weights.astype(jnp.float32), values.astype(jnp.float32))
        attended = (summed / row_total.T[:, :, None]).astype(jnp.bfloat16)
        live_rows = jnp.arange(GROUP, dtype=jnp.int32) < new_len[block_id]
        attended = jnp.where(live_rows[:, None, None], attended, jnp.zeros_like(attended))
        outputs.append(attended.reshape(GROUP, HEADS * VDIM))
    attended_all = jnp.concatenate(outputs, 0)
    return jnp.dot(attended_all, w_out, preferred_element_type=jnp.float32).astype(jnp.bfloat16)
```

```python
import math

import jax
import jax.numpy as jnp
from jax import lax
from jax.sharding import PartitionSpec as P

NOPE = 64
ROPE = 32
VDIM = 64


epsilon = 1e-05


def rms_scale(values, gain):
    return values * lax.rsqrt(jnp.mean(values * values, axis=-1, keepdims=True) + epsilon) * gain


def angle_tables(positions, width):
    half_dim = width // 2
    frequency = 10000.0 ** (-2.0 * jnp.arange(half_dim, dtype=jnp.float32) / width)
    angles = positions.astype(jnp.float32)[:, None] * frequency[None, :]
    return (jnp.cos(angles), jnp.sin(angles))


def rotary(values, cosine, sine_table):
    half_dim = values.shape[-1] // 2
    first_half = values[..., :half_dim]
    second_half = values[..., half_dim:]
    return jnp.concatenate(
        [
            first_half * cosine - second_half * sine_table,
            second_half * cosine + first_half * sine_table,
        ],
        -1,
    )


def body(
    tokens,
    w_down,
    q_gain,
    kv_gain,
    w_q_up,
    w_kv_up,
    w_out,
    latent_cache,
    cache_len,
    new_len,
    page_table,
    home_slot,
):
    columns = lax.axis_size("col")
    column_id = lax.axis_index("col")
    row_id = lax.axis_index("row")
    group_rows = tokens.shape[0]
    own_rows = group_rows // columns
    q_width = q_gain.shape[0]
    kv_width = kv_gain.shape[0]
    slot_index = home_slot[row_id]
    cached_count = cache_len[slot_index]
    live_count = new_len[row_id]
    combined = lax.psum(
        jnp.dot(tokens, w_down, preferred_element_type=jnp.float32), "col"
    )
    query_cos, query_sin = angle_tables(
        cached_count + jnp.arange(group_rows, dtype=jnp.int32), ROPE
    )
    query_latent = rms_scale(combined[:, :q_width], q_gain).astype(jnp.bfloat16)
    new_latent = rms_scale(combined[:, q_width : q_width + kv_width], kv_gain).astype(jnp.bfloat16)
    new_rope = rotary(combined[:, q_width + kv_width :], query_cos, query_sin).astype(jnp.bfloat16)
    fresh_latents = jnp.concatenate([new_latent, new_rope], 1)
    projected = jnp.dot(query_latent, w_q_up, preferred_element_type=jnp.float32)
    queries = jnp.concatenate(
        [projected[:, :NOPE], rotary(projected[:, NOPE:], query_cos, query_sin)], 1
    ).astype(jnp.bfloat16)
    segment = lax.all_gather(latent_cache, "row", axis=0, tiled=True)
    matches = jnp.arange(segment.shape[0], dtype=jnp.int32) == slot_index
    own_cache = jnp.sum(
        jnp.where(matches[:, None, None], segment.astype(jnp.float32), 0.0), 0
    ).astype(jnp.bfloat16)
    head_width = NOPE + VDIM
    head_weight = lax.dynamic_slice_in_dim(w_kv_up, column_id * head_width, head_width, 1)

    def expand(latents):
        lifted = jnp.dot(
            latents[:, :kv_width], head_weight, preferred_element_type=jnp.float32
        ).astype(jnp.bfloat16)
        return (jnp.concatenate([lifted[:, :NOPE], latents[:, kv_width:]], 1), lifted[:, NOPE:])

    cache_latents = lax.all_gather(own_cache, "col", axis=0, tiled=True)
    cache_keys, cache_values = expand(cache_latents)
    fresh_keys, fresh_values = expand(fresh_latents)
    key_total = cache_keys.shape[0]
    page_row = page_table[slot_index]
    page_count = page_row.shape[0]
    page_size = key_total // page_count
    block_size = min(512, key_total)
    offsets = jnp.arange(page_size, dtype=jnp.int32)
    page_ids = jnp.arange(page_count, dtype=jnp.int32)
    logical_page = jnp.sum(
        page_ids[:, None] * (page_row[:, None] == page_ids[None, :]).astype(jnp.int32), 0
    )
    cached_visible = (logical_page[:, None] * page_size + offsets[None, :]).reshape(
        key_total
    ) < cached_count
    block_limit = key_total // block_size
    score_scale = 1.0 / math.sqrt(NOPE + ROPE)
    query_index = jnp.arange(group_rows, dtype=jnp.int32)[:, None]
    key_index = jnp.arange(group_rows, dtype=jnp.int32)[None, :]
    fresh_visible = (key_index <= query_index) & (key_index < live_count)
    fresh_scores = (
        jnp.einsum("qd,kd->qk", queries, fresh_keys, preferred_element_type=jnp.float32)
        * score_scale
    )
    fresh_scores = jnp.where(fresh_visible, fresh_scores, -jnp.inf)
    first_peak = jnp.max(fresh_scores, 1)
    fresh_exponent = jnp.exp(fresh_scores - first_peak[:, None])
    start_state = (
        first_peak,
        jnp.sum(fresh_exponent, 1),
        jnp.dot(
            fresh_exponent.astype(jnp.bfloat16), fresh_values, preferred_element_type=jnp.float32
        ),
    )

    def accumulate(block_id, running):
        row_peak, row_total, summed = running
        key_block = lax.dynamic_slice_in_dim(cache_keys, block_id * block_size, block_size, 0)
        mask_block = lax.dynamic_slice_in_dim(cached_visible, block_id * block_size, block_size, 0)
        value_block = lax.dynamic_slice_in_dim(cache_values, block_id * block_size, block_size, 0)
        raw_scores = (
            jnp.einsum("qd,kd->qk", queries, key_block, preferred_element_type=jnp.float32)
            * score_scale
        )
        raw_scores = jnp.where(mask_block[None, :], raw_scores, -jnp.inf)
        next_peak = jnp.maximum(row_peak, jnp.max(raw_scores, 1))
        factor = jnp.exp(row_peak - next_peak)
        exponent = jnp.exp(raw_scores - next_peak[:, None])
        next_total = row_total * factor + jnp.sum(exponent, 1)
        next_summed = summed * factor[:, None] + jnp.dot(
            exponent.astype(jnp.bfloat16), value_block, preferred_element_type=jnp.float32
        )
        return (next_peak, next_total, next_summed)

    row_peak, row_total, summed = lax.fori_loop(0, block_limit, accumulate, start_state)
    attended = (summed / row_total[:, None]).astype(jnp.bfloat16)
    live_rows = jnp.arange(group_rows, dtype=jnp.int32) < live_count
    attended = jnp.where(live_rows[:, None], attended, jnp.zeros_like(attended))
    summed_out = lax.psum_scatter(
        lax.dot_general(
            w_out, attended, (((0,), (1,)), ((), ())), preferred_element_type=jnp.float32
        ).astype(jnp.bfloat16),
        "col",
        scatter_dimension=0,
        tiled=True,
    ).astype(jnp.float32)
    result = summed_out.T.astype(jnp.bfloat16)
    return result


def solution(mesh):
    return jax.shard_map(
        body,
        mesh=mesh,
        in_specs=(
            P("row", "col"),
            P("col", None),
            P(),
            P(),
            P(None, "col"),
            P(),
            P("col", None),
            P("row", "col", None),
            P(),
            P(),
            P(),
            P(),
        ),
        out_specs=P("row", "col"),
        check_vma=False,
    )
```

```python
import functools
import math

import jax
import jax.numpy as jnp
from jax import lax
from jax.experimental import pallas as pl
from jax.experimental.pallas import tpu as pltpu
from jax.sharding import PartitionSpec as P

MESH = pl.DeviceIdType.MESH

NOPE = 64
ROPE = 32
VDIM = 64


epsilon = 1e-05


def rms_scale(values, gain):
    return values * lax.rsqrt(jnp.mean(values * values, axis=-1, keepdims=True) + epsilon) * gain


def angle_tables(positions, width):
    half_dim = width // 2
    frequency = 10000.0 ** (-2.0 * jnp.arange(half_dim, dtype=jnp.float32) / width)
    angles = positions.astype(jnp.float32)[:, None] * frequency[None, :]
    return (jnp.cos(angles), jnp.sin(angles))


def rotary(values, cosine, sine_table):
    half_dim = values.shape[-1] // 2
    first_half = values[..., :half_dim]
    second_half = values[..., half_dim:]
    return jnp.concatenate(
        [
            first_half * cosine - second_half * sine_table,
            second_half * cosine + first_half * sine_table,
        ],
        -1,
    )


def _exchange_kernel(n, axis, gather, x_ref, y_ref, send_sem, recv_sem):
    me = lax.axis_index(axis)
    barrier = pltpu.get_barrier_semaphore()
    for k in range(1, n):
        pl.semaphore_signal(
            barrier, inc=1, device_id={axis: lax.rem(me + k, n)}, device_id_type=MESH
        )
    pl.semaphore_wait(barrier, n - 1)
    sends = []
    for k in range(1, n):
        peer = lax.rem(me + k, n)
        copy = pltpu.make_async_remote_copy(
            src_ref=x_ref if gather else x_ref.at[peer],
            dst_ref=y_ref.at[me],
            send_sem=send_sem.at[k],
            recv_sem=recv_sem.at[k],
            device_id={axis: peer},
            device_id_type=MESH,
        )
        copy.start()
        sends.append(copy)
    if gather:
        y_ref[me] = x_ref[...]
    else:
        y_ref[me] = x_ref[me]
    for copy in sends:
        copy.wait_send()
    for k in range(1, n):
        source = lax.rem(me + n - k, n)
        pltpu.make_async_remote_copy(
            src_ref=x_ref if gather else x_ref.at[source],
            dst_ref=y_ref.at[source],
            send_sem=send_sem.at[k],
            recv_sem=recv_sem.at[k],
            device_id={axis: source},
            device_id_type=MESH,
        ).wait_recv()


def exchange(x, axis, gather, collective_id):
    n = lax.axis_size(axis)
    shape = ((n,) + x.shape) if gather else x.shape
    return pl.pallas_call(
        functools.partial(_exchange_kernel, n, axis, gather),
        out_shape=jax.ShapeDtypeStruct(shape, x.dtype),
        in_specs=[pl.BlockSpec(memory_space=pltpu.VMEM)],
        out_specs=pl.BlockSpec(memory_space=pltpu.VMEM),
        scratch_shapes=[pltpu.SemaphoreType.DMA((n,)), pltpu.SemaphoreType.DMA((n,))],
        compiler_params=pltpu.CompilerParams(collective_id=collective_id, has_side_effects=True),
    )(x)


def body(
    tokens,
    w_down,
    q_gain,
    kv_gain,
    w_q_up,
    w_kv_up,
    w_out,
    latent_cache,
    cache_len,
    new_len,
    page_table,
    home_slot,
):
    columns = lax.axis_size("col")
    column_id = lax.axis_index("col")
    row_id = lax.axis_index("row")
    group_rows = tokens.shape[0]
    own_rows = group_rows // columns
    q_width = q_gain.shape[0]
    kv_width = kv_gain.shape[0]
    slot_index = home_slot[row_id]
    cached_count = cache_len[slot_index]
    live_count = new_len[row_id]
    partial_sums = jnp.dot(tokens, w_down, preferred_element_type=jnp.float32)
    pieces = exchange(partial_sums.reshape(columns, own_rows, -1), "col", False, 0)
    combined = jnp.sum(pieces, 0)
    own_position = cached_count + column_id * own_rows + jnp.arange(own_rows, dtype=jnp.int32)
    own_cos, own_sin = angle_tables(own_position, ROPE)
    own_query = rms_scale(combined[:, :q_width], q_gain).astype(jnp.bfloat16)
    own_latent = rms_scale(combined[:, q_width : q_width + kv_width], kv_gain).astype(jnp.bfloat16)
    own_rope = rotary(combined[:, q_width + kv_width :], own_cos, own_sin).astype(jnp.bfloat16)
    own_rows_all = jnp.concatenate([own_query, own_latent, own_rope], 1)
    all_rows = exchange(own_rows_all, "col", True, 1).reshape(group_rows, -1)
    query_latent = all_rows[:, :q_width]
    fresh_latents = all_rows[:, q_width:]
    query_cos, query_sin = angle_tables(
        cached_count + jnp.arange(group_rows, dtype=jnp.int32), ROPE
    )
    projected = jnp.dot(query_latent, w_q_up, preferred_element_type=jnp.float32)
    queries = jnp.concatenate(
        [projected[:, :NOPE], rotary(projected[:, NOPE:], query_cos, query_sin)], 1
    ).astype(jnp.bfloat16)
    segment = lax.all_gather(latent_cache, "row", axis=0, tiled=True)
    matches = jnp.arange(segment.shape[0], dtype=jnp.int32) == slot_index
    own_cache = jnp.sum(
        jnp.where(matches[:, None, None], segment.astype(jnp.float32), 0.0), 0
    ).astype(jnp.bfloat16)
    head_width = NOPE + VDIM
    head_weight = lax.dynamic_slice_in_dim(w_kv_up, column_id * head_width, head_width, 1)

    def expand(latents):
        lifted = jnp.dot(
            latents[:, :kv_width], head_weight, preferred_element_type=jnp.float32
        ).astype(jnp.bfloat16)
        return (jnp.concatenate([lifted[:, :NOPE], latents[:, kv_width:]], 1), lifted[:, NOPE:])

    cache_latents = exchange(own_cache, "col", True, 2).reshape(-1, own_cache.shape[-1])
    cache_keys, cache_values = expand(cache_latents)
    fresh_keys, fresh_values = expand(fresh_latents)
    key_total = cache_keys.shape[0]
    page_row = page_table[slot_index]
    page_count = page_row.shape[0]
    page_size = key_total // page_count
    block_size = min(512, key_total)
    offsets = jnp.arange(page_size, dtype=jnp.int32)
    page_ids = jnp.arange(page_count, dtype=jnp.int32)
    logical_page = jnp.sum(
        page_ids[:, None] * (page_row[:, None] == page_ids[None, :]).astype(jnp.int32), 0
    )
    cached_visible = (logical_page[:, None] * page_size + offsets[None, :]).reshape(
        key_total
    ) < cached_count
    block_limit = key_total // block_size
    score_scale = 1.0 / math.sqrt(NOPE + ROPE)
    query_index = jnp.arange(group_rows, dtype=jnp.int32)[:, None]
    key_index = jnp.arange(group_rows, dtype=jnp.int32)[None, :]
    fresh_visible = (key_index <= query_index) & (key_index < live_count)
    fresh_scores = (
        jnp.einsum("qd,kd->qk", queries, fresh_keys, preferred_element_type=jnp.float32)
        * score_scale
    )
    fresh_scores = jnp.where(fresh_visible, fresh_scores, -jnp.inf)
    first_peak = jnp.max(fresh_scores, 1)
    fresh_exponent = jnp.exp(fresh_scores - first_peak[:, None])
    start_state = (
        first_peak,
        jnp.sum(fresh_exponent, 1),
        jnp.dot(
            fresh_exponent.astype(jnp.bfloat16), fresh_values, preferred_element_type=jnp.float32
        ),
    )

    def accumulate(block_id, running):
        row_peak, row_total, summed = running
        key_block = lax.dynamic_slice_in_dim(cache_keys, block_id * block_size, block_size, 0)
        mask_block = lax.dynamic_slice_in_dim(cached_visible, block_id * block_size, block_size, 0)
        value_block = lax.dynamic_slice_in_dim(cache_values, block_id * block_size, block_size, 0)
        raw_scores = (
            jnp.einsum("qd,kd->qk", queries, key_block, preferred_element_type=jnp.float32)
            * score_scale
        )
        raw_scores = jnp.where(mask_block[None, :], raw_scores, -jnp.inf)
        next_peak = jnp.maximum(row_peak, jnp.max(raw_scores, 1))
        factor = jnp.exp(row_peak - next_peak)
        exponent = jnp.exp(raw_scores - next_peak[:, None])
        next_total = row_total * factor + jnp.sum(exponent, 1)
        next_summed = summed * factor[:, None] + jnp.dot(
            exponent.astype(jnp.bfloat16), value_block, preferred_element_type=jnp.float32
        )
        return (next_peak, next_total, next_summed)

    row_peak, row_total, summed = lax.fori_loop(0, block_limit, accumulate, start_state)
    attended = (summed / row_total[:, None]).astype(jnp.bfloat16)
    live_rows = jnp.arange(group_rows, dtype=jnp.int32) < live_count
    attended = jnp.where(live_rows[:, None], attended, jnp.zeros_like(attended))
    out_parts = lax.dot_general(
        w_out, attended, (((0,), (1,)), ((), ())), preferred_element_type=jnp.float32
    ).astype(jnp.bfloat16)
    out_pieces = exchange(out_parts.reshape(columns, -1, group_rows), "col", False, 3)
    summed_out = jnp.sum(out_pieces.astype(jnp.float32), 0)
    result = summed_out.T.astype(jnp.bfloat16)
    return result


def solution(mesh):
    return jax.shard_map(
        body,
        mesh=mesh,
        in_specs=(
            P("row", "col"),
            P("col", None),
            P(),
            P(),
            P(None, "col"),
            P(),
            P("col", None),
            P("row", "col", None),
            P(),
            P(),
            P(),
            P(),
        ),
        out_specs=P("row", "col"),
        check_vma=False,
    )
```

```python
import functools
import math

import jax
import jax.numpy as jnp
from jax import lax
from jax.experimental import pallas as pl
from jax.experimental.pallas import tpu as pltpu
from jax.sharding import PartitionSpec as P

MESH = pl.DeviceIdType.MESH

NOPE = 64
ROPE = 32
VDIM = 64


epsilon = 1e-05


def rms_scale(values, gain):
    return values * lax.rsqrt(jnp.mean(values * values, axis=-1, keepdims=True) + epsilon) * gain


def angle_tables(positions, width):
    half_dim = width // 2
    frequency = 10000.0 ** (-2.0 * jnp.arange(half_dim, dtype=jnp.float32) / width)
    angles = positions.astype(jnp.float32)[:, None] * frequency[None, :]
    return (jnp.cos(angles), jnp.sin(angles))


def rotary(values, cosine, sine_table):
    half_dim = values.shape[-1] // 2
    first_half = values[..., :half_dim]
    second_half = values[..., half_dim:]
    return jnp.concatenate(
        [
            first_half * cosine - second_half * sine_table,
            second_half * cosine + first_half * sine_table,
        ],
        -1,
    )


def _exchange_kernel(n, axis, modes, *refs):
    count = len(modes)
    sources, targets = refs[:count], refs[count : 2 * count]
    send_sem, recv_sem = refs[2 * count :]
    me = lax.axis_index(axis)
    barrier = pltpu.get_barrier_semaphore()
    for k in range(1, n):
        pl.semaphore_signal(
            barrier, inc=1, device_id={axis: lax.rem(me + k, n)}, device_id_type=MESH
        )
    pl.semaphore_wait(barrier, n - 1)

    def remote(a, k, peer, landing):
        x_ref = sources[a]
        return pltpu.make_async_remote_copy(
            src_ref=x_ref if modes[a] else x_ref.at[peer],
            dst_ref=targets[a].at[landing],
            send_sem=send_sem.at[a, k],
            recv_sem=recv_sem.at[a, k],
            device_id={axis: peer},
            device_id_type=MESH,
        )

    sends = []
    for k in range(1, n):
        for a in range(count):
            copy = remote(a, k, lax.rem(me + k, n), me)
            copy.start()
            sends.append(copy)
    for a in range(count):
        if modes[a]:
            targets[a][me] = sources[a][...]
        else:
            targets[a][me] = sources[a][me]
    for copy in sends:
        copy.wait_send()
    for k in range(1, n):
        source = lax.rem(me + n - k, n)
        for a in range(count):
            remote(a, k, source, source).wait_recv()


def exchange(arrays, modes, axis, collective_id):
    n = lax.axis_size(axis)
    shapes = [
        jax.ShapeDtypeStruct(((n,) + x.shape) if gather else x.shape, x.dtype)
        for x, gather in zip(arrays, modes)
    ]
    return pl.pallas_call(
        functools.partial(_exchange_kernel, n, axis, tuple(modes)),
        out_shape=shapes,
        in_specs=[pl.BlockSpec(memory_space=pltpu.VMEM)] * len(arrays),
        out_specs=[pl.BlockSpec(memory_space=pltpu.VMEM)] * len(arrays),
        scratch_shapes=[
            pltpu.SemaphoreType.DMA((len(arrays), n)),
            pltpu.SemaphoreType.DMA((len(arrays), n)),
        ],
        compiler_params=pltpu.CompilerParams(collective_id=collective_id, has_side_effects=True),
    )(*arrays)


def body(
    tokens,
    w_down,
    q_gain,
    kv_gain,
    w_q_up,
    w_kv_up,
    w_out,
    latent_cache,
    cache_len,
    new_len,
    page_table,
    home_slot,
):
    columns = lax.axis_size("col")
    column_id = lax.axis_index("col")
    row_id = lax.axis_index("row")
    group_rows = tokens.shape[0]
    own_rows = group_rows // columns
    q_width = q_gain.shape[0]
    kv_width = kv_gain.shape[0]
    slot_index = home_slot[row_id]
    cached_count = cache_len[slot_index]
    live_count = new_len[row_id]
    partial_sums = jnp.dot(tokens, w_down, preferred_element_type=jnp.float32)
    (pieces,) = exchange([partial_sums.reshape(columns, own_rows, -1)], [False], "col", 0)
    combined = jnp.sum(pieces, 0)
    own_position = cached_count + column_id * own_rows + jnp.arange(own_rows, dtype=jnp.int32)
    own_cos, own_sin = angle_tables(own_position, ROPE)
    own_query = rms_scale(combined[:, :q_width], q_gain).astype(jnp.bfloat16)
    own_latent = rms_scale(combined[:, q_width : q_width + kv_width], kv_gain).astype(jnp.bfloat16)
    own_rope = rotary(combined[:, q_width + kv_width :], own_cos, own_sin).astype(jnp.bfloat16)
    own_rows_all = jnp.concatenate([own_query, own_latent, own_rope], 1)
    (all_rows,) = exchange([own_rows_all], [True], "col", 1)
    all_rows = all_rows.reshape(group_rows, -1)
    query_latent = all_rows[:, :q_width]
    fresh_latents = all_rows[:, q_width:]
    query_cos, query_sin = angle_tables(
        cached_count + jnp.arange(group_rows, dtype=jnp.int32), ROPE
    )
    projected = jnp.dot(query_latent, w_q_up, preferred_element_type=jnp.float32)
    queries = jnp.concatenate(
        [projected[:, :NOPE], rotary(projected[:, NOPE:], query_cos, query_sin)], 1
    ).astype(jnp.bfloat16)
    segment = lax.all_gather(latent_cache, "row", axis=0, tiled=True)
    matches = jnp.arange(segment.shape[0], dtype=jnp.int32) == slot_index
    own_cache = jnp.sum(
        jnp.where(matches[:, None, None], segment.astype(jnp.float32), 0.0), 0
    ).astype(jnp.bfloat16)
    head_width = NOPE + VDIM
    head_weight = lax.dynamic_slice_in_dim(w_kv_up, column_id * head_width, head_width, 1)
    chunk = own_cache.shape[0]
    own_lifted = (
        jnp.dot(own_cache[:, :kv_width], w_kv_up, preferred_element_type=jnp.float32)
        .astype(jnp.bfloat16)
        .reshape(chunk, columns, head_width)
        .transpose(1, 0, 2)
    )
    lifted_parts, rope_parts = exchange(
        [own_lifted, own_cache[:, kv_width:].T], [False, True], "col", 2
    )
    key_total = columns * chunk
    lifted_parts = lifted_parts.reshape(key_total, head_width)
    fresh_lifted = jnp.dot(
        fresh_latents[:, :kv_width], head_weight, preferred_element_type=jnp.float32
    ).astype(jnp.bfloat16)
    all_keys = jnp.concatenate(
        [
            jnp.concatenate(
                [lifted_parts[:, :NOPE], rope_parts.transpose(0, 2, 1).reshape(key_total, ROPE)], 1
            ),
            jnp.concatenate([fresh_lifted[:, :NOPE], fresh_latents[:, kv_width:]], 1),
        ],
        0,
    )
    all_values = jnp.concatenate([lifted_parts[:, NOPE:], fresh_lifted[:, NOPE:]], 0)
    page_row = page_table[slot_index]
    page_count = page_row.shape[0]
    page_size = key_total // page_count
    offsets = jnp.arange(page_size, dtype=jnp.int32)
    page_ids = jnp.arange(page_count, dtype=jnp.int32)
    logical_page = jnp.sum(
        page_ids[:, None] * (page_row[:, None] == page_ids[None, :]).astype(jnp.int32), 0
    )
    cached_visible = (logical_page[:, None] * page_size + offsets[None, :]).reshape(
        key_total
    ) < cached_count
    score_scale = 1.0 / math.sqrt(NOPE + ROPE)
    query_index = jnp.arange(group_rows, dtype=jnp.int32)[:, None]
    key_index = jnp.arange(group_rows, dtype=jnp.int32)[None, :]
    fresh_visible = (key_index <= query_index) & (key_index < live_count)
    visible = jnp.concatenate(
        [jnp.broadcast_to(cached_visible[None, :], (group_rows, key_total)), fresh_visible], 1
    )
    scores = (
        jnp.einsum("qd,kd->qk", queries, all_keys, preferred_element_type=jnp.float32)
        * score_scale
    )
    scores = jnp.where(visible, scores, -jnp.inf)
    row_peak = jnp.max(scores, 1, keepdims=True)
    exponent = jnp.exp(scores - row_peak)
    row_total = jnp.sum(exponent, 1)
    summed = jnp.dot(
        exponent.astype(jnp.bfloat16), all_values, preferred_element_type=jnp.float32
    )
    attended = (summed / row_total[:, None]).astype(jnp.bfloat16)
    live_rows = jnp.arange(group_rows, dtype=jnp.int32) < live_count
    attended = jnp.where(live_rows[:, None], attended, jnp.zeros_like(attended))
    out_parts = lax.dot_general(
        w_out, attended, (((0,), (1,)), ((), ())), preferred_element_type=jnp.float32
    ).astype(jnp.bfloat16)
    (out_pieces,) = exchange([out_parts.reshape(columns, -1, group_rows)], [False], "col", 3)
    summed_out = jnp.sum(out_pieces.astype(jnp.float32), 0)
    result = summed_out.T.astype(jnp.bfloat16)
    return result


def solution(mesh):
    return jax.shard_map(
        body,
        mesh=mesh,
        in_specs=(
            P("row", "col"),
            P("col", None),
            P(),
            P(),
            P(None, "col"),
            P(),
            P("col", None),
            P("row", "col", None),
            P(),
            P(),
            P(),
            P(),
        ),
        out_specs=P("row", "col"),
        check_vma=False,
    )
```

```python
import functools
import math

import jax
import jax.numpy as jnp
from jax import lax
from jax.experimental import pallas as pl
from jax.experimental.pallas import tpu as pltpu
from jax.sharding import PartitionSpec as P

MESH = pl.DeviceIdType.MESH

NOPE = 64
ROPE = 32
VDIM = 64


epsilon = 1e-05


def rms_scale(values, gain):
    return values * lax.rsqrt(jnp.mean(values * values, axis=-1, keepdims=True) + epsilon) * gain


def angle_tables(positions, width):
    half_dim = width // 2
    frequency = 10000.0 ** (-2.0 * jnp.arange(half_dim, dtype=jnp.float32) / width)
    angles = positions.astype(jnp.float32)[:, None] * frequency[None, :]
    return (jnp.cos(angles), jnp.sin(angles))


def rotary(values, cosine, sine_table):
    half_dim = values.shape[-1] // 2
    first_half = values[..., :half_dim]
    second_half = values[..., half_dim:]
    return jnp.concatenate(
        [
            first_half * cosine - second_half * sine_table,
            second_half * cosine + first_half * sine_table,
        ],
        -1,
    )


def _exchange_kernel(n, axis, modes, *refs):
    count = len(modes)
    sources, targets = refs[:count], refs[count : 2 * count]
    send_sem, recv_sem = refs[2 * count :]
    me = lax.axis_index(axis)
    barrier = pltpu.get_barrier_semaphore()
    for k in range(1, n):
        pl.semaphore_signal(
            barrier, inc=1, device_id={axis: lax.rem(me + k, n)}, device_id_type=MESH
        )
    pl.semaphore_wait(barrier, n - 1)

    def remote(a, k, peer, landing):
        x_ref = sources[a]
        return pltpu.make_async_remote_copy(
            src_ref=x_ref if modes[a] else x_ref.at[peer],
            dst_ref=targets[a].at[landing],
            send_sem=send_sem.at[a, k],
            recv_sem=recv_sem.at[a, k],
            device_id={axis: peer},
            device_id_type=MESH,
        )

    sends = []
    for k in range(1, n):
        for a in range(count):
            copy = remote(a, k, lax.rem(me + k, n), me)
            copy.start()
            sends.append(copy)
    for a in range(count):
        if modes[a]:
            targets[a][me] = sources[a][...]
        else:
            targets[a][me] = sources[a][me]
    for copy in sends:
        copy.wait_send()
    for k in range(1, n):
        source = lax.rem(me + n - k, n)
        for a in range(count):
            remote(a, k, source, source).wait_recv()


def exchange(arrays, modes, axis, collective_id):
    n = lax.axis_size(axis)
    shapes = [
        jax.ShapeDtypeStruct(((n,) + x.shape) if gather else x.shape, x.dtype)
        for x, gather in zip(arrays, modes)
    ]
    return pl.pallas_call(
        functools.partial(_exchange_kernel, n, axis, tuple(modes)),
        out_shape=shapes,
        in_specs=[pl.BlockSpec(memory_space=pltpu.VMEM)] * len(arrays),
        out_specs=[pl.BlockSpec(memory_space=pltpu.VMEM)] * len(arrays),
        scratch_shapes=[
            pltpu.SemaphoreType.DMA((len(arrays), n)),
            pltpu.SemaphoreType.DMA((len(arrays), n)),
        ],
        compiler_params=pltpu.CompilerParams(collective_id=collective_id, has_side_effects=True),
    )(*arrays)


def body(
    tokens,
    w_down,
    q_gain,
    kv_gain,
    w_q_up,
    w_kv_up,
    w_out,
    latent_cache,
    cache_len,
    new_len,
    page_table,
    home_slot,
):
    columns = lax.axis_size("col")
    column_id = lax.axis_index("col")
    row_id = lax.axis_index("row")
    group_rows = tokens.shape[0]
    own_rows = group_rows // columns
    q_width = q_gain.shape[0]
    kv_width = kv_gain.shape[0]
    slot_index = home_slot[row_id]
    cached_count = cache_len[slot_index]
    live_count = new_len[row_id]
    partial_sums = jnp.dot(tokens, w_down, preferred_element_type=jnp.float32)
    (pieces,) = exchange([partial_sums.reshape(columns, own_rows, -1)], [False], "col", 0)
    combined = jnp.sum(pieces, 0)
    own_position = cached_count + column_id * own_rows + jnp.arange(own_rows, dtype=jnp.int32)
    own_cos, own_sin = angle_tables(own_position, ROPE)
    own_query = rms_scale(combined[:, :q_width], q_gain).astype(jnp.bfloat16)
    own_latent = rms_scale(combined[:, q_width : q_width + kv_width], kv_gain).astype(jnp.bfloat16)
    own_rope = rotary(combined[:, q_width + kv_width :], own_cos, own_sin).astype(jnp.bfloat16)
    own_rows_all = jnp.concatenate([own_query, own_latent, own_rope], 1)
    segment = lax.all_gather(latent_cache, "row", axis=0, tiled=True)
    matches = jnp.arange(segment.shape[0], dtype=jnp.int32) == slot_index
    own_cache = jnp.sum(
        jnp.where(matches[:, None, None], segment.astype(jnp.float32), 0.0), 0
    ).astype(jnp.bfloat16)
    head_width = NOPE + VDIM
    head_weight = lax.dynamic_slice_in_dim(w_kv_up, column_id * head_width, head_width, 1)
    chunk = own_cache.shape[0]
    own_lifted = (
        jnp.dot(own_cache[:, :kv_width], w_kv_up, preferred_element_type=jnp.float32)
        .astype(jnp.bfloat16)
        .reshape(chunk, columns, head_width)
        .transpose(1, 0, 2)
    )
    lifted_parts, rope_parts, all_rows = exchange(
        [own_lifted, own_cache[:, kv_width:].T, own_rows_all], [False, True, True], "col", 2
    )
    all_rows = all_rows.reshape(group_rows, -1)
    query_latent = all_rows[:, :q_width]
    fresh_latents = all_rows[:, q_width:]
    query_cos, query_sin = angle_tables(
        cached_count + jnp.arange(group_rows, dtype=jnp.int32), ROPE
    )
    projected = jnp.dot(query_latent, w_q_up, preferred_element_type=jnp.float32)
    queries = jnp.concatenate(
        [projected[:, :NOPE], rotary(projected[:, NOPE:], query_cos, query_sin)], 1
    ).astype(jnp.bfloat16)
    key_total = columns * chunk
    lifted_parts = lifted_parts.reshape(key_total, head_width)
    fresh_lifted = jnp.dot(
        fresh_latents[:, :kv_width], head_weight, preferred_element_type=jnp.float32
    ).astype(jnp.bfloat16)
    all_keys = jnp.concatenate(
        [
            jnp.concatenate(
                [lifted_parts[:, :NOPE], rope_parts.transpose(0, 2, 1).reshape(key_total, ROPE)], 1
            ),
            jnp.concatenate([fresh_lifted[:, :NOPE], fresh_latents[:, kv_width:]], 1),
        ],
        0,
    )
    all_values = jnp.concatenate([lifted_parts[:, NOPE:], fresh_lifted[:, NOPE:]], 0)
    page_row = page_table[slot_index]
    page_count = page_row.shape[0]
    page_size = key_total // page_count
    offsets = jnp.arange(page_size, dtype=jnp.int32)
    page_ids = jnp.arange(page_count, dtype=jnp.int32)
    logical_page = jnp.sum(
        page_ids[:, None] * (page_row[:, None] == page_ids[None, :]).astype(jnp.int32), 0
    )
    cached_visible = (logical_page[:, None] * page_size + offsets[None, :]).reshape(
        key_total
    ) < cached_count
    score_scale = 1.0 / math.sqrt(NOPE + ROPE)
    query_index = jnp.arange(group_rows, dtype=jnp.int32)[:, None]
    key_index = jnp.arange(group_rows, dtype=jnp.int32)[None, :]
    fresh_visible = (key_index <= query_index) & (key_index < live_count)
    visible = jnp.concatenate(
        [jnp.broadcast_to(cached_visible[None, :], (group_rows, key_total)), fresh_visible], 1
    )
    scores = (
        jnp.einsum("qd,kd->qk", queries, all_keys, preferred_element_type=jnp.float32)
        * score_scale
    )
    scores = jnp.where(visible, scores, -jnp.inf)
    row_peak = jnp.max(scores, 1, keepdims=True)
    exponent = jnp.exp(scores - row_peak)
    row_total = jnp.sum(exponent, 1)
    summed = jnp.dot(
        exponent.astype(jnp.bfloat16), all_values, preferred_element_type=jnp.float32
    )
    attended = (summed / row_total[:, None]).astype(jnp.bfloat16)
    live_rows = jnp.arange(group_rows, dtype=jnp.int32) < live_count
    attended = jnp.where(live_rows[:, None], attended, jnp.zeros_like(attended))
    out_parts = lax.dot_general(
        w_out, attended, (((0,), (1,)), ((), ())), preferred_element_type=jnp.float32
    ).astype(jnp.bfloat16)
    (out_pieces,) = exchange([out_parts.reshape(columns, -1, group_rows)], [False], "col", 3)
    summed_out = jnp.sum(out_pieces.astype(jnp.float32), 0)
    result = summed_out.T.astype(jnp.bfloat16)
    return result


def solution(mesh):
    return jax.shard_map(
        body,
        mesh=mesh,
        in_specs=(
            P("row", "col"),
            P("col", None),
            P(),
            P(),
            P(None, "col"),
            P(),
            P("col", None),
            P("row", "col", None),
            P(),
            P(),
            P(),
            P(),
        ),
        out_specs=P("row", "col"),
        check_vma=False,
    )
```

```python
import functools
import math

import jax
import jax.numpy as jnp
from jax import lax
from jax.experimental import pallas as pl
from jax.experimental.pallas import tpu as pltpu
from jax.sharding import PartitionSpec as P

MESH = pl.DeviceIdType.MESH

NOPE = 64
ROPE = 32
VDIM = 64


epsilon = 1e-05


def rms_scale(values, gain):
    return values * lax.rsqrt(jnp.mean(values * values, axis=-1, keepdims=True) + epsilon) * gain


def angle_tables(positions, width):
    half_dim = width // 2
    frequency = 10000.0 ** (-2.0 * jnp.arange(half_dim, dtype=jnp.float32) / width)
    angles = positions.astype(jnp.float32)[:, None] * frequency[None, :]
    return (jnp.cos(angles), jnp.sin(angles))


def rotary(values, cosine, sine_table):
    half_dim = values.shape[-1] // 2
    first_half = values[..., :half_dim]
    second_half = values[..., half_dim:]
    return jnp.concatenate(
        [
            first_half * cosine - second_half * sine_table,
            second_half * cosine + first_half * sine_table,
        ],
        -1,
    )


def _exchange_kernel(n, axis, modes, *refs):
    count = len(modes)
    sources, targets = refs[:count], refs[count : 2 * count]
    send_sem, recv_sem = refs[2 * count :]
    me = lax.axis_index(axis)
    barrier = pltpu.get_barrier_semaphore()
    for k in range(1, n):
        pl.semaphore_signal(
            barrier, inc=1, device_id={axis: lax.rem(me + k, n)}, device_id_type=MESH
        )
    pl.semaphore_wait(barrier, n - 1)

    def remote(a, k, peer, landing):
        x_ref = sources[a]
        return pltpu.make_async_remote_copy(
            src_ref=x_ref if modes[a] else x_ref.at[peer],
            dst_ref=targets[a].at[landing],
            send_sem=send_sem.at[a, k],
            recv_sem=recv_sem.at[a, k],
            device_id={axis: peer},
            device_id_type=MESH,
        )

    sends = []
    for k in range(1, n):
        for a in range(count):
            copy = remote(a, k, lax.rem(me + k, n), me)
            copy.start()
            sends.append(copy)
    for a in range(count):
        if modes[a]:
            targets[a][me] = sources[a][...]
        else:
            targets[a][me] = sources[a][me]
    for copy in sends:
        copy.wait_send()
    for k in range(1, n):
        source = lax.rem(me + n - k, n)
        for a in range(count):
            remote(a, k, source, source).wait_recv()


def exchange(arrays, modes, axis, collective_id):
    n = lax.axis_size(axis)
    shapes = [
        jax.ShapeDtypeStruct(((n,) + x.shape) if gather else x.shape, x.dtype)
        for x, gather in zip(arrays, modes)
    ]
    return pl.pallas_call(
        functools.partial(_exchange_kernel, n, axis, tuple(modes)),
        out_shape=shapes,
        in_specs=[pl.BlockSpec(memory_space=pltpu.VMEM)] * len(arrays),
        out_specs=[pl.BlockSpec(memory_space=pltpu.VMEM)] * len(arrays),
        scratch_shapes=[
            pltpu.SemaphoreType.DMA((len(arrays), n)),
            pltpu.SemaphoreType.DMA((len(arrays), n)),
        ],
        compiler_params=pltpu.CompilerParams(collective_id=collective_id, has_side_effects=True),
    )(*arrays)


def body(
    tokens,
    w_down,
    q_gain,
    kv_gain,
    w_q_up,
    w_kv_up,
    w_out,
    latent_cache,
    cache_len,
    new_len,
    page_table,
    home_slot,
):
    columns = lax.axis_size("col")
    column_id = lax.axis_index("col")
    row_id = lax.axis_index("row")
    group_rows = tokens.shape[0]
    own_rows = group_rows // columns
    q_width = q_gain.shape[0]
    kv_width = kv_gain.shape[0]
    slot_index = home_slot[row_id]
    cached_count = cache_len[slot_index]
    live_count = new_len[row_id]
    partial_sums = jnp.dot(tokens, w_down, preferred_element_type=jnp.float32)
    (pieces,) = exchange(
        [partial_sums.astype(jnp.bfloat16).reshape(columns, -1, 128)], [False], "col", 0
    )
    combined = jnp.sum(pieces.astype(jnp.float32), 0).reshape(own_rows, -1)
    own_position = cached_count + column_id * own_rows + jnp.arange(own_rows, dtype=jnp.int32)
    own_cos, own_sin = angle_tables(own_position, ROPE)
    own_query = rms_scale(combined[:, :q_width], q_gain).astype(jnp.bfloat16)
    own_latent = rms_scale(combined[:, q_width : q_width + kv_width], kv_gain).astype(jnp.bfloat16)
    own_rope = rotary(combined[:, q_width + kv_width :], own_cos, own_sin).astype(jnp.bfloat16)
    own_rows_all = jnp.concatenate([own_query, own_latent, own_rope], 1)
    segment = lax.all_gather(latent_cache, "row", axis=0, tiled=True)
    matches = jnp.arange(segment.shape[0], dtype=jnp.int32) == slot_index
    own_cache = jnp.sum(
        jnp.where(matches[:, None, None], segment.astype(jnp.float32), 0.0), 0
    ).astype(jnp.bfloat16)
    head_width = NOPE + VDIM
    head_weight = lax.dynamic_slice_in_dim(w_kv_up, column_id * head_width, head_width, 1)
    chunk = own_cache.shape[0]
    own_lifted = (
        jnp.dot(own_cache[:, :kv_width], w_kv_up, preferred_element_type=jnp.float32)
        .astype(jnp.bfloat16)
        .reshape(chunk, columns, head_width)
        .transpose(1, 0, 2)
    )
    lifted_parts, rope_parts, all_rows = exchange(
        [own_lifted, own_cache[:, kv_width:].T, own_rows_all], [False, True, True], "col", 2
    )
    all_rows = all_rows.reshape(group_rows, -1)
    query_latent = all_rows[:, :q_width]
    fresh_latents = all_rows[:, q_width:]
    query_cos, query_sin = angle_tables(
        cached_count + jnp.arange(group_rows, dtype=jnp.int32), ROPE
    )
    projected = jnp.dot(query_latent, w_q_up, preferred_element_type=jnp.float32)
    queries = jnp.concatenate(
        [projected[:, :NOPE], rotary(projected[:, NOPE:], query_cos, query_sin)], 1
    ).astype(jnp.bfloat16)
    key_total = columns * chunk
    lifted_parts = lifted_parts.reshape(key_total, head_width)
    fresh_lifted = jnp.dot(
        fresh_latents[:, :kv_width], head_weight, preferred_element_type=jnp.float32
    ).astype(jnp.bfloat16)
    all_keys = jnp.concatenate(
        [
            jnp.concatenate(
                [lifted_parts[:, :NOPE], rope_parts.transpose(0, 2, 1).reshape(key_total, ROPE)], 1
            ),
            jnp.concatenate([fresh_lifted[:, :NOPE], fresh_latents[:, kv_width:]], 1),
        ],
        0,
    )
    all_values = jnp.concatenate([lifted_parts[:, NOPE:], fresh_lifted[:, NOPE:]], 0)
    page_row = page_table[slot_index]
    page_count = page_row.shape[0]
    page_size = key_total // page_count
    offsets = jnp.arange(page_size, dtype=jnp.int32)
    page_ids = jnp.arange(page_count, dtype=jnp.int32)
    logical_page = jnp.sum(
        page_ids[:, None] * (page_row[:, None] == page_ids[None, :]).astype(jnp.int32), 0
    )
    cached_visible = (logical_page[:, None] * page_size + offsets[None, :]).reshape(
        key_total
    ) < cached_count
    score_scale = 1.0 / math.sqrt(NOPE + ROPE)
    query_index = jnp.arange(group_rows, dtype=jnp.int32)[:, None]
    key_index = jnp.arange(group_rows, dtype=jnp.int32)[None, :]
    fresh_visible = (key_index <= query_index) & (key_index < live_count)
    visible = jnp.concatenate(
        [jnp.broadcast_to(cached_visible[None, :], (group_rows, key_total)), fresh_visible], 1
    )
    scores = (
        jnp.einsum("qd,kd->qk", queries, all_keys, preferred_element_type=jnp.float32)
        * score_scale
    )
    scores = jnp.where(visible, scores, -jnp.inf)
    row_peak = jnp.max(scores, 1, keepdims=True)
    exponent = jnp.exp(scores - row_peak)
    row_total = jnp.sum(exponent, 1)
    summed = jnp.dot(
        exponent.astype(jnp.bfloat16), all_values, preferred_element_type=jnp.float32
    )
    attended = (summed / row_total[:, None]).astype(jnp.bfloat16)
    live_rows = jnp.arange(group_rows, dtype=jnp.int32) < live_count
    attended = jnp.where(live_rows[:, None], attended, jnp.zeros_like(attended))
    out_parts = lax.dot_general(
        w_out, attended, (((0,), (1,)), ((), ())), preferred_element_type=jnp.float32
    ).astype(jnp.bfloat16)
    (out_pieces,) = exchange([out_parts.reshape(columns, -1, group_rows)], [False], "col", 3)
    summed_out = jnp.sum(out_pieces.astype(jnp.float32), 0)
    result = summed_out.T.astype(jnp.bfloat16)
    return result


def solution(mesh):
    return jax.shard_map(
        body,
        mesh=mesh,
        in_specs=(
            P("row", "col"),
            P("col", None),
            P(),
            P(),
            P(None, "col"),
            P(),
            P("col", None),
            P("row", "col", None),
            P(),
            P(),
            P(),
            P(),
        ),
        out_specs=P("row", "col"),
        check_vma=False,
    )
```

```python
import functools
import math

import jax
import jax.numpy as jnp
from jax import lax
from jax.experimental import pallas as pl
from jax.experimental.pallas import tpu as pltpu
from jax.sharding import PartitionSpec as P

MESH = pl.DeviceIdType.MESH

NOPE = 64
ROPE = 32
VDIM = 64


epsilon = 1e-05


def rms_scale(values, gain):
    return values * lax.rsqrt(jnp.mean(values * values, axis=-1, keepdims=True) + epsilon) * gain


def angle_tables(positions, width):
    half_dim = width // 2
    frequency = 10000.0 ** (-2.0 * jnp.arange(half_dim, dtype=jnp.float32) / width)
    angles = positions.astype(jnp.float32)[:, None] * frequency[None, :]
    return (jnp.cos(angles), jnp.sin(angles))


def rotary(values, cosine, sine_table):
    half_dim = values.shape[-1] // 2
    first_half = values[..., :half_dim]
    second_half = values[..., half_dim:]
    return jnp.concatenate(
        [
            first_half * cosine - second_half * sine_table,
            second_half * cosine + first_half * sine_table,
        ],
        -1,
    )


def _exchange_kernel(n, axis, modes, *refs):
    count = len(modes)
    sources, targets = refs[:count], refs[count : 2 * count]
    send_sem, recv_sem = refs[2 * count :]
    me = lax.axis_index(axis)
    barrier = pltpu.get_barrier_semaphore()
    for k in range(1, n):
        pl.semaphore_signal(
            barrier, inc=1, device_id={axis: lax.rem(me + k, n)}, device_id_type=MESH
        )
    pl.semaphore_wait(barrier, n - 1)

    def remote(a, k, peer, landing):
        x_ref = sources[a]
        return pltpu.make_async_remote_copy(
            src_ref=x_ref if modes[a] else x_ref.at[peer],
            dst_ref=targets[a].at[landing],
            send_sem=send_sem.at[a, k],
            recv_sem=recv_sem.at[a, k],
            device_id={axis: peer},
            device_id_type=MESH,
        )

    sends = []
    for k in range(1, n):
        for a in range(count):
            copy = remote(a, k, lax.rem(me + k, n), me)
            copy.start()
            sends.append(copy)
    for a in range(count):
        if modes[a]:
            targets[a][me] = sources[a][...]
        else:
            targets[a][me] = sources[a][me]
    for copy in sends:
        copy.wait_send()
    for k in range(1, n):
        source = lax.rem(me + n - k, n)
        for a in range(count):
            remote(a, k, source, source).wait_recv()


def exchange(arrays, modes, axis, collective_id):
    n = lax.axis_size(axis)
    shapes = [
        jax.ShapeDtypeStruct(((n,) + x.shape) if gather else x.shape, x.dtype)
        for x, gather in zip(arrays, modes)
    ]
    return pl.pallas_call(
        functools.partial(_exchange_kernel, n, axis, tuple(modes)),
        out_shape=shapes,
        in_specs=[pl.BlockSpec(memory_space=pltpu.VMEM)] * len(arrays),
        out_specs=[pl.BlockSpec(memory_space=pltpu.VMEM)] * len(arrays),
        scratch_shapes=[
            pltpu.SemaphoreType.DMA((len(arrays), n)),
            pltpu.SemaphoreType.DMA((len(arrays), n)),
        ],
        compiler_params=pltpu.CompilerParams(collective_id=collective_id, has_side_effects=True),
    )(*arrays)


def _attention_kernel(
    scale, q_nope_ref, q_rope_ref, lifted_ref, rope_ref, bias_ref, fresh_keys_ref,
    fresh_values_ref, fresh_bias_ref, out_ref, scores_ref,
):
    blocks, _, width = rope_ref.shape
    q_nope = q_nope_ref[...]
    q_rope = q_rope_ref[...]
    transposed = (((1,), (1,)), ((), ()))
    fresh = (
        lax.dot_general(
            jnp.concatenate([q_nope, q_rope], 1), fresh_keys_ref[...], transposed,
            preferred_element_type=jnp.float32,
        )
        * scale
        + fresh_bias_ref[...]
    )

    def score(j, peak):
        rows = pl.ds(pl.multiple_of(j * width, width), width)
        block = (
            lax.dot_general(
                q_nope, lifted_ref[rows, pl.ds(0, NOPE)], transposed,
                preferred_element_type=jnp.float32,
            )
            + jnp.dot(q_rope, rope_ref[j], preferred_element_type=jnp.float32)
        ) * scale + bias_ref[pl.ds(j, 1), :]
        scores_ref[:, rows] = block
        return jnp.maximum(peak, jnp.max(block, axis=1, keepdims=True))

    peak = lax.fori_loop(0, blocks, score, jnp.max(fresh, axis=1, keepdims=True))
    fresh_exp = jnp.exp(fresh - peak)
    start = (
        jnp.sum(fresh_exp, axis=1, keepdims=True),
        jnp.dot(
            fresh_exp.astype(jnp.bfloat16), fresh_values_ref[...],
            preferred_element_type=jnp.float32,
        ),
    )

    def accumulate(j, carry):
        total, summed = carry
        rows = pl.ds(pl.multiple_of(j * width, width), width)
        exponent = jnp.exp(scores_ref[:, rows] - peak)
        return (
            total + jnp.sum(exponent, axis=1, keepdims=True),
            summed
            + jnp.dot(
                exponent.astype(jnp.bfloat16), lifted_ref[rows, pl.ds(NOPE, VDIM)],
                preferred_element_type=jnp.float32,
            ),
        )

    total, summed = lax.fori_loop(0, blocks, accumulate, start)
    out_ref[...] = (summed / total).astype(out_ref.dtype)


def attention(q_nope, q_rope, lifted, rope, bias, fresh_keys, fresh_values, fresh_bias):
    rows = q_nope.shape[0]
    vmem = pl.BlockSpec(memory_space=pltpu.VMEM)
    return pl.pallas_call(
        functools.partial(_attention_kernel, 1.0 / math.sqrt(NOPE + ROPE)),
        out_shape=jax.ShapeDtypeStruct((rows, VDIM), jnp.bfloat16),
        in_specs=[vmem] * 8,
        out_specs=vmem,
        scratch_shapes=[pltpu.VMEM((rows, lifted.shape[0]), jnp.float32)],
    )(q_nope, q_rope, lifted, rope, bias, fresh_keys, fresh_values, fresh_bias)


def body(
    tokens,
    w_down,
    q_gain,
    kv_gain,
    w_q_up,
    w_kv_up,
    w_out,
    latent_cache,
    cache_len,
    new_len,
    page_table,
    home_slot,
):
    columns = lax.axis_size("col")
    column_id = lax.axis_index("col")
    row_id = lax.axis_index("row")
    group_rows = tokens.shape[0]
    own_rows = group_rows // columns
    q_width = q_gain.shape[0]
    kv_width = kv_gain.shape[0]
    slot_index = home_slot[row_id]
    cached_count = cache_len[slot_index]
    live_count = new_len[row_id]
    partial_sums = jnp.dot(tokens, w_down, preferred_element_type=jnp.float32)
    (pieces,) = exchange(
        [partial_sums.astype(jnp.bfloat16).reshape(columns, -1, 128)], [False], "col", 0
    )
    combined = jnp.sum(pieces.astype(jnp.float32), 0).reshape(own_rows, -1)
    own_position = cached_count + column_id * own_rows + jnp.arange(own_rows, dtype=jnp.int32)
    own_cos, own_sin = angle_tables(own_position, ROPE)
    own_query = rms_scale(combined[:, :q_width], q_gain).astype(jnp.bfloat16)
    own_latent = rms_scale(combined[:, q_width : q_width + kv_width], kv_gain).astype(jnp.bfloat16)
    own_rope = rotary(combined[:, q_width + kv_width :], own_cos, own_sin).astype(jnp.bfloat16)
    own_rows_all = jnp.concatenate([own_query, own_latent, own_rope], 1)
    segment = lax.all_gather(latent_cache, "row", axis=0, tiled=True)
    matches = jnp.arange(segment.shape[0], dtype=jnp.int32) == slot_index
    own_cache = jnp.sum(
        jnp.where(matches[:, None, None], segment.astype(jnp.float32), 0.0), 0
    ).astype(jnp.bfloat16)
    head_width = NOPE + VDIM
    head_weight = lax.dynamic_slice_in_dim(w_kv_up, column_id * head_width, head_width, 1)
    chunk = own_cache.shape[0]
    own_lifted = (
        jnp.dot(own_cache[:, :kv_width], w_kv_up, preferred_element_type=jnp.float32)
        .astype(jnp.bfloat16)
        .reshape(chunk, columns, head_width)
        .transpose(1, 0, 2)
    )
    lifted_parts, rope_parts, all_rows = exchange(
        [own_lifted, own_cache[:, kv_width:].T, own_rows_all], [False, True, True], "col", 2
    )
    all_rows = all_rows.reshape(group_rows, -1)
    query_latent = all_rows[:, :q_width]
    fresh_latents = all_rows[:, q_width:]
    query_cos, query_sin = angle_tables(
        cached_count + jnp.arange(group_rows, dtype=jnp.int32), ROPE
    )
    projected = jnp.dot(query_latent, w_q_up, preferred_element_type=jnp.float32)
    queries = jnp.concatenate(
        [projected[:, :NOPE], rotary(projected[:, NOPE:], query_cos, query_sin)], 1
    ).astype(jnp.bfloat16)
    key_total = columns * chunk
    lifted_parts = lifted_parts.reshape(key_total, head_width)
    fresh_lifted = jnp.dot(
        fresh_latents[:, :kv_width], head_weight, preferred_element_type=jnp.float32
    ).astype(jnp.bfloat16)
    page_row = page_table[slot_index]
    page_count = page_row.shape[0]
    page_size = key_total // page_count
    offsets = jnp.arange(page_size, dtype=jnp.int32)
    page_ids = jnp.arange(page_count, dtype=jnp.int32)
    logical_page = jnp.sum(
        page_ids[:, None] * (page_row[:, None] == page_ids[None, :]).astype(jnp.int32), 0
    )
    cached_visible = (logical_page[:, None] * page_size + offsets[None, :]).reshape(
        key_total
    ) < cached_count
    score_scale = 1.0 / math.sqrt(NOPE + ROPE)
    query_index = jnp.arange(group_rows, dtype=jnp.int32)[:, None]
    key_index = jnp.arange(group_rows, dtype=jnp.int32)[None, :]
    fresh_visible = (key_index <= query_index) & (key_index < live_count)
    fresh_bias = jnp.where(fresh_visible, 0.0, -jnp.inf).astype(jnp.float32)
    cached_bias = jnp.where(cached_visible, 0.0, -jnp.inf).astype(jnp.float32)
    attended = attention(
        queries[:, :NOPE],
        queries[:, NOPE:],
        lifted_parts,
        rope_parts,
        cached_bias.reshape(columns, chunk),
        jnp.concatenate([fresh_lifted[:, :NOPE], fresh_latents[:, kv_width:]], 1),
        fresh_lifted[:, NOPE:],
        fresh_bias,
    )
    live_rows = jnp.arange(group_rows, dtype=jnp.int32) < live_count
    attended = jnp.where(live_rows[:, None], attended, jnp.zeros_like(attended))
    out_parts = lax.dot_general(
        w_out, attended, (((0,), (1,)), ((), ())), preferred_element_type=jnp.float32
    ).astype(jnp.bfloat16)
    (out_pieces,) = exchange([out_parts.reshape(columns, -1, group_rows)], [False], "col", 3)
    summed_out = jnp.sum(out_pieces.astype(jnp.float32), 0)
    result = summed_out.T.astype(jnp.bfloat16)
    return result


def solution(mesh):
    return jax.shard_map(
        body,
        mesh=mesh,
        in_specs=(
            P("row", "col"),
            P("col", None),
            P(),
            P(),
            P(None, "col"),
            P(),
            P("col", None),
            P("row", "col", None),
            P(),
            P(),
            P(),
            P(),
        ),
        out_specs=P("row", "col"),
        check_vma=False,
    )
```

```python
import functools
import math

import jax
import jax.numpy as jnp
from jax import lax
from jax.experimental import pallas as pl
from jax.experimental.pallas import tpu as pltpu
from jax.sharding import PartitionSpec as P

MESH = pl.DeviceIdType.MESH

NOPE = 64
ROPE = 32
VDIM = 64


epsilon = 1e-05


def rms_scale(values, gain):
    return values * lax.rsqrt(jnp.mean(values * values, axis=-1, keepdims=True) + epsilon) * gain


def angle_tables(positions, width):
    half_dim = width // 2
    frequency = 10000.0 ** (-2.0 * jnp.arange(half_dim, dtype=jnp.float32) / width)
    angles = positions.astype(jnp.float32)[:, None] * frequency[None, :]
    return (jnp.cos(angles), jnp.sin(angles))


def rotary(values, cosine, sine_table):
    half_dim = values.shape[-1] // 2
    first_half = values[..., :half_dim]
    second_half = values[..., half_dim:]
    return jnp.concatenate(
        [
            first_half * cosine - second_half * sine_table,
            second_half * cosine + first_half * sine_table,
        ],
        -1,
    )


PLANE_X = 4


def _group_size(group, n):
    return {"all": n, "x": PLANE_X, "y": n // PLANE_X}[group]


def _group_peer(group, n, me, k):
    if group == "x":
        return (me // PLANE_X) * PLANE_X + lax.rem(me % PLANE_X + k, PLANE_X)
    if group == "y":
        return lax.rem(me // PLANE_X + k, n // PLANE_X) * PLANE_X + me % PLANE_X
    return lax.rem(me + k, n)


def _group_slot(group, device):
    if group == "x":
        return device % PLANE_X
    if group == "y":
        return device // PLANE_X
    return device


def _exchange_kernel(n, plan, *refs):
    count = len(plan)
    sources, targets = refs[:count], refs[count : 2 * count]
    send_sem, recv_sem = refs[2 * count :]
    me = lax.axis_index("col")
    barrier = pltpu.get_barrier_semaphore()
    for k in range(1, n):
        pl.semaphore_signal(
            barrier, inc=1, device_id={"col": lax.rem(me + k, n)}, device_id_type=MESH
        )
    pl.semaphore_wait(barrier, n - 1)

    def remote(a, k, peer, landing):
        group, gather = plan[a]
        x_ref = sources[a]
        return pltpu.make_async_remote_copy(
            src_ref=x_ref if gather else x_ref.at[_group_slot(group, peer)],
            dst_ref=targets[a].at[landing],
            send_sem=send_sem.at[a, k],
            recv_sem=recv_sem.at[a, k],
            device_id={"col": peer},
            device_id_type=MESH,
        )

    sends = []
    for a, (group, gather) in enumerate(plan):
        for k in range(1, _group_size(group, n)):
            copy = remote(a, k, _group_peer(group, n, me, k), _group_slot(group, me))
            copy.start()
            sends.append(copy)
    for a, (group, gather) in enumerate(plan):
        mine = _group_slot(group, me)
        if gather:
            targets[a][mine] = sources[a][...]
        else:
            targets[a][mine] = sources[a][mine]
    for copy in sends:
        copy.wait_send()
    for a, (group, gather) in enumerate(plan):
        size = _group_size(group, n)
        for k in range(1, size):
            source = _group_peer(group, n, me, size - k)
            remote(a, k, source, _group_slot(group, source)).wait_recv()


def exchange(arrays, plan, collective_id):
    n = lax.axis_size("col")
    shapes = [
        jax.ShapeDtypeStruct(
            ((_group_size(group, n),) + x.shape) if gather else x.shape, x.dtype
        )
        for x, (group, gather) in zip(arrays, plan)
    ]
    return pl.pallas_call(
        functools.partial(_exchange_kernel, n, tuple(plan)),
        out_shape=shapes,
        in_specs=[pl.BlockSpec(memory_space=pltpu.VMEM)] * len(arrays),
        out_specs=[pl.BlockSpec(memory_space=pltpu.VMEM)] * len(arrays),
        scratch_shapes=[
            pltpu.SemaphoreType.DMA((len(arrays), n)),
            pltpu.SemaphoreType.DMA((len(arrays), n)),
        ],
        compiler_params=pltpu.CompilerParams(collective_id=collective_id, has_side_effects=True),
    )(*arrays)


def body(
    tokens,
    w_down,
    q_gain,
    kv_gain,
    w_q_up,
    w_kv_up,
    w_out,
    latent_cache,
    cache_len,
    new_len,
    page_table,
    home_slot,
):
    columns = lax.axis_size("col")
    column_id = lax.axis_index("col")
    row_id = lax.axis_index("row")
    lines = columns // PLANE_X
    line_id = column_id // PLANE_X
    lane_id = column_id % PLANE_X
    group_rows = tokens.shape[0]
    own_rows = group_rows // columns
    q_width = q_gain.shape[0]
    kv_width = kv_gain.shape[0]
    slot_index = home_slot[row_id]
    cached_count = cache_len[slot_index]
    live_count = new_len[row_id]
    partial_sums = jnp.dot(tokens, w_down, preferred_element_type=jnp.float32)
    (pieces,) = exchange(
        [partial_sums.astype(jnp.bfloat16).reshape(columns, -1, 128)], [("all", False)], 0
    )
    combined = jnp.sum(pieces.astype(jnp.float32), 0).reshape(own_rows, -1)
    own_position = cached_count + column_id * own_rows + jnp.arange(own_rows, dtype=jnp.int32)
    own_cos, own_sin = angle_tables(own_position, ROPE)
    own_query = rms_scale(combined[:, :q_width], q_gain).astype(jnp.bfloat16)
    own_latent = rms_scale(combined[:, q_width : q_width + kv_width], kv_gain).astype(jnp.bfloat16)
    own_rope = rotary(combined[:, q_width + kv_width :], own_cos, own_sin).astype(jnp.bfloat16)
    own_rows_all = jnp.concatenate([own_query, own_latent, own_rope], 1)
    segment = lax.all_gather(latent_cache, "row", axis=0, tiled=True)
    matches = jnp.arange(segment.shape[0], dtype=jnp.int32) == slot_index
    own_cache = jnp.sum(
        jnp.where(matches[:, None, None], segment.astype(jnp.float32), 0.0), 0
    ).astype(jnp.bfloat16)
    chunk = own_cache.shape[0]
    cache_parts, all_rows = exchange(
        [own_cache.T, own_rows_all], [("x", True), ("all", True)], 2
    )
    all_rows = all_rows.reshape(group_rows, -1)
    query_latent = all_rows[:, :q_width]
    fresh_latents = all_rows[:, q_width:]
    query_cos, query_sin = angle_tables(
        cached_count + jnp.arange(group_rows, dtype=jnp.int32), ROPE
    )
    projected = jnp.dot(query_latent, w_q_up, preferred_element_type=jnp.float32)
    queries = jnp.concatenate(
        [projected[:, :NOPE], rotary(projected[:, NOPE:], query_cos, query_sin)], 1
    ).astype(jnp.bfloat16)
    (head_queries,) = exchange([queries], [("y", True)], 1)
    head_width = NOPE + VDIM
    heads = columns
    line_weight = lax.dynamic_index_in_dim(
        w_kv_up.reshape(kv_width, lines, PLANE_X, head_width), lane_id, axis=2, keepdims=False
    ).reshape(kv_width, lines * head_width)
    span = PLANE_X * chunk
    span_latents = cache_parts[:, :kv_width, :].transpose(0, 2, 1).reshape(span, kv_width)
    span_rope = cache_parts[:, kv_width:, :].transpose(0, 2, 1).reshape(span, ROPE)
    span_lifted = (
        jnp.dot(span_latents, line_weight, preferred_element_type=jnp.float32)
        .astype(jnp.bfloat16)
        .reshape(span, lines, head_width)
    )
    fresh_lifted = (
        jnp.dot(fresh_latents[:, :kv_width], line_weight, preferred_element_type=jnp.float32)
        .astype(jnp.bfloat16)
        .reshape(group_rows, lines, head_width)
    )
    fresh_rope = fresh_latents[:, kv_width:]
    q_nope = head_queries[:, :, :NOPE]
    q_rope = head_queries[:, :, NOPE:]
    score_scale = 1.0 / math.sqrt(NOPE + ROPE)

    def score(lifted, rope):
        return (
            jnp.einsum("hqd,khd->hqk", q_nope, lifted[:, :, :NOPE], preferred_element_type=jnp.float32)
            + jnp.einsum("hqd,kd->hqk", q_rope, rope, preferred_element_type=jnp.float32)
        ) * score_scale

    key_total = columns * chunk
    page_row = page_table[slot_index]
    page_count = page_row.shape[0]
    page_size = key_total // page_count
    offsets = jnp.arange(page_size, dtype=jnp.int32)
    page_ids = jnp.arange(page_count, dtype=jnp.int32)
    logical_page = jnp.sum(
        page_ids[:, None] * (page_row[:, None] == page_ids[None, :]).astype(jnp.int32), 0
    )
    cached_visible = (logical_page[:, None] * page_size + offsets[None, :]).reshape(
        key_total
    ) < cached_count
    span_visible = lax.dynamic_slice_in_dim(cached_visible, line_id * span, span, 0)
    share = group_rows // lines
    query_index = jnp.arange(group_rows, dtype=jnp.int32)[:, None]
    key_index = jnp.arange(group_rows, dtype=jnp.int32)[None, :]
    fresh_visible = (
        (key_index <= query_index) & (key_index < live_count) & (key_index // share == line_id)
    )
    visible = jnp.concatenate(
        [jnp.broadcast_to(span_visible[None, :], (group_rows, span)), fresh_visible], 1
    )
    scores = jnp.concatenate(
        [score(span_lifted, span_rope), score(fresh_lifted, fresh_rope)], 2
    )
    scores = jnp.where(visible[None], scores, -jnp.inf)
    row_peak = jnp.max(scores, 2)
    safe_peak = jnp.where(row_peak == -jnp.inf, 0.0, row_peak)
    exponent = jnp.exp(scores - safe_peak[:, :, None])
    row_total = jnp.sum(exponent, 2)
    values = jnp.concatenate([span_lifted[:, :, NOPE:], fresh_lifted[:, :, NOPE:]], 0)
    summed = jnp.einsum(
        "hqk,khd->hdq", exponent.astype(jnp.bfloat16), values, preferred_element_type=jnp.float32
    )
    stats = jnp.stack([row_peak, row_total], 1)
    summed_parts, stat_parts = exchange([summed, stats], [("y", False), ("y", False)], 4)
    peak = jnp.max(stat_parts[:, 0, :], 0)
    factor = jnp.exp(stat_parts[:, 0, :] - peak[None, :])
    total = jnp.sum(factor * stat_parts[:, 1, :], 0)
    merged = jnp.sum(factor[:, None, :] * summed_parts, 0)
    attended = (merged / total[None, :]).astype(jnp.bfloat16)
    live_rows = jnp.arange(group_rows, dtype=jnp.int32) < live_count
    attended = jnp.where(live_rows[None, :], attended, jnp.zeros_like(attended))
    out_parts = lax.dot_general(
        w_out, attended, (((0,), (0,)), ((), ())), preferred_element_type=jnp.float32
    ).astype(jnp.bfloat16)
    (out_pieces,) = exchange([out_parts.reshape(columns, -1, group_rows)], [("all", False)], 3)
    summed_out = jnp.sum(out_pieces.astype(jnp.float32), 0)
    result = summed_out.T.astype(jnp.bfloat16)
    return result


def solution(mesh):
    return jax.shard_map(
        body,
        mesh=mesh,
        in_specs=(
            P("row", "col"),
            P("col", None),
            P(),
            P(),
            P(None, "col"),
            P(),
            P("col", None),
            P("row", "col", None),
            P(),
            P(),
            P(),
            P(),
        ),
        out_specs=P("row", "col"),
        check_vma=False,
    )
```

```python
import functools
import math

import jax
import jax.numpy as jnp
from jax import lax
from jax.experimental import pallas as pl
from jax.experimental.pallas import tpu as pltpu
from jax.sharding import PartitionSpec as P

MESH = pl.DeviceIdType.MESH

NOPE = 64
ROPE = 32
VDIM = 64


epsilon = 1e-05


def rms_scale(values, gain):
    return values * lax.rsqrt(jnp.mean(values * values, axis=-1, keepdims=True) + epsilon) * gain


def angle_tables(positions, width):
    half_dim = width // 2
    frequency = 10000.0 ** (-2.0 * jnp.arange(half_dim, dtype=jnp.float32) / width)
    angles = positions.astype(jnp.float32)[:, None] * frequency[None, :]
    return (jnp.cos(angles), jnp.sin(angles))


def rotary(values, cosine, sine_table):
    half_dim = values.shape[-1] // 2
    first_half = values[..., :half_dim]
    second_half = values[..., half_dim:]
    return jnp.concatenate(
        [
            first_half * cosine - second_half * sine_table,
            second_half * cosine + first_half * sine_table,
        ],
        -1,
    )


PLANE_X = 4


def _group_size(group, n):
    return {"all": n, "x": PLANE_X, "y": n // PLANE_X}[group]


def _group_peer(group, n, me, k):
    if group == "x":
        return (me // PLANE_X) * PLANE_X + lax.rem(me % PLANE_X + k, PLANE_X)
    if group == "y":
        return lax.rem(me // PLANE_X + k, n // PLANE_X) * PLANE_X + me % PLANE_X
    return lax.rem(me + k, n)


def _group_slot(group, device):
    if group == "x":
        return device % PLANE_X
    if group == "y":
        return device // PLANE_X
    return device


def _exchange_kernel(n, plan, *refs):
    count = len(plan)
    sources, targets = refs[:count], refs[count : 2 * count]
    send_sem, recv_sem = refs[2 * count :]
    me = lax.axis_index("col")
    barrier = pltpu.get_barrier_semaphore()
    for k in range(1, n):
        pl.semaphore_signal(
            barrier, inc=1, device_id={"col": lax.rem(me + k, n)}, device_id_type=MESH
        )
    pl.semaphore_wait(barrier, n - 1)

    def remote(a, k, peer, landing):
        group, gather = plan[a]
        x_ref = sources[a]
        return pltpu.make_async_remote_copy(
            src_ref=x_ref if gather else x_ref.at[_group_slot(group, peer)],
            dst_ref=targets[a].at[landing],
            send_sem=send_sem.at[a, k],
            recv_sem=recv_sem.at[a, k],
            device_id={"col": peer},
            device_id_type=MESH,
        )

    sends = []
    for a, (group, gather) in enumerate(plan):
        for k in range(1, _group_size(group, n)):
            copy = remote(a, k, _group_peer(group, n, me, k), _group_slot(group, me))
            copy.start()
            sends.append(copy)
    for a, (group, gather) in enumerate(plan):
        mine = _group_slot(group, me)
        if gather:
            targets[a][mine] = sources[a][...]
        else:
            targets[a][mine] = sources[a][mine]
    for copy in sends:
        copy.wait_send()
    for a, (group, gather) in enumerate(plan):
        size = _group_size(group, n)
        for k in range(1, size):
            source = _group_peer(group, n, me, size - k)
            remote(a, k, source, _group_slot(group, source)).wait_recv()


def exchange(arrays, plan, collective_id):
    n = lax.axis_size("col")
    shapes = [
        jax.ShapeDtypeStruct(
            ((_group_size(group, n),) + x.shape) if gather else x.shape, x.dtype
        )
        for x, (group, gather) in zip(arrays, plan)
    ]
    return pl.pallas_call(
        functools.partial(_exchange_kernel, n, tuple(plan)),
        out_shape=shapes,
        in_specs=[pl.BlockSpec(memory_space=pltpu.VMEM)] * len(arrays),
        out_specs=[pl.BlockSpec(memory_space=pltpu.VMEM)] * len(arrays),
        scratch_shapes=[
            pltpu.SemaphoreType.DMA((len(arrays), n)),
            pltpu.SemaphoreType.DMA((len(arrays), n)),
        ],
        compiler_params=pltpu.CompilerParams(collective_id=collective_id, has_side_effects=True),
    )(*arrays)


def body(
    tokens,
    w_down,
    q_gain,
    kv_gain,
    w_q_up,
    w_kv_up,
    w_out,
    latent_cache,
    cache_len,
    new_len,
    page_table,
    home_slot,
):
    columns = lax.axis_size("col")
    column_id = lax.axis_index("col")
    row_id = lax.axis_index("row")
    lines = columns // PLANE_X
    line_id = column_id // PLANE_X
    lane_id = column_id % PLANE_X
    group_rows = tokens.shape[0]
    own_rows = group_rows // columns
    q_width = q_gain.shape[0]
    kv_width = kv_gain.shape[0]
    slot_index = home_slot[row_id]
    cached_count = cache_len[slot_index]
    live_count = new_len[row_id]
    partial_sums = jnp.dot(tokens, w_down, preferred_element_type=jnp.float32)
    pieces, line_query_weight = exchange(
        [partial_sums.astype(jnp.bfloat16).reshape(columns, -1, 128), w_q_up.T],
        [("all", False), ("y", True)],
        0,
    )
    combined = jnp.sum(pieces.astype(jnp.float32), 0).reshape(own_rows, -1)
    own_position = cached_count + column_id * own_rows + jnp.arange(own_rows, dtype=jnp.int32)
    own_cos, own_sin = angle_tables(own_position, ROPE)
    own_query = rms_scale(combined[:, :q_width], q_gain).astype(jnp.bfloat16)
    own_latent = rms_scale(combined[:, q_width : q_width + kv_width], kv_gain).astype(jnp.bfloat16)
    own_rope = rotary(combined[:, q_width + kv_width :], own_cos, own_sin).astype(jnp.bfloat16)
    own_rows_all = jnp.concatenate([own_query, own_latent, own_rope], 1)
    segment = lax.all_gather(latent_cache, "row", axis=0, tiled=True)
    matches = jnp.arange(segment.shape[0], dtype=jnp.int32) == slot_index
    own_cache = jnp.sum(
        jnp.where(matches[:, None, None], segment.astype(jnp.float32), 0.0), 0
    ).astype(jnp.bfloat16)
    chunk = own_cache.shape[0]
    cache_parts, all_rows = exchange(
        [own_cache.T, own_rows_all], [("x", True), ("all", True)], 2
    )
    all_rows = all_rows.reshape(group_rows, -1)
    query_latent = all_rows[:, :q_width]
    fresh_latents = all_rows[:, q_width:]
    query_cos, query_sin = angle_tables(
        cached_count + jnp.arange(group_rows, dtype=jnp.int32), ROPE
    )
    projected = jnp.einsum(
        "qk,hdk->hqd", query_latent, line_query_weight, preferred_element_type=jnp.float32
    )
    head_queries = jnp.concatenate(
        [
            projected[:, :, :NOPE],
            rotary(projected[:, :, NOPE:], query_cos[None], query_sin[None]),
        ],
        2,
    ).astype(jnp.bfloat16)
    head_width = NOPE + VDIM
    heads = columns
    line_weight = lax.dynamic_index_in_dim(
        w_kv_up.reshape(kv_width, lines, PLANE_X, head_width), lane_id, axis=2, keepdims=False
    ).reshape(kv_width, lines * head_width)
    span = PLANE_X * chunk
    span_latents = cache_parts[:, :kv_width, :].transpose(0, 2, 1).reshape(span, kv_width)
    span_rope = cache_parts[:, kv_width:, :].transpose(0, 2, 1).reshape(span, ROPE)
    span_lifted = (
        jnp.dot(span_latents, line_weight, preferred_element_type=jnp.float32)
        .astype(jnp.bfloat16)
        .reshape(span, lines, head_width)
    )
    fresh_lifted = (
        jnp.dot(fresh_latents[:, :kv_width], line_weight, preferred_element_type=jnp.float32)
        .astype(jnp.bfloat16)
        .reshape(group_rows, lines, head_width)
    )
    fresh_rope = fresh_latents[:, kv_width:]
    q_nope = head_queries[:, :, :NOPE]
    q_rope = head_queries[:, :, NOPE:]
    score_scale = 1.0 / math.sqrt(NOPE + ROPE)

    def score(lifted, rope):
        return (
            jnp.einsum("hqd,khd->hqk", q_nope, lifted[:, :, :NOPE], preferred_element_type=jnp.float32)
            + jnp.einsum("hqd,kd->hqk", q_rope, rope, preferred_element_type=jnp.float32)
        ) * score_scale

    key_total = columns * chunk
    page_row = page_table[slot_index]
    page_count = page_row.shape[0]
    page_size = key_total // page_count
    offsets = jnp.arange(page_size, dtype=jnp.int32)
    page_ids = jnp.arange(page_count, dtype=jnp.int32)
    logical_page = jnp.sum(
        page_ids[:, None] * (page_row[:, None] == page_ids[None, :]).astype(jnp.int32), 0
    )
    cached_visible = (logical_page[:, None] * page_size + offsets[None, :]).reshape(
        key_total
    ) < cached_count
    span_visible = lax.dynamic_slice_in_dim(cached_visible, line_id * span, span, 0)
    share = group_rows // lines
    query_index = jnp.arange(group_rows, dtype=jnp.int32)[:, None]
    key_index = jnp.arange(group_rows, dtype=jnp.int32)[None, :]
    fresh_visible = (
        (key_index <= query_index) & (key_index < live_count) & (key_index // share == line_id)
    )
    visible = jnp.concatenate(
        [jnp.broadcast_to(span_visible[None, :], (group_rows, span)), fresh_visible], 1
    )
    scores = jnp.concatenate(
        [score(span_lifted, span_rope), score(fresh_lifted, fresh_rope)], 2
    )
    scores = jnp.where(visible[None], scores, -jnp.inf)
    row_peak = jnp.max(scores, 2)
    safe_peak = jnp.where(row_peak == -jnp.inf, 0.0, row_peak)
    exponent = jnp.exp(scores - safe_peak[:, :, None])
    row_total = jnp.sum(exponent, 2)
    values = jnp.concatenate([span_lifted[:, :, NOPE:], fresh_lifted[:, :, NOPE:]], 0)
    summed = jnp.einsum(
        "hqk,khd->hdq", exponent.astype(jnp.bfloat16), values, preferred_element_type=jnp.float32
    )
    stats = jnp.stack([row_peak, row_total], 1)
    summed_parts, stat_parts = exchange([summed, stats], [("y", False), ("y", False)], 4)
    peak = jnp.max(stat_parts[:, 0, :], 0)
    factor = jnp.exp(stat_parts[:, 0, :] - peak[None, :])
    total = jnp.sum(factor * stat_parts[:, 1, :], 0)
    merged = jnp.sum(factor[:, None, :] * summed_parts, 0)
    attended = (merged / total[None, :]).astype(jnp.bfloat16)
    live_rows = jnp.arange(group_rows, dtype=jnp.int32) < live_count
    attended = jnp.where(live_rows[None, :], attended, jnp.zeros_like(attended))
    out_parts = lax.dot_general(
        w_out, attended, (((0,), (0,)), ((), ())), preferred_element_type=jnp.float32
    ).astype(jnp.bfloat16)
    (out_pieces,) = exchange([out_parts.reshape(columns, -1, group_rows)], [("all", False)], 3)
    summed_out = jnp.sum(out_pieces.astype(jnp.float32), 0)
    result = summed_out.T.astype(jnp.bfloat16)
    return result


def solution(mesh):
    return jax.shard_map(
        body,
        mesh=mesh,
        in_specs=(
            P("row", "col"),
            P("col", None),
            P(),
            P(),
            P(None, "col"),
            P(),
            P("col", None),
            P("row", "col", None),
            P(),
            P(),
            P(),
            P(),
        ),
        out_specs=P("row", "col"),
        check_vma=False,
    )
```

```python
import functools
import math

import jax
import jax.numpy as jnp
from jax import lax
from jax.experimental import pallas as pl
from jax.experimental.pallas import tpu as pltpu
from jax.sharding import PartitionSpec as P

MESH = pl.DeviceIdType.MESH

NOPE = 64
ROPE = 32
VDIM = 64


epsilon = 1e-05


def rms_scale(values, gain):
    return values * lax.rsqrt(jnp.mean(values * values, axis=-1, keepdims=True) + epsilon) * gain


def angle_tables(positions, width):
    half_dim = width // 2
    frequency = 10000.0 ** (-2.0 * jnp.arange(half_dim, dtype=jnp.float32) / width)
    angles = positions.astype(jnp.float32)[:, None] * frequency[None, :]
    return (jnp.cos(angles), jnp.sin(angles))


def rotary(values, cosine, sine_table):
    half_dim = values.shape[-1] // 2
    first_half = values[..., :half_dim]
    second_half = values[..., half_dim:]
    return jnp.concatenate(
        [
            first_half * cosine - second_half * sine_table,
            second_half * cosine + first_half * sine_table,
        ],
        -1,
    )


PLANE_X = 4


def _group_size(group, n):
    return {"all": n, "x": PLANE_X, "y": n // PLANE_X}[group]


def _group_peer(group, n, me, k):
    if group == "x":
        return (me // PLANE_X) * PLANE_X + lax.rem(me % PLANE_X + k, PLANE_X)
    if group == "y":
        return lax.rem(me // PLANE_X + k, n // PLANE_X) * PLANE_X + me % PLANE_X
    return lax.rem(me + k, n)


def _group_slot(group, device):
    if group == "x":
        return device % PLANE_X
    if group == "y":
        return device // PLANE_X
    return device


def _exchange_kernel(n, plan, *refs):
    count = len(plan)
    sources, targets = refs[:count], refs[count : 2 * count]
    send_sem, recv_sem = refs[2 * count :]
    me = lax.axis_index("col")
    barrier = pltpu.get_barrier_semaphore()
    for k in range(1, n):
        pl.semaphore_signal(
            barrier, inc=1, device_id={"col": lax.rem(me + k, n)}, device_id_type=MESH
        )
    pl.semaphore_wait(barrier, n - 1)

    def remote(a, k, peer, landing):
        group, gather = plan[a]
        x_ref = sources[a]
        return pltpu.make_async_remote_copy(
            src_ref=x_ref if gather else x_ref.at[_group_slot(group, peer)],
            dst_ref=targets[a].at[landing],
            send_sem=send_sem.at[a, k],
            recv_sem=recv_sem.at[a, k],
            device_id={"col": peer},
            device_id_type=MESH,
        )

    sends = []
    for a, (group, gather) in enumerate(plan):
        for k in range(1, _group_size(group, n)):
            copy = remote(a, k, _group_peer(group, n, me, k), _group_slot(group, me))
            copy.start()
            sends.append(copy)
    for a, (group, gather) in enumerate(plan):
        mine = _group_slot(group, me)
        if gather:
            targets[a][mine] = sources[a][...]
        else:
            targets[a][mine] = sources[a][mine]
    for copy in sends:
        copy.wait_send()
    for a, (group, gather) in enumerate(plan):
        size = _group_size(group, n)
        for k in range(1, size):
            source = _group_peer(group, n, me, size - k)
            remote(a, k, source, _group_slot(group, source)).wait_recv()


def exchange(arrays, plan, collective_id):
    n = lax.axis_size("col")
    shapes = [
        jax.ShapeDtypeStruct(
            ((_group_size(group, n),) + x.shape) if gather else x.shape, x.dtype
        )
        for x, (group, gather) in zip(arrays, plan)
    ]
    return pl.pallas_call(
        functools.partial(_exchange_kernel, n, tuple(plan)),
        out_shape=shapes,
        in_specs=[pl.BlockSpec(memory_space=pltpu.VMEM)] * len(arrays),
        out_specs=[pl.BlockSpec(memory_space=pltpu.VMEM)] * len(arrays),
        scratch_shapes=[
            pltpu.SemaphoreType.DMA((len(arrays), n)),
            pltpu.SemaphoreType.DMA((len(arrays), n)),
        ],
        compiler_params=pltpu.CompilerParams(collective_id=collective_id, has_side_effects=True),
    )(*arrays)


def body(
    tokens,
    w_down,
    q_gain,
    kv_gain,
    w_q_up,
    w_kv_up,
    w_out,
    latent_cache,
    cache_len,
    new_len,
    page_table,
    home_slot,
):
    columns = lax.axis_size("col")
    column_id = lax.axis_index("col")
    row_id = lax.axis_index("row")
    lines = columns // PLANE_X
    line_id = column_id // PLANE_X
    lane_id = column_id % PLANE_X
    group_rows = tokens.shape[0]
    own_rows = group_rows // columns
    q_width = q_gain.shape[0]
    kv_width = kv_gain.shape[0]
    slot_index = home_slot[row_id]
    cached_count = cache_len[slot_index]
    live_count = new_len[row_id]
    partial_sums = jnp.dot(tokens, w_down, preferred_element_type=jnp.float32)
    pieces, line_query_weight = exchange(
        [partial_sums.astype(jnp.bfloat16).reshape(columns, -1, 128), w_q_up.T],
        [("all", False), ("y", True)],
        0,
    )
    combined = jnp.sum(pieces.astype(jnp.float32), 0).reshape(own_rows, -1)
    own_position = cached_count + column_id * own_rows + jnp.arange(own_rows, dtype=jnp.int32)
    own_cos, own_sin = angle_tables(own_position, ROPE)
    own_query = rms_scale(combined[:, :q_width], q_gain).astype(jnp.bfloat16)
    own_latent = rms_scale(combined[:, q_width : q_width + kv_width], kv_gain).astype(jnp.bfloat16)
    own_rope = rotary(combined[:, q_width + kv_width :], own_cos, own_sin).astype(jnp.bfloat16)
    own_rows_all = jnp.concatenate([own_query, own_latent, own_rope], 1)
    segment = lax.all_gather(latent_cache, "row", axis=0, tiled=True)
    matches = jnp.arange(segment.shape[0], dtype=jnp.int32) == slot_index
    own_cache = jnp.sum(
        jnp.where(matches[:, None, None], segment.astype(jnp.float32), 0.0), 0
    ).astype(jnp.bfloat16)
    chunk = own_cache.shape[0]
    cache_parts, all_rows = exchange(
        [own_cache.T, own_rows_all], [("x", True), ("all", True)], 2
    )
    all_rows = all_rows.reshape(group_rows, -1)
    query_latent = all_rows[:, :q_width]
    fresh_latents = all_rows[:, q_width:]
    query_cos, query_sin = angle_tables(
        cached_count + jnp.arange(group_rows, dtype=jnp.int32), ROPE
    )
    projected = jnp.einsum(
        "qk,hdk->hqd", query_latent, line_query_weight, preferred_element_type=jnp.float32
    )
    head_queries = jnp.concatenate(
        [
            projected[:, :, :NOPE],
            rotary(projected[:, :, NOPE:], query_cos[None], query_sin[None]),
        ],
        2,
    ).astype(jnp.bfloat16)
    head_width = NOPE + VDIM
    heads = columns
    line_weight = lax.dynamic_index_in_dim(
        w_kv_up.reshape(kv_width, lines, PLANE_X, head_width), lane_id, axis=2, keepdims=False
    ).reshape(kv_width, lines * head_width)
    span = PLANE_X * chunk
    span_latents = cache_parts[:, :kv_width, :].transpose(0, 2, 1).reshape(span, kv_width)
    span_rope = cache_parts[:, kv_width:, :].transpose(0, 2, 1).reshape(span, ROPE)
    span_lifted = (
        jnp.dot(span_latents, line_weight, preferred_element_type=jnp.float32)
        .astype(jnp.bfloat16)
        .reshape(span, lines, head_width)
    )
    fresh_lifted = (
        jnp.dot(fresh_latents[:, :kv_width], line_weight, preferred_element_type=jnp.float32)
        .astype(jnp.bfloat16)
        .reshape(group_rows, lines, head_width)
    )
    fresh_rope = fresh_latents[:, kv_width:]
    q_nope = head_queries[:, :, :NOPE]
    q_rope = head_queries[:, :, NOPE:]
    score_scale = 1.0 / math.sqrt(NOPE + ROPE)

    def score(lifted, rope):
        return (
            jnp.einsum("hqd,khd->hqk", q_nope, lifted[:, :, :NOPE], preferred_element_type=jnp.float32)
            + jnp.einsum("hqd,kd->hqk", q_rope, rope, preferred_element_type=jnp.float32)
        ) * score_scale

    key_total = columns * chunk
    page_row = page_table[slot_index]
    page_count = page_row.shape[0]
    page_size = key_total // page_count
    offsets = jnp.arange(page_size, dtype=jnp.int32)
    page_ids = jnp.arange(page_count, dtype=jnp.int32)
    logical_page = jnp.sum(
        page_ids[:, None] * (page_row[:, None] == page_ids[None, :]).astype(jnp.int32), 0
    )
    cached_visible = (logical_page[:, None] * page_size + offsets[None, :]).reshape(
        key_total
    ) < cached_count
    span_visible = lax.dynamic_slice_in_dim(cached_visible, line_id * span, span, 0)
    share = group_rows // lines
    query_index = jnp.arange(group_rows, dtype=jnp.int32)[:, None]
    key_index = jnp.arange(group_rows, dtype=jnp.int32)[None, :]
    fresh_visible = (
        (key_index <= query_index) & (key_index < live_count) & (key_index // share == line_id)
    )
    visible = jnp.concatenate(
        [jnp.broadcast_to(span_visible[None, :], (group_rows, span)), fresh_visible], 1
    )
    scores = jnp.concatenate(
        [score(span_lifted, span_rope), score(fresh_lifted, fresh_rope)], 2
    )
    scores = jnp.where(visible[None], scores, -jnp.inf)
    row_peak = jnp.max(scores, 2)
    safe_peak = jnp.where(row_peak == -jnp.inf, 0.0, row_peak)
    exponent = jnp.exp(scores - safe_peak[:, :, None])
    row_total = jnp.sum(exponent, 2)
    values = jnp.concatenate([span_lifted[:, :, NOPE:], fresh_lifted[:, :, NOPE:]], 0)
    summed = jnp.einsum(
        "hqk,khd->hdq", exponent.astype(jnp.bfloat16), values, preferred_element_type=jnp.float32
    )
    stats = jnp.stack([row_peak, row_total], 1)
    summed_parts, stat_parts = exchange(
        [summed.astype(jnp.bfloat16), stats], [("y", False), ("y", False)], 4
    )
    peak = jnp.max(stat_parts[:, 0, :], 0)
    factor = jnp.exp(stat_parts[:, 0, :] - peak[None, :])
    total = jnp.sum(factor * stat_parts[:, 1, :], 0)
    merged = jnp.sum(factor[:, None, :] * summed_parts.astype(jnp.float32), 0)
    attended = (merged / total[None, :]).astype(jnp.bfloat16)
    live_rows = jnp.arange(group_rows, dtype=jnp.int32) < live_count
    attended = jnp.where(live_rows[None, :], attended, jnp.zeros_like(attended))
    out_parts = lax.dot_general(
        w_out, attended, (((0,), (0,)), ((), ())), preferred_element_type=jnp.float32
    ).astype(jnp.bfloat16)
    (out_pieces,) = exchange([out_parts.reshape(columns, -1, group_rows)], [("all", False)], 3)
    summed_out = jnp.sum(out_pieces.astype(jnp.float32), 0)
    result = summed_out.T.astype(jnp.bfloat16)
    return result


def solution(mesh):
    return jax.shard_map(
        body,
        mesh=mesh,
        in_specs=(
            P("row", "col"),
            P("col", None),
            P(),
            P(),
            P(None, "col"),
            P(),
            P("col", None),
            P("row", "col", None),
            P(),
            P(),
            P(),
            P(),
        ),
        out_specs=P("row", "col"),
        check_vma=False,
    )
```

```python
import functools
import math

import jax
import jax.numpy as jnp
from jax import lax
from jax.experimental import pallas as pl
from jax.experimental.pallas import tpu as pltpu
from jax.sharding import PartitionSpec as P

MESH = pl.DeviceIdType.MESH

NOPE = 64
ROPE = 32
VDIM = 64


epsilon = 1e-05


def rms_scale(values, gain):
    return values * lax.rsqrt(jnp.mean(values * values, axis=-1, keepdims=True) + epsilon) * gain


def angle_tables(positions, width):
    half_dim = width // 2
    frequency = 10000.0 ** (-2.0 * jnp.arange(half_dim, dtype=jnp.float32) / width)
    angles = positions.astype(jnp.float32)[:, None] * frequency[None, :]
    return (jnp.cos(angles), jnp.sin(angles))


def rotary(values, cosine, sine_table):
    half_dim = values.shape[-1] // 2
    first_half = values[..., :half_dim]
    second_half = values[..., half_dim:]
    return jnp.concatenate(
        [
            first_half * cosine - second_half * sine_table,
            second_half * cosine + first_half * sine_table,
        ],
        -1,
    )


PLANE_X = 4


def _group_size(group, n):
    return {"all": n, "x": PLANE_X, "y": n // PLANE_X}[group]


def _group_peer(group, n, me, k):
    if group == "x":
        return (me // PLANE_X) * PLANE_X + lax.rem(me % PLANE_X + k, PLANE_X)
    if group == "y":
        return lax.rem(me // PLANE_X + k, n // PLANE_X) * PLANE_X + me % PLANE_X
    return lax.rem(me + k, n)


def _group_slot(group, device):
    if group == "x":
        return device % PLANE_X
    if group == "y":
        return device // PLANE_X
    return device


def _exchange_kernel(n, plan, *refs):
    count = len(plan)
    sources, targets = refs[:count], refs[count : 2 * count]
    send_sem, recv_sem = refs[2 * count :]
    me = lax.axis_index("col")
    barrier = pltpu.get_barrier_semaphore()
    for k in range(1, n):
        pl.semaphore_signal(
            barrier, inc=1, device_id={"col": lax.rem(me + k, n)}, device_id_type=MESH
        )
    pl.semaphore_wait(barrier, n - 1)

    def remote(a, k, peer, landing):
        group, gather = plan[a]
        x_ref = sources[a]
        return pltpu.make_async_remote_copy(
            src_ref=x_ref if gather else x_ref.at[_group_slot(group, peer)],
            dst_ref=targets[a].at[landing],
            send_sem=send_sem.at[a, k],
            recv_sem=recv_sem.at[a, k],
            device_id={"col": peer},
            device_id_type=MESH,
        )

    sends = []
    for a, (group, gather) in enumerate(plan):
        for k in range(1, _group_size(group, n)):
            copy = remote(a, k, _group_peer(group, n, me, k), _group_slot(group, me))
            copy.start()
            sends.append(copy)
    for a, (group, gather) in enumerate(plan):
        mine = _group_slot(group, me)
        if gather:
            targets[a][mine] = sources[a][...]
        else:
            targets[a][mine] = sources[a][mine]
    for copy in sends:
        copy.wait_send()
    for a, (group, gather) in enumerate(plan):
        size = _group_size(group, n)
        for k in range(1, size):
            source = _group_peer(group, n, me, size - k)
            remote(a, k, source, _group_slot(group, source)).wait_recv()


def exchange(arrays, plan, collective_id):
    n = lax.axis_size("col")
    shapes = [
        jax.ShapeDtypeStruct(
            ((_group_size(group, n),) + x.shape) if gather else x.shape, x.dtype
        )
        for x, (group, gather) in zip(arrays, plan)
    ]
    return pl.pallas_call(
        functools.partial(_exchange_kernel, n, tuple(plan)),
        out_shape=shapes,
        in_specs=[pl.BlockSpec(memory_space=pltpu.VMEM)] * len(arrays),
        out_specs=[pl.BlockSpec(memory_space=pltpu.VMEM)] * len(arrays),
        scratch_shapes=[
            pltpu.SemaphoreType.DMA((len(arrays), n)),
            pltpu.SemaphoreType.DMA((len(arrays), n)),
        ],
        compiler_params=pltpu.CompilerParams(collective_id=collective_id, has_side_effects=True),
    )(*arrays)


def body(
    tokens,
    w_down,
    q_gain,
    kv_gain,
    w_q_up,
    w_kv_up,
    w_out,
    latent_cache,
    cache_len,
    new_len,
    page_table,
    home_slot,
):
    columns = lax.axis_size("col")
    column_id = lax.axis_index("col")
    row_id = lax.axis_index("row")
    lines = columns // PLANE_X
    line_id = column_id // PLANE_X
    lane_id = column_id % PLANE_X
    group_rows = tokens.shape[0]
    own_rows = group_rows // columns
    q_width = q_gain.shape[0]
    kv_width = kv_gain.shape[0]
    slot_index = home_slot[row_id]
    cached_count = cache_len[slot_index]
    live_count = new_len[row_id]
    partial_sums = jnp.dot(tokens, w_down, preferred_element_type=jnp.float32)
    pieces, line_query_weight = exchange(
        [partial_sums.astype(jnp.bfloat16).reshape(columns, -1, 128), w_q_up.T],
        [("all", False), ("y", True)],
        0,
    )
    combined = jnp.sum(pieces.astype(jnp.float32), 0).reshape(own_rows, -1)
    own_position = cached_count + column_id * own_rows + jnp.arange(own_rows, dtype=jnp.int32)
    own_cos, own_sin = angle_tables(own_position, ROPE)
    own_query = rms_scale(combined[:, :q_width], q_gain).astype(jnp.bfloat16)
    own_latent = rms_scale(combined[:, q_width : q_width + kv_width], kv_gain).astype(jnp.bfloat16)
    own_rope = rotary(combined[:, q_width + kv_width :], own_cos, own_sin).astype(jnp.bfloat16)
    own_rows_all = jnp.concatenate([own_query, own_latent, own_rope], 1)
    segment = lax.all_gather(latent_cache, "row", axis=0, tiled=True)
    matches = jnp.arange(segment.shape[0], dtype=jnp.int32) == slot_index
    own_cache = jnp.sum(
        jnp.where(matches[:, None, None], segment.astype(jnp.float32), 0.0), 0
    ).astype(jnp.bfloat16)
    chunk = own_cache.shape[0]
    cache_parts, all_rows = exchange(
        [own_cache.T, own_rows_all], [("x", True), ("all", True)], 2
    )
    all_rows = all_rows.reshape(group_rows, -1)
    query_latent = all_rows[:, :q_width]
    fresh_latents = all_rows[:, q_width:]
    query_cos, query_sin = angle_tables(
        cached_count + jnp.arange(group_rows, dtype=jnp.int32), ROPE
    )
    projected = jnp.einsum(
        "qk,hdk->hqd", query_latent, line_query_weight, preferred_element_type=jnp.float32
    )
    head_queries = jnp.concatenate(
        [
            projected[:, :, :NOPE],
            rotary(projected[:, :, NOPE:], query_cos[None], query_sin[None]),
        ],
        2,
    ).astype(jnp.bfloat16)
    head_width = NOPE + VDIM
    heads = columns
    line_weight = lax.dynamic_index_in_dim(
        w_kv_up.reshape(kv_width, lines, PLANE_X, head_width), lane_id, axis=2, keepdims=False
    ).reshape(kv_width, lines * head_width)
    span = PLANE_X * chunk
    span_latents = cache_parts[:, :kv_width, :].transpose(0, 2, 1).reshape(span, kv_width)
    span_rope = cache_parts[:, kv_width:, :].transpose(0, 2, 1).reshape(span, ROPE)
    key_latents = jnp.concatenate([span_latents, fresh_latents[:, :kv_width]], 0)
    key_rope = jnp.concatenate([span_rope, fresh_latents[:, kv_width:]], 0)
    key_count = key_latents.shape[0]
    lifted = (
        jnp.dot(key_latents, line_weight, preferred_element_type=jnp.float32)
        .astype(jnp.bfloat16)
        .reshape(key_count, lines, head_width)
    )
    keys = jnp.concatenate(
        [
            lifted[:, :, :NOPE],
            jnp.broadcast_to(key_rope[:, None, :], (key_count, lines, ROPE)),
        ],
        2,
    )
    score_scale = 1.0 / math.sqrt(NOPE + ROPE)
    key_total = columns * chunk
    page_row = page_table[slot_index]
    page_count = page_row.shape[0]
    page_size = key_total // page_count
    offsets = jnp.arange(page_size, dtype=jnp.int32)
    page_ids = jnp.arange(page_count, dtype=jnp.int32)
    logical_page = jnp.sum(
        page_ids[:, None] * (page_row[:, None] == page_ids[None, :]).astype(jnp.int32), 0
    )
    cached_visible = (logical_page[:, None] * page_size + offsets[None, :]).reshape(
        key_total
    ) < cached_count
    span_visible = lax.dynamic_slice_in_dim(cached_visible, line_id * span, span, 0)
    share = group_rows // lines
    query_index = jnp.arange(group_rows, dtype=jnp.int32)[:, None]
    key_index = jnp.arange(group_rows, dtype=jnp.int32)[None, :]
    fresh_visible = (
        (key_index <= query_index) & (key_index < live_count) & (key_index // share == line_id)
    )
    visible = jnp.concatenate(
        [jnp.broadcast_to(span_visible[None, :], (group_rows, span)), fresh_visible], 1
    )
    scores = (
        jnp.einsum("hqd,khd->hqk", head_queries, keys, preferred_element_type=jnp.float32)
        * score_scale
    )
    scores = jnp.where(visible[None], scores, -jnp.inf)
    row_peak = jnp.max(scores, 2)
    safe_peak = jnp.where(row_peak == -jnp.inf, 0.0, row_peak)
    exponent = jnp.exp(scores - safe_peak[:, :, None])
    row_total = jnp.sum(exponent, 2)
    values = lifted[:, :, NOPE:]
    summed = jnp.einsum(
        "hqk,khd->hdq", exponent.astype(jnp.bfloat16), values, preferred_element_type=jnp.float32
    )
    stats = jnp.stack([row_peak, row_total], 1)
    summed_parts, stat_parts = exchange(
        [summed.astype(jnp.bfloat16), stats], [("y", False), ("y", False)], 4
    )
    peak = jnp.max(stat_parts[:, 0, :], 0)
    factor = jnp.exp(stat_parts[:, 0, :] - peak[None, :])
    total = jnp.sum(factor * stat_parts[:, 1, :], 0)
    merged = jnp.sum(factor[:, None, :] * summed_parts.astype(jnp.float32), 0)
    attended = (merged / total[None, :]).astype(jnp.bfloat16)
    live_rows = jnp.arange(group_rows, dtype=jnp.int32) < live_count
    attended = jnp.where(live_rows[None, :], attended, jnp.zeros_like(attended))
    out_parts = lax.dot_general(
        w_out, attended, (((0,), (0,)), ((), ())), preferred_element_type=jnp.float32
    ).astype(jnp.bfloat16)
    (out_pieces,) = exchange([out_parts.reshape(columns, -1, group_rows)], [("all", False)], 3)
    summed_out = jnp.sum(out_pieces.astype(jnp.float32), 0)
    result = summed_out.T.astype(jnp.bfloat16)
    return result


def solution(mesh):
    return jax.shard_map(
        body,
        mesh=mesh,
        in_specs=(
            P("row", "col"),
            P("col", None),
            P(),
            P(),
            P(None, "col"),
            P(),
            P("col", None),
            P("row", "col", None),
            P(),
            P(),
            P(),
            P(),
        ),
        out_specs=P("row", "col"),
        check_vma=False,
    )
```

```python
import functools
import math

import jax
import jax.numpy as jnp
from jax import lax
from jax.experimental import pallas as pl
from jax.experimental.pallas import tpu as pltpu
from jax.sharding import PartitionSpec as P

MESH = pl.DeviceIdType.MESH

NOPE = 64
ROPE = 32
VDIM = 64


epsilon = 1e-05


def rms_scale(values, gain):
    return values * lax.rsqrt(jnp.mean(values * values, axis=-1, keepdims=True) + epsilon) * gain


def angle_tables(positions, width):
    half_dim = width // 2
    frequency = 10000.0 ** (-2.0 * jnp.arange(half_dim, dtype=jnp.float32) / width)
    angles = positions.astype(jnp.float32)[:, None] * frequency[None, :]
    return (jnp.cos(angles), jnp.sin(angles))


def rotary(values, cosine, sine_table):
    half_dim = values.shape[-1] // 2
    first_half = values[..., :half_dim]
    second_half = values[..., half_dim:]
    return jnp.concatenate(
        [
            first_half * cosine - second_half * sine_table,
            second_half * cosine + first_half * sine_table,
        ],
        -1,
    )


PLANE_X = 4


def _group_size(group, n):
    return {"all": n, "x": PLANE_X, "y": n // PLANE_X}[group]


def _group_peer(group, n, me, k):
    if group == "x":
        return (me // PLANE_X) * PLANE_X + lax.rem(me % PLANE_X + k, PLANE_X)
    if group == "y":
        return lax.rem(me // PLANE_X + k, n // PLANE_X) * PLANE_X + me % PLANE_X
    return lax.rem(me + k, n)


def _group_slot(group, device):
    if group == "x":
        return device % PLANE_X
    if group == "y":
        return device // PLANE_X
    return device


def _exchange_kernel(n, plan, *refs):
    count = len(plan)
    sources, targets = refs[:count], refs[count : 2 * count]
    send_sem, recv_sem = refs[2 * count :]
    me = lax.axis_index("col")
    barrier = pltpu.get_barrier_semaphore()
    for k in range(1, n):
        pl.semaphore_signal(
            barrier, inc=1, device_id={"col": lax.rem(me + k, n)}, device_id_type=MESH
        )
    pl.semaphore_wait(barrier, n - 1)

    def remote(a, k, peer, landing):
        group, gather = plan[a]
        x_ref = sources[a]
        return pltpu.make_async_remote_copy(
            src_ref=x_ref if gather else x_ref.at[_group_slot(group, peer)],
            dst_ref=targets[a].at[landing],
            send_sem=send_sem.at[a, k],
            recv_sem=recv_sem.at[a, k],
            device_id={"col": peer},
            device_id_type=MESH,
        )

    sends = []
    for a, (group, gather) in enumerate(plan):
        for k in range(1, _group_size(group, n)):
            copy = remote(a, k, _group_peer(group, n, me, k), _group_slot(group, me))
            copy.start()
            sends.append(copy)
    for a, (group, gather) in enumerate(plan):
        mine = _group_slot(group, me)
        if gather:
            targets[a][mine] = sources[a][...]
        else:
            targets[a][mine] = sources[a][mine]
    for copy in sends:
        copy.wait_send()
    for a, (group, gather) in enumerate(plan):
        size = _group_size(group, n)
        for k in range(1, size):
            source = _group_peer(group, n, me, size - k)
            remote(a, k, source, _group_slot(group, source)).wait_recv()


def exchange(arrays, plan, collective_id):
    n = lax.axis_size("col")
    shapes = [
        jax.ShapeDtypeStruct(
            ((_group_size(group, n),) + x.shape) if gather else x.shape, x.dtype
        )
        for x, (group, gather) in zip(arrays, plan)
    ]
    return pl.pallas_call(
        functools.partial(_exchange_kernel, n, tuple(plan)),
        out_shape=shapes,
        in_specs=[pl.BlockSpec(memory_space=pltpu.VMEM)] * len(arrays),
        out_specs=[pl.BlockSpec(memory_space=pltpu.VMEM)] * len(arrays),
        scratch_shapes=[
            pltpu.SemaphoreType.DMA((len(arrays), n)),
            pltpu.SemaphoreType.DMA((len(arrays), n)),
        ],
        compiler_params=pltpu.CompilerParams(collective_id=collective_id, has_side_effects=True),
    )(*arrays)


def body(
    tokens,
    w_down,
    q_gain,
    kv_gain,
    w_q_up,
    w_kv_up,
    w_out,
    latent_cache,
    cache_len,
    new_len,
    page_table,
    home_slot,
):
    columns = lax.axis_size("col")
    column_id = lax.axis_index("col")
    row_id = lax.axis_index("row")
    lines = columns // PLANE_X
    line_id = column_id // PLANE_X
    lane_id = column_id % PLANE_X
    group_rows = tokens.shape[0]
    own_rows = group_rows // columns
    q_width = q_gain.shape[0]
    kv_width = kv_gain.shape[0]
    request_ids = jnp.arange(home_slot.shape[0], dtype=jnp.int32)
    slot_index = jnp.sum(jnp.where(request_ids == row_id, home_slot, 0))
    cached_count = jnp.sum(jnp.where(request_ids == slot_index, cache_len, 0))
    live_count = jnp.sum(jnp.where(request_ids == row_id, new_len, 0))
    partial_sums = jnp.dot(tokens, w_down, preferred_element_type=jnp.float32)
    pieces, line_query_weight = exchange(
        [partial_sums.astype(jnp.bfloat16).reshape(columns, -1, 128), w_q_up.T],
        [("all", False), ("y", True)],
        0,
    )
    combined = jnp.sum(pieces.astype(jnp.float32), 0).reshape(own_rows, -1)
    own_position = cached_count + column_id * own_rows + jnp.arange(own_rows, dtype=jnp.int32)
    own_cos, own_sin = angle_tables(own_position, ROPE)
    own_query = rms_scale(combined[:, :q_width], q_gain).astype(jnp.bfloat16)
    own_latent = rms_scale(combined[:, q_width : q_width + kv_width], kv_gain).astype(jnp.bfloat16)
    own_rope = rotary(combined[:, q_width + kv_width :], own_cos, own_sin).astype(jnp.bfloat16)
    own_rows_all = jnp.concatenate([own_query, own_latent, own_rope], 1)
    segment = lax.all_gather(latent_cache, "row", axis=0, tiled=True)
    matches = jnp.arange(segment.shape[0], dtype=jnp.int32) == slot_index
    own_cache = jnp.sum(
        jnp.where(matches[:, None, None], segment.astype(jnp.float32), 0.0), 0
    ).astype(jnp.bfloat16)
    chunk = own_cache.shape[0]
    cache_parts, all_rows = exchange(
        [own_cache.T, own_rows_all], [("x", True), ("all", True)], 2
    )
    all_rows = all_rows.reshape(group_rows, -1)
    query_latent = all_rows[:, :q_width]
    fresh_latents = all_rows[:, q_width:]
    query_cos, query_sin = angle_tables(
        cached_count + jnp.arange(group_rows, dtype=jnp.int32), ROPE
    )
    projected = jnp.einsum(
        "qk,hdk->hqd", query_latent, line_query_weight, preferred_element_type=jnp.float32
    )
    head_queries = jnp.concatenate(
        [
            projected[:, :, :NOPE],
            rotary(projected[:, :, NOPE:], query_cos[None], query_sin[None]),
        ],
        2,
    ).astype(jnp.bfloat16)
    head_width = NOPE + VDIM
    heads = columns
    line_weight = lax.dynamic_slice_in_dim(
        w_kv_up.reshape(kv_width, lines, PLANE_X * head_width),
        lane_id * head_width,
        head_width,
        2,
    ).reshape(kv_width, lines * head_width)
    span = PLANE_X * chunk
    span_latents = cache_parts[:, :kv_width, :].transpose(0, 2, 1).reshape(span, kv_width)
    span_rope = cache_parts[:, kv_width:, :].transpose(0, 2, 1).reshape(span, ROPE)
    key_latents = jnp.concatenate([span_latents, fresh_latents[:, :kv_width]], 0)
    key_rope = jnp.concatenate([span_rope, fresh_latents[:, kv_width:]], 0)
    key_count = key_latents.shape[0]
    lifted = (
        jnp.dot(key_latents, line_weight, preferred_element_type=jnp.float32)
        .astype(jnp.bfloat16)
        .reshape(key_count, lines, head_width)
    )
    keys = jnp.concatenate(
        [
            lifted[:, :, :NOPE],
            jnp.broadcast_to(key_rope[:, None, :], (key_count, lines, ROPE)),
        ],
        2,
    )
    score_scale = 1.0 / math.sqrt(NOPE + ROPE)
    key_total = columns * chunk
    page_row = page_table[slot_index]
    page_count = page_row.shape[0]
    page_size = key_total // page_count
    offsets = jnp.arange(page_size, dtype=jnp.int32)
    page_ids = jnp.arange(page_count, dtype=jnp.int32)
    logical_page = jnp.sum(
        page_ids[:, None] * (page_row[:, None] == page_ids[None, :]).astype(jnp.int32), 0
    )
    cached_visible = (logical_page[:, None] * page_size + offsets[None, :]).reshape(
        key_total
    ) < cached_count
    span_visible = lax.dynamic_slice_in_dim(cached_visible, line_id * span, span, 0)
    share = group_rows // lines
    query_index = jnp.arange(group_rows, dtype=jnp.int32)[:, None]
    key_index = jnp.arange(group_rows, dtype=jnp.int32)[None, :]
    fresh_visible = (
        (key_index <= query_index) & (key_index < live_count) & (key_index // share == line_id)
    )
    visible = jnp.concatenate(
        [jnp.broadcast_to(span_visible[None, :], (group_rows, span)), fresh_visible], 1
    )
    scores = (
        jnp.einsum("hqd,khd->hqk", head_queries, keys, preferred_element_type=jnp.float32)
        * score_scale
    )
    scores = jnp.where(visible[None], scores, -jnp.inf)
    row_peak = jnp.max(scores, 2)
    safe_peak = jnp.where(row_peak == -jnp.inf, 0.0, row_peak)
    exponent = jnp.exp(scores - safe_peak[:, :, None])
    row_total = jnp.sum(exponent, 2)
    values = lifted[:, :, NOPE:]
    summed = jnp.einsum(
        "hqk,khd->hdq", exponent.astype(jnp.bfloat16), values, preferred_element_type=jnp.float32
    )
    stats = jnp.stack([row_peak, row_total], 1)
    summed_parts, stat_parts = exchange(
        [summed.astype(jnp.bfloat16), stats], [("y", False), ("y", False)], 4
    )
    peak = jnp.max(stat_parts[:, 0, :], 0)
    factor = jnp.exp(stat_parts[:, 0, :] - peak[None, :])
    total = jnp.sum(factor * stat_parts[:, 1, :], 0)
    merged = jnp.sum(factor[:, None, :] * summed_parts.astype(jnp.float32), 0)
    attended = (merged / total[None, :]).astype(jnp.bfloat16)
    live_rows = jnp.arange(group_rows, dtype=jnp.int32) < live_count
    attended = jnp.where(live_rows[None, :], attended, jnp.zeros_like(attended))
    out_parts = lax.dot_general(
        w_out, attended, (((0,), (0,)), ((), ())), preferred_element_type=jnp.float32
    ).astype(jnp.bfloat16)
    (out_pieces,) = exchange([out_parts.reshape(columns, -1, group_rows)], [("all", False)], 3)
    summed_out = jnp.sum(out_pieces.astype(jnp.float32), 0)
    result = summed_out.T.astype(jnp.bfloat16)
    return result


def solution(mesh):
    return jax.shard_map(
        body,
        mesh=mesh,
        in_specs=(
            P("row", "col"),
            P("col", None),
            P(),
            P(),
            P(None, "col"),
            P(),
            P("col", None),
            P("row", "col", None),
            P(),
            P(),
            P(),
            P(),
        ),
        out_specs=P("row", "col"),
        check_vma=False,
    )
```

```python
import functools
import math

import jax
import jax.numpy as jnp
from jax import lax
from jax.experimental import pallas as pl
from jax.experimental.pallas import tpu as pltpu
from jax.sharding import PartitionSpec as P

MESH = pl.DeviceIdType.MESH

NOPE = 64
ROPE = 32
VDIM = 64


epsilon = 1e-05


def rms_scale(values, gain):
    return values * lax.rsqrt(jnp.mean(values * values, axis=-1, keepdims=True) + epsilon) * gain


def angle_tables(positions, width):
    half_dim = width // 2
    frequency = 10000.0 ** (-2.0 * jnp.arange(half_dim, dtype=jnp.float32) / width)
    angles = positions.astype(jnp.float32)[:, None] * frequency[None, :]
    return (jnp.cos(angles), jnp.sin(angles))


def rotary(values, cosine, sine_table):
    half_dim = values.shape[-1] // 2
    first_half = values[..., :half_dim]
    second_half = values[..., half_dim:]
    return jnp.concatenate(
        [
            first_half * cosine - second_half * sine_table,
            second_half * cosine + first_half * sine_table,
        ],
        -1,
    )


PLANE_X = 4


def _group_size(group, n):
    return {"all": n, "x": PLANE_X, "y": n // PLANE_X}[group]


def _group_peer(group, n, me, k):
    if group == "x":
        return (me // PLANE_X) * PLANE_X + lax.rem(me % PLANE_X + k, PLANE_X)
    if group == "y":
        return lax.rem(me // PLANE_X + k, n // PLANE_X) * PLANE_X + me % PLANE_X
    return lax.rem(me + k, n)


def _group_slot(group, device):
    if group == "x":
        return device % PLANE_X
    if group == "y":
        return device // PLANE_X
    return device


def _exchange_kernel(n, plan, *refs):
    count = len(plan)
    sources, targets = refs[:count], refs[count : 2 * count]
    send_sem, recv_sem = refs[2 * count :]
    me = lax.axis_index("col")
    barrier = pltpu.get_barrier_semaphore()
    for k in range(1, n):
        pl.semaphore_signal(
            barrier, inc=1, device_id={"col": lax.rem(me + k, n)}, device_id_type=MESH
        )
    pl.semaphore_wait(barrier, n - 1)

    def remote(a, k, peer, landing):
        group, gather = plan[a]
        x_ref = sources[a]
        return pltpu.make_async_remote_copy(
            src_ref=x_ref if gather else x_ref.at[_group_slot(group, peer)],
            dst_ref=targets[a].at[landing],
            send_sem=send_sem.at[a, k],
            recv_sem=recv_sem.at[a, k],
            device_id={"col": peer},
            device_id_type=MESH,
        )

    sends = []
    for a, (group, gather) in enumerate(plan):
        for k in range(1, _group_size(group, n)):
            copy = remote(a, k, _group_peer(group, n, me, k), _group_slot(group, me))
            copy.start()
            sends.append(copy)
    for a, (group, gather) in enumerate(plan):
        mine = _group_slot(group, me)
        if gather:
            targets[a][mine] = sources[a][...]
        else:
            targets[a][mine] = sources[a][mine]
    for copy in sends:
        copy.wait_send()
    for a, (group, gather) in enumerate(plan):
        size = _group_size(group, n)
        for k in range(1, size):
            source = _group_peer(group, n, me, size - k)
            remote(a, k, source, _group_slot(group, source)).wait_recv()


def exchange(arrays, plan, collective_id):
    n = lax.axis_size("col")
    shapes = [
        jax.ShapeDtypeStruct(
            ((_group_size(group, n),) + x.shape) if gather else x.shape, x.dtype
        )
        for x, (group, gather) in zip(arrays, plan)
    ]
    return pl.pallas_call(
        functools.partial(_exchange_kernel, n, tuple(plan)),
        out_shape=shapes,
        in_specs=[pl.BlockSpec(memory_space=pltpu.VMEM)] * len(arrays),
        out_specs=[pl.BlockSpec(memory_space=pltpu.VMEM)] * len(arrays),
        scratch_shapes=[
            pltpu.SemaphoreType.DMA((len(arrays), n)),
            pltpu.SemaphoreType.DMA((len(arrays), n)),
        ],
        compiler_params=pltpu.CompilerParams(collective_id=collective_id, has_side_effects=True),
    )(*arrays)


def body(
    tokens,
    w_down,
    q_gain,
    kv_gain,
    w_q_up,
    w_kv_up,
    w_out,
    latent_cache,
    cache_len,
    new_len,
    page_table,
    home_slot,
):
    columns = lax.axis_size("col")
    column_id = lax.axis_index("col")
    row_id = lax.axis_index("row")
    lines = columns // PLANE_X
    line_id = column_id // PLANE_X
    lane_id = column_id % PLANE_X
    group_rows = tokens.shape[0]
    own_rows = group_rows // columns
    q_width = q_gain.shape[0]
    kv_width = kv_gain.shape[0]
    partial_sums = jnp.dot(tokens, w_down, preferred_element_type=jnp.float32)
    pieces, line_query_weight = exchange(
        [partial_sums.astype(jnp.bfloat16).reshape(columns, -1, 128), w_q_up.T],
        [("all", False), ("y", True)],
        0,
    )
    pieces, line_query_weight, home_slot, cache_len, new_len = lax.optimization_barrier(
        (pieces, line_query_weight, home_slot, cache_len, new_len)
    )
    request_ids = jnp.arange(home_slot.shape[0], dtype=jnp.int32)
    slot_index = jnp.sum(jnp.where(request_ids == row_id, home_slot, 0))
    cached_count = jnp.sum(jnp.where(request_ids == slot_index, cache_len, 0))
    live_count = jnp.sum(jnp.where(request_ids == row_id, new_len, 0))
    combined = jnp.sum(pieces.astype(jnp.float32), 0).reshape(own_rows, -1)
    own_position = cached_count + column_id * own_rows + jnp.arange(own_rows, dtype=jnp.int32)
    own_cos, own_sin = angle_tables(own_position, ROPE)
    own_query = rms_scale(combined[:, :q_width], q_gain).astype(jnp.bfloat16)
    own_latent = rms_scale(combined[:, q_width : q_width + kv_width], kv_gain).astype(jnp.bfloat16)
    own_rope = rotary(combined[:, q_width + kv_width :], own_cos, own_sin).astype(jnp.bfloat16)
    own_rows_all = jnp.concatenate([own_query, own_latent, own_rope], 1)
    segment = lax.all_gather(latent_cache, "row", axis=0, tiled=True)
    matches = jnp.arange(segment.shape[0], dtype=jnp.int32) == slot_index
    own_cache = jnp.sum(
        jnp.where(matches[:, None, None], segment.astype(jnp.float32), 0.0), 0
    ).astype(jnp.bfloat16)
    chunk = own_cache.shape[0]
    cache_parts, all_rows = exchange(
        [own_cache.T, own_rows_all], [("x", True), ("all", True)], 2
    )
    all_rows = all_rows.reshape(group_rows, -1)
    query_latent = all_rows[:, :q_width]
    fresh_latents = all_rows[:, q_width:]
    query_cos, query_sin = angle_tables(
        cached_count + jnp.arange(group_rows, dtype=jnp.int32), ROPE
    )
    projected = jnp.einsum(
        "qk,hdk->hqd", query_latent, line_query_weight, preferred_element_type=jnp.float32
    )
    head_queries = jnp.concatenate(
        [
            projected[:, :, :NOPE],
            rotary(projected[:, :, NOPE:], query_cos[None], query_sin[None]),
        ],
        2,
    ).astype(jnp.bfloat16)
    head_width = NOPE + VDIM
    heads = columns
    line_weight = lax.dynamic_slice_in_dim(
        w_kv_up.reshape(kv_width, lines, PLANE_X * head_width),
        lane_id * head_width,
        head_width,
        2,
    ).reshape(kv_width, lines * head_width)
    span = PLANE_X * chunk
    span_latents = cache_parts[:, :kv_width, :].transpose(0, 2, 1).reshape(span, kv_width)
    span_rope = cache_parts[:, kv_width:, :].transpose(0, 2, 1).reshape(span, ROPE)
    key_latents = jnp.concatenate([span_latents, fresh_latents[:, :kv_width]], 0)
    key_rope = jnp.concatenate([span_rope, fresh_latents[:, kv_width:]], 0)
    key_count = key_latents.shape[0]
    lifted = (
        jnp.dot(key_latents, line_weight, preferred_element_type=jnp.float32)
        .astype(jnp.bfloat16)
        .reshape(key_count, lines, head_width)
    )
    keys = jnp.concatenate(
        [
            lifted[:, :, :NOPE],
            jnp.broadcast_to(key_rope[:, None, :], (key_count, lines, ROPE)),
        ],
        2,
    )
    score_scale = 1.0 / math.sqrt(NOPE + ROPE)
    key_total = columns * chunk
    page_row = page_table[slot_index]
    page_count = page_row.shape[0]
    page_size = key_total // page_count
    offsets = jnp.arange(page_size, dtype=jnp.int32)
    page_ids = jnp.arange(page_count, dtype=jnp.int32)
    logical_page = jnp.sum(
        page_ids[:, None] * (page_row[:, None] == page_ids[None, :]).astype(jnp.int32), 0
    )
    cached_visible = (logical_page[:, None] * page_size + offsets[None, :]).reshape(
        key_total
    ) < cached_count
    span_visible = lax.dynamic_slice_in_dim(cached_visible, line_id * span, span, 0)
    share = group_rows // lines
    query_index = jnp.arange(group_rows, dtype=jnp.int32)[:, None]
    key_index = jnp.arange(group_rows, dtype=jnp.int32)[None, :]
    fresh_visible = (
        (key_index <= query_index) & (key_index < live_count) & (key_index // share == line_id)
    )
    visible = jnp.concatenate(
        [jnp.broadcast_to(span_visible[None, :], (group_rows, span)), fresh_visible], 1
    )
    scores = (
        jnp.einsum("hqd,khd->hqk", head_queries, keys, preferred_element_type=jnp.float32)
        * score_scale
    )
    scores = jnp.where(visible[None], scores, -jnp.inf)
    row_peak = jnp.max(scores, 2)
    safe_peak = jnp.where(row_peak == -jnp.inf, 0.0, row_peak)
    exponent = jnp.exp(scores - safe_peak[:, :, None])
    row_total = jnp.sum(exponent, 2)
    values = lifted[:, :, NOPE:]
    summed = jnp.einsum(
        "hqk,khd->hdq", exponent.astype(jnp.bfloat16), values, preferred_element_type=jnp.float32
    )
    stats = jnp.stack([row_peak, row_total], 1)
    summed_parts, stat_parts = exchange(
        [summed.astype(jnp.bfloat16), stats], [("y", False), ("y", False)], 4
    )
    peak = jnp.max(stat_parts[:, 0, :], 0)
    factor = jnp.exp(stat_parts[:, 0, :] - peak[None, :])
    total = jnp.sum(factor * stat_parts[:, 1, :], 0)
    merged = jnp.sum(factor[:, None, :] * summed_parts.astype(jnp.float32), 0)
    attended = (merged / total[None, :]).astype(jnp.bfloat16)
    live_rows = jnp.arange(group_rows, dtype=jnp.int32) < live_count
    attended = jnp.where(live_rows[None, :], attended, jnp.zeros_like(attended))
    out_parts = lax.dot_general(
        w_out, attended, (((0,), (0,)), ((), ())), preferred_element_type=jnp.float32
    ).astype(jnp.bfloat16)
    (out_pieces,) = exchange([out_parts.reshape(columns, -1, group_rows)], [("all", False)], 3)
    summed_out = jnp.sum(out_pieces.astype(jnp.float32), 0)
    result = summed_out.T.astype(jnp.bfloat16)
    return result


def solution(mesh):
    return jax.shard_map(
        body,
        mesh=mesh,
        in_specs=(
            P("row", "col"),
            P("col", None),
            P(),
            P(),
            P(None, "col"),
            P(),
            P("col", None),
            P("row", "col", None),
            P(),
            P(),
            P(),
            P(),
        ),
        out_specs=P("row", "col"),
        check_vma=False,
    )
```

```python
import functools
import math

import jax
import jax.numpy as jnp
from jax import lax
from jax.experimental import pallas as pl
from jax.experimental.pallas import tpu as pltpu
from jax.sharding import PartitionSpec as P

MESH = pl.DeviceIdType.MESH

NOPE = 64
ROPE = 32
VDIM = 64


epsilon = 1e-05


def rms_scale(values, gain):
    return values * lax.rsqrt(jnp.mean(values * values, axis=-1, keepdims=True) + epsilon) * gain


def angle_tables(positions, width):
    half_dim = width // 2
    frequency = 10000.0 ** (-2.0 * jnp.arange(half_dim, dtype=jnp.float32) / width)
    angles = positions.astype(jnp.float32)[:, None] * frequency[None, :]
    return (jnp.cos(angles), jnp.sin(angles))


def rotary(values, cosine, sine_table):
    half_dim = values.shape[-1] // 2
    first_half = values[..., :half_dim]
    second_half = values[..., half_dim:]
    return jnp.concatenate(
        [
            first_half * cosine - second_half * sine_table,
            second_half * cosine + first_half * sine_table,
        ],
        -1,
    )


PLANE_X = 4


def _group_size(group, n):
    return {"all": n, "x": PLANE_X, "y": n // PLANE_X}[group]


def _group_peer(group, n, me, k):
    if group == "x":
        return (me // PLANE_X) * PLANE_X + lax.rem(me % PLANE_X + k, PLANE_X)
    if group == "y":
        return lax.rem(me // PLANE_X + k, n // PLANE_X) * PLANE_X + me % PLANE_X
    return lax.rem(me + k, n)


def _group_slot(group, device):
    if group == "x":
        return device % PLANE_X
    if group == "y":
        return device // PLANE_X
    return device


def _exchange_kernel(n, plan, *refs):
    count = len(plan)
    sources, targets = refs[:count], refs[count : 2 * count]
    send_sem, recv_sem = refs[2 * count :]
    me = lax.axis_index("col")
    barrier = pltpu.get_barrier_semaphore()
    for k in range(1, n):
        pl.semaphore_signal(
            barrier, inc=1, device_id={"col": lax.rem(me + k, n)}, device_id_type=MESH
        )
    pl.semaphore_wait(barrier, n - 1)

    def remote(a, k, peer, landing):
        group, gather = plan[a]
        x_ref = sources[a]
        return pltpu.make_async_remote_copy(
            src_ref=x_ref if gather else x_ref.at[_group_slot(group, peer)],
            dst_ref=targets[a].at[landing],
            send_sem=send_sem.at[a, k],
            recv_sem=recv_sem.at[a, k],
            device_id={"col": peer},
            device_id_type=MESH,
        )

    sends = []
    for a, (group, gather) in enumerate(plan):
        for k in range(1, _group_size(group, n)):
            copy = remote(a, k, _group_peer(group, n, me, k), _group_slot(group, me))
            copy.start()
            sends.append(copy)
    for a, (group, gather) in enumerate(plan):
        mine = _group_slot(group, me)
        if gather:
            targets[a][mine] = sources[a][...]
        else:
            targets[a][mine] = sources[a][mine]
    for copy in sends:
        copy.wait_send()
    for a, (group, gather) in enumerate(plan):
        size = _group_size(group, n)
        for k in range(1, size):
            source = _group_peer(group, n, me, size - k)
            remote(a, k, source, _group_slot(group, source)).wait_recv()


def exchange(arrays, plan, collective_id):
    n = lax.axis_size("col")
    shapes = [
        jax.ShapeDtypeStruct(
            ((_group_size(group, n),) + x.shape) if gather else x.shape, x.dtype
        )
        for x, (group, gather) in zip(arrays, plan)
    ]
    return pl.pallas_call(
        functools.partial(_exchange_kernel, n, tuple(plan)),
        out_shape=shapes,
        in_specs=[pl.BlockSpec(memory_space=pltpu.VMEM)] * len(arrays),
        out_specs=[pl.BlockSpec(memory_space=pltpu.VMEM)] * len(arrays),
        scratch_shapes=[
            pltpu.SemaphoreType.DMA((len(arrays), n)),
            pltpu.SemaphoreType.DMA((len(arrays), n)),
        ],
        compiler_params=pltpu.CompilerParams(collective_id=collective_id, has_side_effects=True),
    )(*arrays)


def body(
    tokens,
    w_down,
    q_gain,
    kv_gain,
    w_q_up,
    w_kv_up,
    w_out,
    latent_cache,
    cache_len,
    new_len,
    page_table,
    home_slot,
):
    columns = lax.axis_size("col")
    column_id = lax.axis_index("col")
    row_id = lax.axis_index("row")
    lines = columns // PLANE_X
    line_id = column_id // PLANE_X
    lane_id = column_id % PLANE_X
    group_rows = tokens.shape[0]
    own_rows = group_rows // columns
    q_width = q_gain.shape[0]
    kv_width = kv_gain.shape[0]
    partial_sums = jnp.dot(tokens, w_down, preferred_element_type=jnp.float32)
    pieces, line_query_weight = exchange(
        [partial_sums.astype(jnp.bfloat16).reshape(columns, -1, 128), w_q_up.T],
        [("all", False), ("y", True)],
        0,
    )
    pieces, line_query_weight, home_slot, cache_len, new_len = lax.optimization_barrier(
        (pieces, line_query_weight, home_slot, cache_len, new_len)
    )
    request_ids = jnp.arange(home_slot.shape[0], dtype=jnp.int32)
    slot_index = jnp.sum(jnp.where(request_ids == row_id, home_slot, 0))
    cached_count = jnp.sum(jnp.where(request_ids == slot_index, cache_len, 0))
    live_count = jnp.sum(jnp.where(request_ids == row_id, new_len, 0))
    combined = jnp.sum(pieces.astype(jnp.float32), 0).reshape(own_rows, -1)
    own_position = cached_count + column_id * own_rows + jnp.arange(own_rows, dtype=jnp.int32)
    own_cos, own_sin = angle_tables(own_position, ROPE)
    own_query = rms_scale(combined[:, :q_width], q_gain).astype(jnp.bfloat16)
    own_latent = rms_scale(combined[:, q_width : q_width + kv_width], kv_gain).astype(jnp.bfloat16)
    own_rope = rotary(combined[:, q_width + kv_width :], own_cos, own_sin).astype(jnp.bfloat16)
    own_rows_all = jnp.concatenate([own_query, own_latent, own_rope], 1)
    segment = lax.all_gather(latent_cache, "row", axis=0, tiled=True)
    own_cache = lax.dynamic_index_in_dim(segment, slot_index, axis=0, keepdims=False)
    chunk = own_cache.shape[0]
    cache_parts, all_rows = exchange(
        [own_cache.T, own_rows_all], [("x", True), ("all", True)], 2
    )
    all_rows = all_rows.reshape(group_rows, -1)
    query_latent = all_rows[:, :q_width]
    fresh_latents = all_rows[:, q_width:]
    query_cos, query_sin = angle_tables(
        cached_count + jnp.arange(group_rows, dtype=jnp.int32), ROPE
    )
    projected = jnp.einsum(
        "qk,hdk->hqd", query_latent, line_query_weight, preferred_element_type=jnp.float32
    )
    head_queries = jnp.concatenate(
        [
            projected[:, :, :NOPE],
            rotary(projected[:, :, NOPE:], query_cos[None], query_sin[None]),
        ],
        2,
    ).astype(jnp.bfloat16)
    head_width = NOPE + VDIM
    heads = columns
    line_weight = lax.dynamic_slice_in_dim(
        w_kv_up.reshape(kv_width, lines, PLANE_X * head_width),
        lane_id * head_width,
        head_width,
        2,
    ).reshape(kv_width, lines * head_width)
    span = PLANE_X * chunk
    span_latents = cache_parts[:, :kv_width, :].transpose(0, 2, 1).reshape(span, kv_width)
    span_rope = cache_parts[:, kv_width:, :].transpose(0, 2, 1).reshape(span, ROPE)
    key_latents = jnp.concatenate([span_latents, fresh_latents[:, :kv_width]], 0)
    key_rope = jnp.concatenate([span_rope, fresh_latents[:, kv_width:]], 0)
    key_count = key_latents.shape[0]
    lifted = (
        jnp.dot(key_latents, line_weight, preferred_element_type=jnp.float32)
        .astype(jnp.bfloat16)
        .reshape(key_count, lines, head_width)
    )
    keys = jnp.concatenate(
        [
            lifted[:, :, :NOPE],
            jnp.broadcast_to(key_rope[:, None, :], (key_count, lines, ROPE)),
        ],
        2,
    )
    score_scale = 1.0 / math.sqrt(NOPE + ROPE)
    key_total = columns * chunk
    page_row = page_table[slot_index]
    page_count = page_row.shape[0]
    page_size = key_total // page_count
    offsets = jnp.arange(page_size, dtype=jnp.int32)
    page_ids = jnp.arange(page_count, dtype=jnp.int32)
    logical_page = jnp.sum(
        page_ids[:, None] * (page_row[:, None] == page_ids[None, :]).astype(jnp.int32), 0
    )
    cached_visible = (logical_page[:, None] * page_size + offsets[None, :]).reshape(
        key_total
    ) < cached_count
    span_visible = lax.dynamic_slice_in_dim(cached_visible, line_id * span, span, 0)
    share = group_rows // lines
    query_index = jnp.arange(group_rows, dtype=jnp.int32)[:, None]
    key_index = jnp.arange(group_rows, dtype=jnp.int32)[None, :]
    fresh_visible = (
        (key_index <= query_index) & (key_index < live_count) & (key_index // share == line_id)
    )
    visible = jnp.concatenate(
        [jnp.broadcast_to(span_visible[None, :], (group_rows, span)), fresh_visible], 1
    )
    scores = (
        jnp.einsum("hqd,khd->hqk", head_queries, keys, preferred_element_type=jnp.float32)
        * score_scale
    )
    scores = jnp.where(visible[None], scores, -jnp.inf)
    row_peak = jnp.max(scores, 2)
    safe_peak = jnp.where(row_peak == -jnp.inf, 0.0, row_peak)
    exponent = jnp.exp(scores - safe_peak[:, :, None])
    row_total = jnp.sum(exponent, 2)
    values = lifted[:, :, NOPE:]
    summed = jnp.einsum(
        "hqk,khd->hdq", exponent.astype(jnp.bfloat16), values, preferred_element_type=jnp.float32
    )
    stats = jnp.stack([row_peak, row_total], 1)
    summed_parts, stat_parts = exchange(
        [summed.astype(jnp.bfloat16), stats], [("y", False), ("y", False)], 4
    )
    peak = jnp.max(stat_parts[:, 0, :], 0)
    factor = jnp.exp(stat_parts[:, 0, :] - peak[None, :])
    total = jnp.sum(factor * stat_parts[:, 1, :], 0)
    merged = jnp.sum(factor[:, None, :] * summed_parts.astype(jnp.float32), 0)
    attended = (merged / total[None, :]).astype(jnp.bfloat16)
    live_rows = jnp.arange(group_rows, dtype=jnp.int32) < live_count
    attended = jnp.where(live_rows[None, :], attended, jnp.zeros_like(attended))
    out_parts = lax.dot_general(
        w_out, attended, (((0,), (0,)), ((), ())), preferred_element_type=jnp.float32
    ).astype(jnp.bfloat16)
    (out_pieces,) = exchange([out_parts.reshape(columns, -1, group_rows)], [("all", False)], 3)
    summed_out = jnp.sum(out_pieces.astype(jnp.float32), 0)
    result = summed_out.T.astype(jnp.bfloat16)
    return result


def solution(mesh):
    return jax.shard_map(
        body,
        mesh=mesh,
        in_specs=(
            P("row", "col"),
            P("col", None),
            P(),
            P(),
            P(None, "col"),
            P(),
            P("col", None),
            P("row", "col", None),
            P(),
            P(),
            P(),
            P(),
        ),
        out_specs=P("row", "col"),
        check_vma=False,
    )
```

```python
import functools
import math

import jax
import jax.numpy as jnp
from jax import lax
from jax.experimental import pallas as pl
from jax.experimental.pallas import tpu as pltpu
from jax.sharding import PartitionSpec as P

MESH = pl.DeviceIdType.MESH

NOPE = 64
ROPE = 32
VDIM = 64


epsilon = 1e-05


def rms_scale(values, gain):
    return values * lax.rsqrt(jnp.mean(values * values, axis=-1, keepdims=True) + epsilon) * gain


def angle_tables(positions, width):
    half_dim = width // 2
    frequency = 10000.0 ** (-2.0 * jnp.arange(half_dim, dtype=jnp.float32) / width)
    angles = positions.astype(jnp.float32)[:, None] * frequency[None, :]
    return (jnp.cos(angles), jnp.sin(angles))


def rotary(values, cosine, sine_table):
    half_dim = values.shape[-1] // 2
    first_half = values[..., :half_dim]
    second_half = values[..., half_dim:]
    return jnp.concatenate(
        [
            first_half * cosine - second_half * sine_table,
            second_half * cosine + first_half * sine_table,
        ],
        -1,
    )


PLANE_X = 4


def _group_size(group, n):
    return {"all": n, "x": PLANE_X, "y": n // PLANE_X}[group]


def _group_peer(group, n, me, k):
    if group == "x":
        return (me // PLANE_X) * PLANE_X + lax.rem(me % PLANE_X + k, PLANE_X)
    if group == "y":
        return lax.rem(me // PLANE_X + k, n // PLANE_X) * PLANE_X + me % PLANE_X
    return lax.rem(me + k, n)


def _group_slot(group, device):
    if group == "x":
        return device % PLANE_X
    if group == "y":
        return device // PLANE_X
    return device


def _exchange_kernel(n, plan, *refs):
    count = len(plan)
    sources, targets = refs[:count], refs[count : 2 * count]
    send_sem, recv_sem = refs[2 * count :]
    me = lax.axis_index("col")
    barrier = pltpu.get_barrier_semaphore()
    for k in range(1, n):
        pl.semaphore_signal(
            barrier, inc=1, device_id={"col": lax.rem(me + k, n)}, device_id_type=MESH
        )
    pl.semaphore_wait(barrier, n - 1)

    def remote(a, k, peer, landing):
        group, gather = plan[a]
        x_ref = sources[a]
        return pltpu.make_async_remote_copy(
            src_ref=x_ref if gather else x_ref.at[_group_slot(group, peer)],
            dst_ref=targets[a].at[landing],
            send_sem=send_sem.at[a, k],
            recv_sem=recv_sem.at[a, k],
            device_id={"col": peer},
            device_id_type=MESH,
        )

    sends = []
    for a, (group, gather) in enumerate(plan):
        for k in range(1, _group_size(group, n)):
            copy = remote(a, k, _group_peer(group, n, me, k), _group_slot(group, me))
            copy.start()
            sends.append(copy)
    for a, (group, gather) in enumerate(plan):
        mine = _group_slot(group, me)
        if gather:
            targets[a][mine] = sources[a][...]
        else:
            targets[a][mine] = sources[a][mine]
    for copy in sends:
        copy.wait_send()
    for a, (group, gather) in enumerate(plan):
        size = _group_size(group, n)
        for k in range(1, size):
            source = _group_peer(group, n, me, size - k)
            remote(a, k, source, _group_slot(group, source)).wait_recv()


def exchange(arrays, plan, collective_id):
    n = lax.axis_size("col")
    shapes = [
        jax.ShapeDtypeStruct(
            ((_group_size(group, n),) + x.shape) if gather else x.shape, x.dtype
        )
        for x, (group, gather) in zip(arrays, plan)
    ]
    return pl.pallas_call(
        functools.partial(_exchange_kernel, n, tuple(plan)),
        out_shape=shapes,
        in_specs=[pl.BlockSpec(memory_space=pltpu.VMEM)] * len(arrays),
        out_specs=[pl.BlockSpec(memory_space=pltpu.VMEM)] * len(arrays),
        scratch_shapes=[
            pltpu.SemaphoreType.DMA((len(arrays), n)),
            pltpu.SemaphoreType.DMA((len(arrays), n)),
        ],
        compiler_params=pltpu.CompilerParams(collective_id=collective_id, has_side_effects=True),
    )(*arrays)


def body(
    tokens,
    w_down,
    q_gain,
    kv_gain,
    w_q_up,
    w_kv_up,
    w_out,
    latent_cache,
    cache_len,
    new_len,
    page_table,
    home_slot,
):
    columns = lax.axis_size("col")
    column_id = lax.axis_index("col")
    row_id = lax.axis_index("row")
    lines = columns // PLANE_X
    line_id = column_id // PLANE_X
    lane_id = column_id % PLANE_X
    group_rows = tokens.shape[0]
    own_rows = group_rows // columns
    q_width = q_gain.shape[0]
    kv_width = kv_gain.shape[0]
    partial_sums = jnp.dot(tokens, w_down, preferred_element_type=jnp.float32)
    pieces, line_query_weight = exchange(
        [partial_sums.astype(jnp.bfloat16).reshape(columns, -1, 128), w_q_up.T],
        [("all", False), ("y", True)],
        0,
    )
    pieces, line_query_weight, home_slot, cache_len, new_len = lax.optimization_barrier(
        (pieces, line_query_weight, home_slot, cache_len, new_len)
    )
    request_ids = jnp.arange(home_slot.shape[0], dtype=jnp.int32)
    slot_index = jnp.sum(jnp.where(request_ids == row_id, home_slot, 0))
    cached_count = jnp.sum(jnp.where(request_ids == slot_index, cache_len, 0))
    live_count = jnp.sum(jnp.where(request_ids == row_id, new_len, 0))
    combined = jnp.sum(pieces.astype(jnp.float32), 0).reshape(own_rows, -1)
    own_position = cached_count + column_id * own_rows + jnp.arange(own_rows, dtype=jnp.int32)
    own_cos, own_sin = angle_tables(own_position, ROPE)
    own_query = rms_scale(combined[:, :q_width], q_gain).astype(jnp.bfloat16)
    own_latent = rms_scale(combined[:, q_width : q_width + kv_width], kv_gain).astype(jnp.bfloat16)
    own_rope = rotary(combined[:, q_width + kv_width :], own_cos, own_sin).astype(jnp.bfloat16)
    own_rows_all = jnp.concatenate([own_query, own_latent, own_rope], 1)
    segment = lax.all_gather(latent_cache, "row", axis=0, tiled=True)
    own_cache = lax.dynamic_index_in_dim(segment, slot_index, axis=0, keepdims=False)
    chunk = own_cache.shape[0]
    cache_parts, all_rows = exchange(
        [own_cache.T, own_rows_all.reshape(-1, 128)], [("x", True), ("all", True)], 2
    )
    all_rows = all_rows.reshape(group_rows, -1)
    query_latent = all_rows[:, :q_width]
    fresh_latents = all_rows[:, q_width:]
    query_cos, query_sin = angle_tables(
        cached_count + jnp.arange(group_rows, dtype=jnp.int32), ROPE
    )
    projected = jnp.einsum(
        "qk,hdk->hqd", query_latent, line_query_weight, preferred_element_type=jnp.float32
    )
    head_queries = jnp.concatenate(
        [
            projected[:, :, :NOPE],
            rotary(projected[:, :, NOPE:], query_cos[None], query_sin[None]),
        ],
        2,
    ).astype(jnp.bfloat16)
    head_width = NOPE + VDIM
    heads = columns
    line_weight = lax.dynamic_slice_in_dim(
        w_kv_up.reshape(kv_width, lines, PLANE_X * head_width),
        lane_id * head_width,
        head_width,
        2,
    ).reshape(kv_width, lines * head_width)
    span = PLANE_X * chunk
    span_latents = cache_parts[:, :kv_width, :].transpose(0, 2, 1).reshape(span, kv_width)
    span_rope = cache_parts[:, kv_width:, :].transpose(0, 2, 1).reshape(span, ROPE)
    key_latents = jnp.concatenate([span_latents, fresh_latents[:, :kv_width]], 0)
    key_rope = jnp.concatenate([span_rope, fresh_latents[:, kv_width:]], 0)
    key_count = key_latents.shape[0]
    lifted = (
        jnp.dot(key_latents, line_weight, preferred_element_type=jnp.float32)
        .astype(jnp.bfloat16)
        .reshape(key_count, lines, head_width)
    )
    keys = jnp.concatenate(
        [
            lifted[:, :, :NOPE],
            jnp.broadcast_to(key_rope[:, None, :], (key_count, lines, ROPE)),
        ],
        2,
    )
    score_scale = 1.0 / math.sqrt(NOPE + ROPE)
    key_total = columns * chunk
    page_row = page_table[slot_index]
    page_count = page_row.shape[0]
    page_size = key_total // page_count
    offsets = jnp.arange(page_size, dtype=jnp.int32)
    page_ids = jnp.arange(page_count, dtype=jnp.int32)
    logical_page = jnp.sum(
        page_ids[:, None] * (page_row[:, None] == page_ids[None, :]).astype(jnp.int32), 0
    )
    cached_visible = (logical_page[:, None] * page_size + offsets[None, :]).reshape(
        key_total
    ) < cached_count
    span_visible = lax.dynamic_slice_in_dim(cached_visible, line_id * span, span, 0)
    share = group_rows // lines
    query_index = jnp.arange(group_rows, dtype=jnp.int32)[:, None]
    key_index = jnp.arange(group_rows, dtype=jnp.int32)[None, :]
    fresh_visible = (
        (key_index <= query_index) & (key_index < live_count) & (key_index // share == line_id)
    )
    visible = jnp.concatenate(
        [jnp.broadcast_to(span_visible[None, :], (group_rows, span)), fresh_visible], 1
    )
    scores = (
        jnp.einsum("hqd,khd->hqk", head_queries, keys, preferred_element_type=jnp.float32)
        * score_scale
    )
    scores = jnp.where(visible[None], scores, -jnp.inf)
    row_peak = jnp.max(scores, 2)
    safe_peak = jnp.where(row_peak == -jnp.inf, 0.0, row_peak)
    exponent = jnp.exp(scores - safe_peak[:, :, None])
    row_total = jnp.sum(exponent, 2)
    values = lifted[:, :, NOPE:]
    summed = jnp.einsum(
        "hqk,khd->hdq", exponent.astype(jnp.bfloat16), values, preferred_element_type=jnp.float32
    )
    stats = jnp.stack([row_peak, row_total], 1)
    summed_parts, stat_parts = exchange(
        [summed.astype(jnp.bfloat16), stats], [("y", False), ("y", False)], 4
    )
    peak = jnp.max(stat_parts[:, 0, :], 0)
    factor = jnp.exp(stat_parts[:, 0, :] - peak[None, :])
    total = jnp.sum(factor * stat_parts[:, 1, :], 0)
    merged = jnp.sum(factor[:, None, :] * summed_parts.astype(jnp.float32), 0)
    attended = (merged / total[None, :]).astype(jnp.bfloat16)
    live_rows = jnp.arange(group_rows, dtype=jnp.int32) < live_count
    attended = jnp.where(live_rows[None, :], attended, jnp.zeros_like(attended))
    out_parts = lax.dot_general(
        w_out, attended, (((0,), (0,)), ((), ())), preferred_element_type=jnp.float32
    ).astype(jnp.bfloat16)
    (out_pieces,) = exchange([out_parts.reshape(columns, -1, group_rows)], [("all", False)], 3)
    summed_out = jnp.sum(out_pieces.astype(jnp.float32), 0)
    result = summed_out.T.astype(jnp.bfloat16)
    return result


def solution(mesh):
    return jax.shard_map(
        body,
        mesh=mesh,
        in_specs=(
            P("row", "col"),
            P("col", None),
            P(),
            P(),
            P(None, "col"),
            P(),
            P("col", None),
            P("row", "col", None),
            P(),
            P(),
            P(),
            P(),
        ),
        out_specs=P("row", "col"),
        check_vma=False,
    )
```

```python
import functools
import math

import jax
import jax.numpy as jnp
from jax import lax
from jax.experimental import pallas as pl
from jax.experimental.pallas import tpu as pltpu
from jax.sharding import PartitionSpec as P

MESH = pl.DeviceIdType.MESH

NOPE = 64
ROPE = 32
VDIM = 64


epsilon = 1e-05


def rms_scale(values, gain):
    return values * lax.rsqrt(jnp.mean(values * values, axis=-1, keepdims=True) + epsilon) * gain


def angle_tables(positions, width):
    half_dim = width // 2
    frequency = 10000.0 ** (-2.0 * jnp.arange(half_dim, dtype=jnp.float32) / width)
    angles = positions.astype(jnp.float32)[:, None] * frequency[None, :]
    return (jnp.cos(angles), jnp.sin(angles))


def rotary(values, cosine, sine_table):
    half_dim = values.shape[-1] // 2
    first_half = values[..., :half_dim]
    second_half = values[..., half_dim:]
    return jnp.concatenate(
        [
            first_half * cosine - second_half * sine_table,
            second_half * cosine + first_half * sine_table,
        ],
        -1,
    )


PLANE_X = 4


def _group_size(group, n):
    return {"all": n, "x": PLANE_X, "y": n // PLANE_X}[group]


def _group_peer(group, n, me, k):
    if group == "x":
        return (me // PLANE_X) * PLANE_X + lax.rem(me % PLANE_X + k, PLANE_X)
    if group == "y":
        return lax.rem(me // PLANE_X + k, n // PLANE_X) * PLANE_X + me % PLANE_X
    return lax.rem(me + k, n)


def _group_slot(group, device):
    if group == "x":
        return device % PLANE_X
    if group == "y":
        return device // PLANE_X
    return device


def _exchange_kernel(n, plan, *refs):
    count = len(plan)
    sources, targets = refs[:count], refs[count : 2 * count]
    send_sem, recv_sem = refs[2 * count :]
    me = lax.axis_index("col")
    barrier = pltpu.get_barrier_semaphore()
    groups = sorted({group for group, _ in plan})
    if "all" in groups:
        groups = ["all"]
    greeted = 0
    for group in groups:
        for k in range(1, _group_size(group, n)):
            pl.semaphore_signal(
                barrier, inc=1, device_id={"col": _group_peer(group, n, me, k)},
                device_id_type=MESH,
            )
            greeted += 1
    pl.semaphore_wait(barrier, greeted)

    def remote(a, k, peer, landing):
        group, gather = plan[a]
        x_ref = sources[a]
        return pltpu.make_async_remote_copy(
            src_ref=x_ref if gather else x_ref.at[_group_slot(group, peer)],
            dst_ref=targets[a].at[landing],
            send_sem=send_sem.at[a, k],
            recv_sem=recv_sem.at[a, k],
            device_id={"col": peer},
            device_id_type=MESH,
        )

    sends = []
    for a, (group, gather) in enumerate(plan):
        for k in range(1, _group_size(group, n)):
            copy = remote(a, k, _group_peer(group, n, me, k), _group_slot(group, me))
            copy.start()
            sends.append(copy)
    for a, (group, gather) in enumerate(plan):
        mine = _group_slot(group, me)
        if gather:
            targets[a][mine] = sources[a][...]
        else:
            targets[a][mine] = sources[a][mine]
    for copy in sends:
        copy.wait_send()
    for a, (group, gather) in enumerate(plan):
        size = _group_size(group, n)
        for k in range(1, size):
            source = _group_peer(group, n, me, size - k)
            remote(a, k, source, _group_slot(group, source)).wait_recv()


def exchange(arrays, plan, collective_id):
    n = lax.axis_size("col")
    shapes = [
        jax.ShapeDtypeStruct(
            ((_group_size(group, n),) + x.shape) if gather else x.shape, x.dtype
        )
        for x, (group, gather) in zip(arrays, plan)
    ]
    return pl.pallas_call(
        functools.partial(_exchange_kernel, n, tuple(plan)),
        out_shape=shapes,
        in_specs=[pl.BlockSpec(memory_space=pltpu.VMEM)] * len(arrays),
        out_specs=[pl.BlockSpec(memory_space=pltpu.VMEM)] * len(arrays),
        scratch_shapes=[
            pltpu.SemaphoreType.DMA((len(arrays), n)),
            pltpu.SemaphoreType.DMA((len(arrays), n)),
        ],
        compiler_params=pltpu.CompilerParams(collective_id=collective_id, has_side_effects=True),
    )(*arrays)


def body(
    tokens,
    w_down,
    q_gain,
    kv_gain,
    w_q_up,
    w_kv_up,
    w_out,
    latent_cache,
    cache_len,
    new_len,
    page_table,
    home_slot,
):
    columns = lax.axis_size("col")
    column_id = lax.axis_index("col")
    row_id = lax.axis_index("row")
    lines = columns // PLANE_X
    line_id = column_id // PLANE_X
    lane_id = column_id % PLANE_X
    group_rows = tokens.shape[0]
    own_rows = group_rows // columns
    q_width = q_gain.shape[0]
    kv_width = kv_gain.shape[0]
    partial_sums = jnp.dot(tokens, w_down, preferred_element_type=jnp.float32)
    pieces, line_query_weight = exchange(
        [partial_sums.astype(jnp.bfloat16).reshape(columns, -1, 128), w_q_up.T],
        [("all", False), ("y", True)],
        0,
    )
    pieces, line_query_weight, home_slot, cache_len, new_len = lax.optimization_barrier(
        (pieces, line_query_weight, home_slot, cache_len, new_len)
    )
    request_ids = jnp.arange(home_slot.shape[0], dtype=jnp.int32)
    slot_index = jnp.sum(jnp.where(request_ids == row_id, home_slot, 0))
    cached_count = jnp.sum(jnp.where(request_ids == slot_index, cache_len, 0))
    live_count = jnp.sum(jnp.where(request_ids == row_id, new_len, 0))
    combined = jnp.sum(pieces.astype(jnp.float32), 0).reshape(own_rows, -1)
    own_position = cached_count + column_id * own_rows + jnp.arange(own_rows, dtype=jnp.int32)
    own_cos, own_sin = angle_tables(own_position, ROPE)
    own_query = rms_scale(combined[:, :q_width], q_gain).astype(jnp.bfloat16)
    own_latent = rms_scale(combined[:, q_width : q_width + kv_width], kv_gain).astype(jnp.bfloat16)
    own_rope = rotary(combined[:, q_width + kv_width :], own_cos, own_sin).astype(jnp.bfloat16)
    own_rows_all = jnp.concatenate([own_query, own_latent, own_rope], 1)
    segment = lax.all_gather(latent_cache, "row", axis=0, tiled=True)
    own_cache = lax.dynamic_index_in_dim(segment, slot_index, axis=0, keepdims=False)
    chunk = own_cache.shape[0]
    cache_parts, all_rows = exchange(
        [own_cache.T, own_rows_all.reshape(-1, 128)], [("x", True), ("all", True)], 2
    )
    all_rows = all_rows.reshape(group_rows, -1)
    query_latent = all_rows[:, :q_width]
    fresh_latents = all_rows[:, q_width:]
    query_cos, query_sin = angle_tables(
        cached_count + jnp.arange(group_rows, dtype=jnp.int32), ROPE
    )
    projected = jnp.einsum(
        "qk,hdk->hqd", query_latent, line_query_weight, preferred_element_type=jnp.float32
    )
    head_queries = jnp.concatenate(
        [
            projected[:, :, :NOPE],
            rotary(projected[:, :, NOPE:], query_cos[None], query_sin[None]),
        ],
        2,
    ).astype(jnp.bfloat16)
    head_width = NOPE + VDIM
    heads = columns
    line_weight = lax.dynamic_slice_in_dim(
        w_kv_up.reshape(kv_width, lines, PLANE_X * head_width),
        lane_id * head_width,
        head_width,
        2,
    ).reshape(kv_width, lines * head_width)
    span = PLANE_X * chunk
    span_latents = cache_parts[:, :kv_width, :].transpose(0, 2, 1).reshape(span, kv_width)
    span_rope = cache_parts[:, kv_width:, :].transpose(0, 2, 1).reshape(span, ROPE)
    key_latents = jnp.concatenate([span_latents, fresh_latents[:, :kv_width]], 0)
    key_rope = jnp.concatenate([span_rope, fresh_latents[:, kv_width:]], 0)
    key_count = key_latents.shape[0]
    lifted = (
        jnp.dot(key_latents, line_weight, preferred_element_type=jnp.float32)
        .astype(jnp.bfloat16)
        .reshape(key_count, lines, head_width)
    )
    keys = jnp.concatenate(
        [
            lifted[:, :, :NOPE],
            jnp.broadcast_to(key_rope[:, None, :], (key_count, lines, ROPE)),
        ],
        2,
    )
    score_scale = 1.0 / math.sqrt(NOPE + ROPE)
    key_total = columns * chunk
    page_row = page_table[slot_index]
    page_count = page_row.shape[0]
    page_size = key_total // page_count
    offsets = jnp.arange(page_size, dtype=jnp.int32)
    page_ids = jnp.arange(page_count, dtype=jnp.int32)
    logical_page = jnp.sum(
        page_ids[:, None] * (page_row[:, None] == page_ids[None, :]).astype(jnp.int32), 0
    )
    cached_visible = (logical_page[:, None] * page_size + offsets[None, :]).reshape(
        key_total
    ) < cached_count
    span_visible = lax.dynamic_slice_in_dim(cached_visible, line_id * span, span, 0)
    share = group_rows // lines
    query_index = jnp.arange(group_rows, dtype=jnp.int32)[:, None]
    key_index = jnp.arange(group_rows, dtype=jnp.int32)[None, :]
    fresh_visible = (
        (key_index <= query_index) & (key_index < live_count) & (key_index // share == line_id)
    )
    visible = jnp.concatenate(
        [jnp.broadcast_to(span_visible[None, :], (group_rows, span)), fresh_visible], 1
    )
    scores = (
        jnp.einsum("hqd,khd->hqk", head_queries, keys, preferred_element_type=jnp.float32)
        * score_scale
    )
    scores = jnp.where(visible[None], scores, -jnp.inf)
    row_peak = jnp.max(scores, 2)
    safe_peak = jnp.where(row_peak == -jnp.inf, 0.0, row_peak)
    exponent = jnp.exp(scores - safe_peak[:, :, None])
    row_total = jnp.sum(exponent, 2)
    values = lifted[:, :, NOPE:]
    summed = jnp.einsum(
        "hqk,khd->hdq", exponent.astype(jnp.bfloat16), values, preferred_element_type=jnp.float32
    )
    stats = jnp.stack([row_peak, row_total], 1)
    summed_parts, stat_parts = exchange(
        [summed.astype(jnp.bfloat16), stats], [("y", False), ("y", False)], 4
    )
    peak = jnp.max(stat_parts[:, 0, :], 0)
    factor = jnp.exp(stat_parts[:, 0, :] - peak[None, :])
    total = jnp.sum(factor * stat_parts[:, 1, :], 0)
    merged = jnp.sum(factor[:, None, :] * summed_parts.astype(jnp.float32), 0)
    attended = (merged / total[None, :]).astype(jnp.bfloat16)
    live_rows = jnp.arange(group_rows, dtype=jnp.int32) < live_count
    attended = jnp.where(live_rows[None, :], attended, jnp.zeros_like(attended))
    out_parts = lax.dot_general(
        w_out, attended, (((0,), (0,)), ((), ())), preferred_element_type=jnp.float32
    ).astype(jnp.bfloat16)
    (out_pieces,) = exchange([out_parts.reshape(columns, -1, group_rows)], [("all", False)], 3)
    summed_out = jnp.sum(out_pieces.astype(jnp.float32), 0)
    result = summed_out.T.astype(jnp.bfloat16)
    return result


def solution(mesh):
    return jax.shard_map(
        body,
        mesh=mesh,
        in_specs=(
            P("row", "col"),
            P("col", None),
            P(),
            P(),
            P(None, "col"),
            P(),
            P("col", None),
            P("row", "col", None),
            P(),
            P(),
            P(),
            P(),
        ),
        out_specs=P("row", "col"),
        check_vma=False,
    )
```

```python
import functools
import math

import jax
import jax.numpy as jnp
from jax import lax
from jax.experimental import pallas as pl
from jax.experimental.pallas import tpu as pltpu
from jax.sharding import PartitionSpec as P

MESH = pl.DeviceIdType.MESH

NOPE = 64
ROPE = 32
VDIM = 64


epsilon = 1e-05


def rms_scale(values, gain):
    return values * lax.rsqrt(jnp.mean(values * values, axis=-1, keepdims=True) + epsilon) * gain


def angle_tables(positions, width):
    half_dim = width // 2
    frequency = 10000.0 ** (-2.0 * jnp.arange(half_dim, dtype=jnp.float32) / width)
    angles = positions.astype(jnp.float32)[:, None] * frequency[None, :]
    return (jnp.cos(angles), jnp.sin(angles))


def rotary(values, cosine, sine_table):
    half_dim = values.shape[-1] // 2
    first_half = values[..., :half_dim]
    second_half = values[..., half_dim:]
    return jnp.concatenate(
        [
            first_half * cosine - second_half * sine_table,
            second_half * cosine + first_half * sine_table,
        ],
        -1,
    )


PLANE_X = 4


def _group_size(group, n):
    return {"all": n, "x": PLANE_X, "y": n // PLANE_X}[group]


def _group_peer(group, n, me, k):
    if group == "x":
        return (me // PLANE_X) * PLANE_X + lax.rem(me % PLANE_X + k, PLANE_X)
    if group == "y":
        return lax.rem(me // PLANE_X + k, n // PLANE_X) * PLANE_X + me % PLANE_X
    return lax.rem(me + k, n)


def _group_slot(group, device):
    if group == "x":
        return device % PLANE_X
    if group == "y":
        return device // PLANE_X
    return device


def _exchange_kernel(n, plan, *refs):
    count = len(plan)
    sources, targets = refs[:count], refs[count : 2 * count]
    send_sem, recv_sem = refs[2 * count :]
    me = lax.axis_index("col")
    barrier = pltpu.get_barrier_semaphore()
    groups = sorted({group for group, _ in plan})
    if "all" in groups:
        groups = ["all"]
    greeted = 0
    for group in groups:
        for k in range(1, _group_size(group, n)):
            pl.semaphore_signal(
                barrier, inc=1, device_id={"col": _group_peer(group, n, me, k)},
                device_id_type=MESH,
            )
            greeted += 1
    pl.semaphore_wait(barrier, greeted)

    def remote(a, k, peer, landing):
        group, gather = plan[a]
        x_ref = sources[a]
        return pltpu.make_async_remote_copy(
            src_ref=x_ref if gather else x_ref.at[_group_slot(group, peer)],
            dst_ref=targets[a].at[landing],
            send_sem=send_sem.at[a, k],
            recv_sem=recv_sem.at[a, k],
            device_id={"col": peer},
            device_id_type=MESH,
        )

    sends = []
    for a, (group, gather) in enumerate(plan):
        for k in range(1, _group_size(group, n)):
            copy = remote(a, k, _group_peer(group, n, me, k), _group_slot(group, me))
            copy.start()
            sends.append(copy)
    for a, (group, gather) in enumerate(plan):
        mine = _group_slot(group, me)
        if gather:
            targets[a][mine] = sources[a][...]
        else:
            targets[a][mine] = sources[a][mine]
    for copy in sends:
        copy.wait_send()
    for a, (group, gather) in enumerate(plan):
        size = _group_size(group, n)
        for k in range(1, size):
            source = _group_peer(group, n, me, size - k)
            remote(a, k, source, _group_slot(group, source)).wait_recv()


def exchange(arrays, plan, collective_id):
    n = lax.axis_size("col")
    shapes = [
        jax.ShapeDtypeStruct(
            ((_group_size(group, n),) + x.shape) if gather else x.shape, x.dtype
        )
        for x, (group, gather) in zip(arrays, plan)
    ]
    return pl.pallas_call(
        functools.partial(_exchange_kernel, n, tuple(plan)),
        out_shape=shapes,
        in_specs=[pl.BlockSpec(memory_space=pltpu.VMEM)] * len(arrays),
        out_specs=[pl.BlockSpec(memory_space=pltpu.VMEM)] * len(arrays),
        scratch_shapes=[
            pltpu.SemaphoreType.DMA((len(arrays), n)),
            pltpu.SemaphoreType.DMA((len(arrays), n)),
        ],
        compiler_params=pltpu.CompilerParams(collective_id=collective_id, has_side_effects=True),
    )(*arrays)


def body(
    tokens,
    w_down,
    q_gain,
    kv_gain,
    w_q_up,
    w_kv_up,
    w_out,
    latent_cache,
    cache_len,
    new_len,
    page_table,
    home_slot,
):
    columns = lax.axis_size("col")
    column_id = lax.axis_index("col")
    row_id = lax.axis_index("row")
    lines = columns // PLANE_X
    line_id = column_id // PLANE_X
    lane_id = column_id % PLANE_X
    group_rows = tokens.shape[0]
    own_rows = group_rows // columns
    q_width = q_gain.shape[0]
    kv_width = kv_gain.shape[0]
    partial_sums = jnp.dot(tokens, w_down, preferred_element_type=jnp.float32)
    pieces, line_query_weight = exchange(
        [partial_sums.astype(jnp.bfloat16).reshape(columns, -1, 128), w_q_up.T],
        [("all", False), ("y", True)],
        0,
    )
    pieces, line_query_weight, home_slot, cache_len, new_len = lax.optimization_barrier(
        (pieces, line_query_weight, home_slot, cache_len, new_len)
    )
    request_ids = jnp.arange(home_slot.shape[0], dtype=jnp.int32)
    slot_index = jnp.sum(jnp.where(request_ids == row_id, home_slot, 0))
    cached_count = jnp.sum(jnp.where(request_ids == slot_index, cache_len, 0))
    live_count = jnp.sum(jnp.where(request_ids == row_id, new_len, 0))
    combined = jnp.sum(pieces.astype(jnp.float32), 0).reshape(own_rows, -1)
    own_position = cached_count + column_id * own_rows + jnp.arange(own_rows, dtype=jnp.int32)
    own_cos, own_sin = angle_tables(own_position, ROPE)
    own_query = rms_scale(combined[:, :q_width], q_gain).astype(jnp.bfloat16)
    own_latent = rms_scale(combined[:, q_width : q_width + kv_width], kv_gain).astype(jnp.bfloat16)
    own_rope = rotary(combined[:, q_width + kv_width :], own_cos, own_sin).astype(jnp.bfloat16)
    own_rows_all = jnp.concatenate([own_query, own_latent, own_rope], 1)
    segment = lax.all_gather(latent_cache, "row", axis=0, tiled=True)
    own_cache = lax.dynamic_index_in_dim(segment, slot_index, axis=0, keepdims=False)
    chunk = own_cache.shape[0]
    cache_parts, all_rows = exchange(
        [own_cache.T, own_rows_all.reshape(-1, 128)], [("x", True), ("all", True)], 2
    )
    all_rows = all_rows.reshape(group_rows, -1)
    query_latent = all_rows[:, :q_width]
    fresh_latents = all_rows[:, q_width:]
    query_cos, query_sin = angle_tables(
        cached_count + jnp.arange(group_rows, dtype=jnp.int32), ROPE
    )
    projected = jnp.einsum(
        "qk,hdk->hqd", query_latent, line_query_weight, preferred_element_type=jnp.float32
    )
    head_queries = jnp.concatenate(
        [
            projected[:, :, :NOPE],
            rotary(projected[:, :, NOPE:], query_cos[None], query_sin[None]),
        ],
        2,
    ).astype(jnp.bfloat16)
    head_width = NOPE + VDIM
    heads = columns
    line_weight = lax.dynamic_slice_in_dim(
        w_kv_up.reshape(kv_width, lines, PLANE_X * head_width),
        lane_id * head_width,
        head_width,
        2,
    ).reshape(kv_width, lines * head_width)
    span = PLANE_X * chunk
    span_latents = cache_parts[:, :kv_width, :].transpose(0, 2, 1).reshape(span, kv_width)
    span_rope = cache_parts[:, kv_width:, :].transpose(0, 2, 1).reshape(span, ROPE)
    key_latents = jnp.concatenate([span_latents, fresh_latents[:, :kv_width]], 0)
    key_rope = jnp.concatenate([span_rope, fresh_latents[:, kv_width:]], 0)
    key_count = key_latents.shape[0]
    lifted = (
        jnp.dot(key_latents, line_weight, preferred_element_type=jnp.float32)
        .astype(jnp.bfloat16)
        .reshape(key_count, lines, head_width)
    )
    keys = jnp.concatenate(
        [
            lifted[:, :, :NOPE],
            jnp.broadcast_to(key_rope[:, None, :], (key_count, lines, ROPE)),
        ],
        2,
    )
    score_scale = 1.0 / math.sqrt(NOPE + ROPE)
    key_total = columns * chunk
    page_row = page_table[slot_index]
    page_count = page_row.shape[0]
    page_size = key_total // page_count
    offsets = jnp.arange(page_size, dtype=jnp.int32)
    page_ids = jnp.arange(page_count, dtype=jnp.int32)
    logical_page = jnp.sum(
        page_ids[:, None] * (page_row[:, None] == page_ids[None, :]).astype(jnp.int32), 0
    )
    cached_visible = (logical_page[:, None] * page_size + offsets[None, :]).reshape(
        key_total
    ) < cached_count
    span_visible = lax.dynamic_slice_in_dim(cached_visible, line_id * span, span, 0)
    share = group_rows // lines
    query_index = jnp.arange(group_rows, dtype=jnp.int32)[:, None]
    key_index = jnp.arange(group_rows, dtype=jnp.int32)[None, :]
    fresh_visible = (
        (key_index <= query_index) & (key_index < live_count) & (key_index // share == line_id)
    )
    visible = jnp.concatenate(
        [jnp.broadcast_to(span_visible[None, :], (group_rows, span)), fresh_visible], 1
    )
    scores = (
        jnp.einsum("hqd,khd->hqk", head_queries, keys, preferred_element_type=jnp.float32)
        * score_scale
    )
    scores = jnp.where(visible[None], scores, -jnp.inf)
    row_peak = jnp.max(scores, 2)
    safe_peak = jnp.where(row_peak == -jnp.inf, 0.0, row_peak)
    exponent = jnp.exp(scores - safe_peak[:, :, None])
    row_total = jnp.sum(exponent, 2)
    values = lifted[:, :, NOPE:]
    summed = jnp.einsum(
        "hqk,khd->hdq", exponent.astype(jnp.bfloat16), values, preferred_element_type=jnp.float32
    )
    stats = jnp.stack([row_peak, row_total], 1)
    summed_parts, stat_parts = exchange(
        [summed.astype(jnp.bfloat16), stats], [("y", False), ("y", False)], 4
    )
    peak = jnp.max(stat_parts[:, 0, :], 0)
    factor = jnp.exp(stat_parts[:, 0, :] - peak[None, :])
    total = jnp.sum(factor * stat_parts[:, 1, :], 0)
    merged = jnp.sum(factor[:, None, :] * summed_parts.astype(jnp.float32), 0)
    attended = (merged / total[None, :]).astype(jnp.bfloat16)
    live_rows = jnp.arange(group_rows, dtype=jnp.int32) < live_count
    attended = jnp.where(live_rows[None, :], attended, jnp.zeros_like(attended))
    out_parts = lax.dot_general(
        w_out, attended, (((0,), (0,)), ((), ())), preferred_element_type=jnp.float32
    ).astype(jnp.bfloat16)
    feature_block = out_parts.shape[0] // columns
    (lane_pieces,) = exchange(
        [out_parts.reshape(lines, PLANE_X, feature_block, group_rows).transpose(1, 0, 2, 3)],
        [("x", False)],
        3,
    )
    lane_sums = jnp.sum(lane_pieces.astype(jnp.float32), 0).astype(jnp.bfloat16)
    (line_pieces,) = exchange([lane_sums], [("y", False)], 5)
    summed_out = jnp.sum(line_pieces.astype(jnp.float32), 0)
    result = summed_out.T.astype(jnp.bfloat16)
    return result


def solution(mesh):
    return jax.shard_map(
        body,
        mesh=mesh,
        in_specs=(
            P("row", "col"),
            P("col", None),
            P(),
            P(),
            P(None, "col"),
            P(),
            P("col", None),
            P("row", "col", None),
            P(),
            P(),
            P(),
            P(),
        ),
        out_specs=P("row", "col"),
        check_vma=False,
    )
```

```python
import functools
import math

import jax
import jax.numpy as jnp
from jax import lax
from jax.experimental import pallas as pl
from jax.experimental.pallas import tpu as pltpu
from jax.sharding import PartitionSpec as P

MESH = pl.DeviceIdType.MESH

NOPE = 64
ROPE = 32
VDIM = 64


epsilon = 1e-05


def rms_scale(values, gain):
    return values * lax.rsqrt(jnp.mean(values * values, axis=-1, keepdims=True) + epsilon) * gain


def angle_tables(positions, width):
    half_dim = width // 2
    frequency = 10000.0 ** (-2.0 * jnp.arange(half_dim, dtype=jnp.float32) / width)
    angles = positions.astype(jnp.float32)[:, None] * frequency[None, :]
    return (jnp.cos(angles), jnp.sin(angles))


def rotary(values, cosine, sine_table):
    half_dim = values.shape[-1] // 2
    first_half = values[..., :half_dim]
    second_half = values[..., half_dim:]
    return jnp.concatenate(
        [
            first_half * cosine - second_half * sine_table,
            second_half * cosine + first_half * sine_table,
        ],
        -1,
    )


PLANE_X = 4


def _group_size(group, n):
    return {"all": n, "x": PLANE_X, "y": n // PLANE_X}[group]


def _group_peer(group, n, me, k):
    if group == "x":
        return (me // PLANE_X) * PLANE_X + lax.rem(me % PLANE_X + k, PLANE_X)
    if group == "y":
        return lax.rem(me // PLANE_X + k, n // PLANE_X) * PLANE_X + me % PLANE_X
    return lax.rem(me + k, n)


def _group_slot(group, device):
    if group == "x":
        return device % PLANE_X
    if group == "y":
        return device // PLANE_X
    return device


def _exchange_kernel(n, plan, *refs):
    count = len(plan)
    sources, results = refs[:count], refs[count : 2 * count]
    send_sem, recv_sem = refs[2 * count : 2 * count + 2]
    landings = iter(refs[2 * count + 2 :])
    targets = [next(landings) if summed else results[a] for a, (_, _, summed) in enumerate(plan)]
    me = lax.axis_index("col")
    barrier = pltpu.get_barrier_semaphore()
    groups = sorted({group for group, _, _ in plan})
    if "all" in groups:
        groups = ["all"]
    greeted = 0
    for group in groups:
        for k in range(1, _group_size(group, n)):
            pl.semaphore_signal(
                barrier, inc=1, device_id={"col": _group_peer(group, n, me, k)},
                device_id_type=MESH,
            )
            greeted += 1
    pl.semaphore_wait(barrier, greeted)

    def remote(a, k, peer, landing):
        group, gather, _ = plan[a]
        x_ref = sources[a]
        return pltpu.make_async_remote_copy(
            src_ref=x_ref if gather else x_ref.at[_group_slot(group, peer)],
            dst_ref=targets[a].at[landing],
            send_sem=send_sem.at[a, k],
            recv_sem=recv_sem.at[a, k],
            device_id={"col": peer},
            device_id_type=MESH,
        )

    sends = []
    for a, (group, gather, _) in enumerate(plan):
        for k in range(1, _group_size(group, n)):
            copy = remote(a, k, _group_peer(group, n, me, k), _group_slot(group, me))
            copy.start()
            sends.append(copy)
    for a, (group, gather, _) in enumerate(plan):
        mine = _group_slot(group, me)
        if gather:
            targets[a][mine] = sources[a][...]
        else:
            targets[a][mine] = sources[a][mine]
    for copy in sends:
        copy.wait_send()
    for a, (group, gather, summed) in enumerate(plan):
        size = _group_size(group, n)
        for k in range(1, size):
            source = _group_peer(group, n, me, size - k)
            remote(a, k, source, _group_slot(group, source)).wait_recv()
        if summed:
            total = targets[a][0].astype(jnp.float32)
            for j in range(1, size):
                total = total + targets[a][j].astype(jnp.float32)
            results[a][...] = total.astype(results[a].dtype)


def exchange(arrays, plan, collective_id):
    n = lax.axis_size("col")
    plan = tuple((entry + (None,))[:3] for entry in plan)
    shapes = []
    landings = []
    for x, (group, gather, summed) in zip(arrays, plan):
        if summed:
            shapes.append(jax.ShapeDtypeStruct(x.shape[1:], summed))
            landings.append(pltpu.VMEM(x.shape, x.dtype))
        else:
            size = _group_size(group, n)
            shapes.append(
                jax.ShapeDtypeStruct(((size,) + x.shape) if gather else x.shape, x.dtype)
            )
    return pl.pallas_call(
        functools.partial(_exchange_kernel, n, plan),
        out_shape=shapes,
        in_specs=[pl.BlockSpec(memory_space=pltpu.VMEM)] * len(arrays),
        out_specs=[pl.BlockSpec(memory_space=pltpu.VMEM)] * len(arrays),
        scratch_shapes=[
            pltpu.SemaphoreType.DMA((len(arrays), n)),
            pltpu.SemaphoreType.DMA((len(arrays), n)),
        ]
        + landings,
        compiler_params=pltpu.CompilerParams(collective_id=collective_id, has_side_effects=True),
    )(*arrays)


def body(
    tokens,
    w_down,
    q_gain,
    kv_gain,
    w_q_up,
    w_kv_up,
    w_out,
    latent_cache,
    cache_len,
    new_len,
    page_table,
    home_slot,
):
    columns = lax.axis_size("col")
    column_id = lax.axis_index("col")
    row_id = lax.axis_index("row")
    lines = columns // PLANE_X
    line_id = column_id // PLANE_X
    lane_id = column_id % PLANE_X
    group_rows = tokens.shape[0]
    own_rows = group_rows // columns
    q_width = q_gain.shape[0]
    kv_width = kv_gain.shape[0]
    partial_sums = jnp.dot(tokens, w_down, preferred_element_type=jnp.float32)
    pieces, line_query_weight = exchange(
        [partial_sums.astype(jnp.bfloat16).reshape(columns, -1, 128), w_q_up.T],
        [("all", False, jnp.float32), ("y", True)],
        0,
    )
    pieces, line_query_weight, home_slot, cache_len, new_len = lax.optimization_barrier(
        (pieces, line_query_weight, home_slot, cache_len, new_len)
    )
    request_ids = jnp.arange(home_slot.shape[0], dtype=jnp.int32)
    slot_index = jnp.sum(jnp.where(request_ids == row_id, home_slot, 0))
    cached_count = jnp.sum(jnp.where(request_ids == slot_index, cache_len, 0))
    live_count = jnp.sum(jnp.where(request_ids == row_id, new_len, 0))
    combined = pieces.reshape(own_rows, -1)
    own_position = cached_count + column_id * own_rows + jnp.arange(own_rows, dtype=jnp.int32)
    own_cos, own_sin = angle_tables(own_position, ROPE)
    own_query = rms_scale(combined[:, :q_width], q_gain).astype(jnp.bfloat16)
    own_latent = rms_scale(combined[:, q_width : q_width + kv_width], kv_gain).astype(jnp.bfloat16)
    own_rope = rotary(combined[:, q_width + kv_width :], own_cos, own_sin).astype(jnp.bfloat16)
    own_rows_all = jnp.concatenate([own_query, own_latent, own_rope], 1)
    segment = lax.all_gather(latent_cache, "row", axis=0, tiled=True)
    own_cache = lax.dynamic_index_in_dim(segment, slot_index, axis=0, keepdims=False)
    chunk = own_cache.shape[0]
    cache_parts, all_rows = exchange(
        [own_cache.T, own_rows_all.reshape(-1, 128)], [("x", True), ("all", True)], 2
    )
    all_rows = all_rows.reshape(group_rows, -1)
    query_latent = all_rows[:, :q_width]
    fresh_latents = all_rows[:, q_width:]
    query_cos, query_sin = angle_tables(
        cached_count + jnp.arange(group_rows, dtype=jnp.int32), ROPE
    )
    projected = jnp.einsum(
        "qk,hdk->hqd", query_latent, line_query_weight, preferred_element_type=jnp.float32
    )
    head_queries = jnp.concatenate(
        [
            projected[:, :, :NOPE],
            rotary(projected[:, :, NOPE:], query_cos[None], query_sin[None]),
        ],
        2,
    ).astype(jnp.bfloat16)
    head_width = NOPE + VDIM
    heads = columns
    line_weight = lax.dynamic_slice_in_dim(
        w_kv_up.reshape(kv_width, lines, PLANE_X * head_width),
        lane_id * head_width,
        head_width,
        2,
    ).reshape(kv_width, lines * head_width)
    span = PLANE_X * chunk
    span_latents = cache_parts[:, :kv_width, :].transpose(0, 2, 1).reshape(span, kv_width)
    span_rope = cache_parts[:, kv_width:, :].transpose(0, 2, 1).reshape(span, ROPE)
    key_latents = jnp.concatenate([span_latents, fresh_latents[:, :kv_width]], 0)
    key_rope = jnp.concatenate([span_rope, fresh_latents[:, kv_width:]], 0)
    key_count = key_latents.shape[0]
    lifted = (
        jnp.dot(key_latents, line_weight, preferred_element_type=jnp.float32)
        .astype(jnp.bfloat16)
        .reshape(key_count, lines, head_width)
    )
    keys = jnp.concatenate(
        [
            lifted[:, :, :NOPE],
            jnp.broadcast_to(key_rope[:, None, :], (key_count, lines, ROPE)),
        ],
        2,
    )
    score_scale = 1.0 / math.sqrt(NOPE + ROPE)
    key_total = columns * chunk
    page_row = page_table[slot_index]
    page_count = page_row.shape[0]
    page_size = key_total // page_count
    offsets = jnp.arange(page_size, dtype=jnp.int32)
    page_ids = jnp.arange(page_count, dtype=jnp.int32)
    logical_page = jnp.sum(
        page_ids[:, None] * (page_row[:, None] == page_ids[None, :]).astype(jnp.int32), 0
    )
    cached_visible = (logical_page[:, None] * page_size + offsets[None, :]).reshape(
        key_total
    ) < cached_count
    span_visible = lax.dynamic_slice_in_dim(cached_visible, line_id * span, span, 0)
    share = group_rows // lines
    query_index = jnp.arange(group_rows, dtype=jnp.int32)[:, None]
    key_index = jnp.arange(group_rows, dtype=jnp.int32)[None, :]
    fresh_visible = (
        (key_index <= query_index) & (key_index < live_count) & (key_index // share == line_id)
    )
    visible = jnp.concatenate(
        [jnp.broadcast_to(span_visible[None, :], (group_rows, span)), fresh_visible], 1
    )
    scores = (
        jnp.einsum("hqd,khd->hqk", head_queries, keys, preferred_element_type=jnp.float32)
        * score_scale
    )
    scores = jnp.where(visible[None], scores, -jnp.inf)
    row_peak = jnp.max(scores, 2)
    safe_peak = jnp.where(row_peak == -jnp.inf, 0.0, row_peak)
    exponent = jnp.exp(scores - safe_peak[:, :, None])
    row_total = jnp.sum(exponent, 2)
    values = lifted[:, :, NOPE:]
    summed = jnp.einsum(
        "hqk,khd->hdq", exponent.astype(jnp.bfloat16), values, preferred_element_type=jnp.float32
    )
    stats = jnp.stack([row_peak, row_total], 1)
    summed_parts, stat_parts = exchange(
        [summed.astype(jnp.bfloat16), stats], [("y", False), ("y", False)], 4
    )
    peak = jnp.max(stat_parts[:, 0, :], 0)
    factor = jnp.exp(stat_parts[:, 0, :] - peak[None, :])
    total = jnp.sum(factor * stat_parts[:, 1, :], 0)
    merged = jnp.sum(factor[:, None, :] * summed_parts.astype(jnp.float32), 0)
    attended = (merged / total[None, :]).astype(jnp.bfloat16)
    live_rows = jnp.arange(group_rows, dtype=jnp.int32) < live_count
    attended = jnp.where(live_rows[None, :], attended, jnp.zeros_like(attended))
    out_parts = lax.dot_general(
        w_out, attended, (((0,), (0,)), ((), ())), preferred_element_type=jnp.float32
    ).astype(jnp.bfloat16)
    feature_block = out_parts.shape[0] // columns
    (lane_pieces,) = exchange(
        [out_parts.reshape(lines, PLANE_X, feature_block, group_rows).transpose(1, 0, 2, 3)],
        [("x", False, jnp.bfloat16)],
        3,
    )
    (summed_out,) = exchange([lane_pieces], [("y", False, jnp.bfloat16)], 5)
    result = summed_out.T
    return result


def solution(mesh):
    return jax.shard_map(
        body,
        mesh=mesh,
        in_specs=(
            P("row", "col"),
            P("col", None),
            P(),
            P(),
            P(None, "col"),
            P(),
            P("col", None),
            P("row", "col", None),
            P(),
            P(),
            P(),
            P(),
        ),
        out_specs=P("row", "col"),
        check_vma=False,
    )
```

```python
import functools
import math

import jax
import jax.numpy as jnp
from jax import lax
from jax.experimental import pallas as pl
from jax.experimental.pallas import tpu as pltpu
from jax.sharding import PartitionSpec as P

MESH = pl.DeviceIdType.MESH

NOPE = 64
ROPE = 32
VDIM = 64


epsilon = 1e-05


def rms_scale(values, gain):
    return values * lax.rsqrt(jnp.mean(values * values, axis=-1, keepdims=True) + epsilon) * gain


def angle_tables(positions, width):
    half_dim = width // 2
    frequency = 10000.0 ** (-2.0 * jnp.arange(half_dim, dtype=jnp.float32) / width)
    angles = positions.astype(jnp.float32)[:, None] * frequency[None, :]
    return (jnp.cos(angles), jnp.sin(angles))


def rotary(values, cosine, sine_table):
    half_dim = values.shape[-1] // 2
    first_half = values[..., :half_dim]
    second_half = values[..., half_dim:]
    return jnp.concatenate(
        [
            first_half * cosine - second_half * sine_table,
            second_half * cosine + first_half * sine_table,
        ],
        -1,
    )


PLANE_X = 4


def _group_size(group, n):
    return {"all": n, "x": PLANE_X, "y": n // PLANE_X}[group]


def _group_peer(group, n, me, k):
    if group == "x":
        return (me // PLANE_X) * PLANE_X + lax.rem(me % PLANE_X + k, PLANE_X)
    if group == "y":
        return lax.rem(me // PLANE_X + k, n // PLANE_X) * PLANE_X + me % PLANE_X
    return lax.rem(me + k, n)


def _group_slot(group, device):
    if group == "x":
        return device % PLANE_X
    if group == "y":
        return device // PLANE_X
    return device


def _exchange_kernel(n, plan, *refs):
    count = len(plan)
    sources, results = refs[:count], refs[count : 2 * count]
    send_sem, recv_sem = refs[2 * count : 2 * count + 2]
    landings = iter(refs[2 * count + 2 :])
    targets = [next(landings) if plan[a][2] else results[a] for a in range(count)]
    me = lax.axis_index("col")
    barrier = pltpu.get_barrier_semaphore()
    groups = sorted({entry[0] for entry in plan})
    if "all" in groups:
        groups = ["all"]
    greeted = 0
    for group in groups:
        for k in range(1, _group_size(group, n)):
            pl.semaphore_signal(
                barrier, inc=1, device_id={"col": _group_peer(group, n, me, k)},
                device_id_type=MESH,
            )
            greeted += 1
    pl.semaphore_wait(barrier, greeted)

    def remote(a, k, peer, landing):
        group, gather, _, axis = plan[a]
        x_ref = sources[a]
        slot = _group_slot(group, peer)
        return pltpu.make_async_remote_copy(
            src_ref=x_ref if gather else (x_ref.at[slot] if axis == 0 else x_ref.at[:, slot]),
            dst_ref=targets[a].at[landing],
            send_sem=send_sem.at[a, k],
            recv_sem=recv_sem.at[a, k],
            device_id={"col": peer},
            device_id_type=MESH,
        )

    sends = []
    for a, (group, gather, _, _) in enumerate(plan):
        for k in range(1, _group_size(group, n)):
            copy = remote(a, k, _group_peer(group, n, me, k), _group_slot(group, me))
            copy.start()
            sends.append(copy)
    for a, (group, gather, _, axis) in enumerate(plan):
        mine = _group_slot(group, me)
        if gather:
            targets[a][mine] = sources[a][...]
        elif axis == 0:
            targets[a][mine] = sources[a][mine]
        else:
            targets[a][mine] = sources[a][:, mine]
    for copy in sends:
        copy.wait_send()
    for a, (group, gather, summed, _) in enumerate(plan):
        size = _group_size(group, n)
        for k in range(1, size):
            source = _group_peer(group, n, me, size - k)
            remote(a, k, source, _group_slot(group, source)).wait_recv()
        if summed:
            total = targets[a][0].astype(jnp.float32)
            for j in range(1, size):
                total = total + targets[a][j].astype(jnp.float32)
            results[a][...] = total.astype(results[a].dtype)


def exchange(arrays, plan, collective_id):
    n = lax.axis_size("col")
    plan = tuple(tuple(entry) + (None, 0)[len(entry) - 2 :] for entry in plan)
    shapes = []
    landings = []
    for x, (group, gather, summed, axis) in zip(arrays, plan):
        if summed:
            chunk_shape = x.shape[:axis] + x.shape[axis + 1 :]
            size = x.shape[axis]
            shapes.append(jax.ShapeDtypeStruct(chunk_shape, summed))
            landings.append(pltpu.VMEM((size,) + chunk_shape, x.dtype))
        else:
            size = _group_size(group, n)
            shapes.append(
                jax.ShapeDtypeStruct(((size,) + x.shape) if gather else x.shape, x.dtype)
            )
    return pl.pallas_call(
        functools.partial(_exchange_kernel, n, plan),
        out_shape=shapes,
        in_specs=[pl.BlockSpec(memory_space=pltpu.VMEM)] * len(arrays),
        out_specs=[pl.BlockSpec(memory_space=pltpu.VMEM)] * len(arrays),
        scratch_shapes=[
            pltpu.SemaphoreType.DMA((len(arrays), n)),
            pltpu.SemaphoreType.DMA((len(arrays), n)),
        ]
        + landings,
        compiler_params=pltpu.CompilerParams(collective_id=collective_id, has_side_effects=True),
    )(*arrays)


def body(
    tokens,
    w_down,
    q_gain,
    kv_gain,
    w_q_up,
    w_kv_up,
    w_out,
    latent_cache,
    cache_len,
    new_len,
    page_table,
    home_slot,
):
    columns = lax.axis_size("col")
    column_id = lax.axis_index("col")
    row_id = lax.axis_index("row")
    lines = columns // PLANE_X
    line_id = column_id // PLANE_X
    lane_id = column_id % PLANE_X
    group_rows = tokens.shape[0]
    own_rows = group_rows // columns
    q_width = q_gain.shape[0]
    kv_width = kv_gain.shape[0]
    partial_sums = jnp.dot(tokens, w_down, preferred_element_type=jnp.float32)
    pieces, line_query_weight = exchange(
        [partial_sums.astype(jnp.bfloat16).reshape(columns, -1, 128), w_q_up.T],
        [("all", False, jnp.float32), ("y", True)],
        0,
    )
    pieces, line_query_weight, home_slot, cache_len, new_len = lax.optimization_barrier(
        (pieces, line_query_weight, home_slot, cache_len, new_len)
    )
    request_ids = jnp.arange(home_slot.shape[0], dtype=jnp.int32)
    slot_index = jnp.sum(jnp.where(request_ids == row_id, home_slot, 0))
    cached_count = jnp.sum(jnp.where(request_ids == slot_index, cache_len, 0))
    live_count = jnp.sum(jnp.where(request_ids == row_id, new_len, 0))
    combined = pieces.reshape(own_rows, -1)
    own_position = cached_count + column_id * own_rows + jnp.arange(own_rows, dtype=jnp.int32)
    own_cos, own_sin = angle_tables(own_position, ROPE)
    own_query = rms_scale(combined[:, :q_width], q_gain).astype(jnp.bfloat16)
    own_latent = rms_scale(combined[:, q_width : q_width + kv_width], kv_gain).astype(jnp.bfloat16)
    own_rope = rotary(combined[:, q_width + kv_width :], own_cos, own_sin).astype(jnp.bfloat16)
    own_rows_all = jnp.concatenate([own_query, own_latent, own_rope], 1)
    segment = lax.all_gather(latent_cache, "row", axis=0, tiled=True)
    own_cache = lax.dynamic_index_in_dim(segment, slot_index, axis=0, keepdims=False)
    chunk = own_cache.shape[0]
    cache_parts, all_rows = exchange(
        [own_cache.T, own_rows_all.reshape(-1, 128)], [("x", True), ("all", True)], 2
    )
    all_rows = all_rows.reshape(group_rows, -1)
    query_latent = all_rows[:, :q_width]
    fresh_latents = all_rows[:, q_width:]
    query_cos, query_sin = angle_tables(
        cached_count + jnp.arange(group_rows, dtype=jnp.int32), ROPE
    )
    projected = jnp.einsum(
        "qk,hdk->hqd", query_latent, line_query_weight, preferred_element_type=jnp.float32
    )
    head_queries = jnp.concatenate(
        [
            projected[:, :, :NOPE],
            rotary(projected[:, :, NOPE:], query_cos[None], query_sin[None]),
        ],
        2,
    ).astype(jnp.bfloat16)
    head_width = NOPE + VDIM
    heads = columns
    line_weight = lax.dynamic_slice_in_dim(
        w_kv_up.reshape(kv_width, lines, PLANE_X * head_width),
        lane_id * head_width,
        head_width,
        2,
    ).reshape(kv_width, lines * head_width)
    span = PLANE_X * chunk
    span_latents = cache_parts[:, :kv_width, :].transpose(0, 2, 1).reshape(span, kv_width)
    span_rope = cache_parts[:, kv_width:, :].transpose(0, 2, 1).reshape(span, ROPE)
    key_latents = jnp.concatenate([span_latents, fresh_latents[:, :kv_width]], 0)
    key_rope = jnp.concatenate([span_rope, fresh_latents[:, kv_width:]], 0)
    key_count = key_latents.shape[0]
    lifted = (
        jnp.dot(key_latents, line_weight, preferred_element_type=jnp.float32)
        .astype(jnp.bfloat16)
        .reshape(key_count, lines, head_width)
    )
    keys = jnp.concatenate(
        [
            lifted[:, :, :NOPE],
            jnp.broadcast_to(key_rope[:, None, :], (key_count, lines, ROPE)),
        ],
        2,
    )
    score_scale = 1.0 / math.sqrt(NOPE + ROPE)
    key_total = columns * chunk
    page_row = page_table[slot_index]
    page_count = page_row.shape[0]
    page_size = key_total // page_count
    offsets = jnp.arange(page_size, dtype=jnp.int32)
    page_ids = jnp.arange(page_count, dtype=jnp.int32)
    logical_page = jnp.sum(
        page_ids[:, None] * (page_row[:, None] == page_ids[None, :]).astype(jnp.int32), 0
    )
    cached_visible = (logical_page[:, None] * page_size + offsets[None, :]).reshape(
        key_total
    ) < cached_count
    span_visible = lax.dynamic_slice_in_dim(cached_visible, line_id * span, span, 0)
    share = group_rows // lines
    query_index = jnp.arange(group_rows, dtype=jnp.int32)[:, None]
    key_index = jnp.arange(group_rows, dtype=jnp.int32)[None, :]
    fresh_visible = (
        (key_index <= query_index) & (key_index < live_count) & (key_index // share == line_id)
    )
    visible = jnp.concatenate(
        [jnp.broadcast_to(span_visible[None, :], (group_rows, span)), fresh_visible], 1
    )
    scores = (
        jnp.einsum("hqd,khd->hqk", head_queries, keys, preferred_element_type=jnp.float32)
        * score_scale
    )
    scores = jnp.where(visible[None], scores, -jnp.inf)
    row_peak = jnp.max(scores, 2)
    safe_peak = jnp.where(row_peak == -jnp.inf, 0.0, row_peak)
    exponent = jnp.exp(scores - safe_peak[:, :, None])
    row_total = jnp.sum(exponent, 2)
    values = lifted[:, :, NOPE:]
    summed = jnp.einsum(
        "hqk,khd->hdq", exponent.astype(jnp.bfloat16), values, preferred_element_type=jnp.float32
    )
    stats = jnp.stack([row_peak, row_total], 1)
    summed_parts, stat_parts = exchange(
        [summed.astype(jnp.bfloat16), stats], [("y", False), ("y", False)], 4
    )
    peak = jnp.max(stat_parts[:, 0, :], 0)
    factor = jnp.exp(stat_parts[:, 0, :] - peak[None, :])
    total = jnp.sum(factor * stat_parts[:, 1, :], 0)
    merged = jnp.sum(factor[:, None, :] * summed_parts.astype(jnp.float32), 0)
    attended = (merged / total[None, :]).astype(jnp.bfloat16)
    live_rows = jnp.arange(group_rows, dtype=jnp.int32) < live_count
    attended = jnp.where(live_rows[None, :], attended, jnp.zeros_like(attended))
    out_parts = lax.dot_general(
        w_out, attended, (((0,), (0,)), ((), ())), preferred_element_type=jnp.float32
    ).astype(jnp.bfloat16)
    feature_block = out_parts.shape[0] // columns
    (lane_pieces,) = exchange(
        [out_parts.reshape(lines, PLANE_X, feature_block, group_rows)],
        [("x", False, jnp.bfloat16, 1)],
        3,
    )
    (summed_out,) = exchange([lane_pieces], [("y", False, jnp.bfloat16)], 5)
    result = summed_out.T
    return result


def solution(mesh):
    return jax.shard_map(
        body,
        mesh=mesh,
        in_specs=(
            P("row", "col"),
            P("col", None),
            P(),
            P(),
            P(None, "col"),
            P(),
            P("col", None),
            P("row", "col", None),
            P(),
            P(),
            P(),
            P(),
        ),
        out_specs=P("row", "col"),
        check_vma=False,
    )
```

```python
import functools
import math

import jax
import jax.numpy as jnp
from jax import lax
from jax.experimental import pallas as pl
from jax.experimental.pallas import tpu as pltpu
from jax.sharding import PartitionSpec as P

MESH = pl.DeviceIdType.MESH

NOPE = 64
ROPE = 32
VDIM = 64


epsilon = 1e-05


def rms_scale(values, gain):
    return values * lax.rsqrt(jnp.mean(values * values, axis=-1, keepdims=True) + epsilon) * gain


def angle_tables(positions, width):
    half_dim = width // 2
    frequency = 10000.0 ** (-2.0 * jnp.arange(half_dim, dtype=jnp.float32) / width)
    angles = positions.astype(jnp.float32)[:, None] * frequency[None, :]
    return (jnp.cos(angles), jnp.sin(angles))


def rotary(values, cosine, sine_table):
    half_dim = values.shape[-1] // 2
    first_half = values[..., :half_dim]
    second_half = values[..., half_dim:]
    return jnp.concatenate(
        [
            first_half * cosine - second_half * sine_table,
            second_half * cosine + first_half * sine_table,
        ],
        -1,
    )


PLANE_X = 4


def _group_size(group, n):
    return {"all": n, "x": PLANE_X, "y": n // PLANE_X}[group]


def _group_peer(group, n, me, k):
    if group == "x":
        return (me // PLANE_X) * PLANE_X + lax.rem(me % PLANE_X + k, PLANE_X)
    if group == "y":
        return lax.rem(me // PLANE_X + k, n // PLANE_X) * PLANE_X + me % PLANE_X
    return lax.rem(me + k, n)


def _group_slot(group, device):
    if group == "x":
        return device % PLANE_X
    if group == "y":
        return device // PLANE_X
    return device


def _exchange_kernel(n, plan, *refs):
    count = len(plan)
    sources, results = refs[:count], refs[count : 2 * count]
    send_sem, recv_sem = refs[2 * count : 2 * count + 2]
    landings = iter(refs[2 * count + 2 :])
    targets = [next(landings) if plan[a][2] else results[a] for a in range(count)]
    me = lax.axis_index("col")
    barrier = pltpu.get_barrier_semaphore()
    groups = sorted({entry[0] for entry in plan})
    if "all" in groups:
        groups = ["all"]
    greeted = 0
    for group in groups:
        for k in range(1, _group_size(group, n)):
            pl.semaphore_signal(
                barrier, inc=1, device_id={"col": _group_peer(group, n, me, k)},
                device_id_type=MESH,
            )
            greeted += 1
    pl.semaphore_wait(barrier, greeted)

    def remote(a, k, peer, landing):
        group, gather, _, axis = plan[a]
        x_ref = sources[a]
        slot = _group_slot(group, peer)
        return pltpu.make_async_remote_copy(
            src_ref=x_ref if gather else (x_ref.at[slot] if axis == 0 else x_ref.at[:, slot]),
            dst_ref=targets[a].at[landing],
            send_sem=send_sem.at[a, k],
            recv_sem=recv_sem.at[a, k],
            device_id={"col": peer},
            device_id_type=MESH,
        )

    sends = []
    for a, (group, gather, _, _) in enumerate(plan):
        for k in range(1, _group_size(group, n)):
            copy = remote(a, k, _group_peer(group, n, me, k), _group_slot(group, me))
            copy.start()
            sends.append(copy)
    for a, (group, gather, _, axis) in enumerate(plan):
        mine = _group_slot(group, me)
        if gather:
            targets[a][mine] = sources[a][...]
        elif axis == 0:
            targets[a][mine] = sources[a][mine]
        else:
            targets[a][mine] = sources[a][:, mine]
    for copy in sends:
        copy.wait_send()
    for a, (group, gather, summed, _) in enumerate(plan):
        size = _group_size(group, n)
        for k in range(1, size):
            source = _group_peer(group, n, me, size - k)
            remote(a, k, source, _group_slot(group, source)).wait_recv()
        if summed == "merge":
            continue
        if summed:
            total = targets[a][0].astype(jnp.float32)
            for j in range(1, size):
                total = total + targets[a][j].astype(jnp.float32)
            results[a][...] = total.astype(results[a].dtype)
    if plan[0][2] == "merge":
        parts, stats = targets[0], targets[1]
        size = parts.shape[0]
        peak = stats[0][0:1, :]
        for j in range(1, size):
            peak = jnp.maximum(peak, stats[j][0:1, :])
        total = jnp.zeros_like(peak)
        merged = jnp.zeros(parts.shape[1:], jnp.float32)
        for j in range(size):
            factor = jnp.exp(stats[j][0:1, :] - peak)
            total = total + factor * stats[j][1:2, :]
            merged = merged + factor * parts[j].astype(jnp.float32)
        results[0][...] = (merged / total).astype(results[0].dtype)


def exchange(arrays, plan, collective_id):
    n = lax.axis_size("col")
    plan = tuple(tuple(entry) + (None, 0)[len(entry) - 2 :] for entry in plan)
    shapes = []
    landings = []
    for x, (group, gather, summed, axis) in zip(arrays, plan):
        if summed:
            chunk_shape = x.shape[:axis] + x.shape[axis + 1 :]
            size = x.shape[axis]
            shapes.append(
                jax.ShapeDtypeStruct(chunk_shape, jnp.bfloat16 if summed == "merge" else summed)
            )
            landings.append(pltpu.VMEM((size,) + chunk_shape, x.dtype))
        else:
            size = _group_size(group, n)
            shapes.append(
                jax.ShapeDtypeStruct(((size,) + x.shape) if gather else x.shape, x.dtype)
            )
    return pl.pallas_call(
        functools.partial(_exchange_kernel, n, plan),
        out_shape=shapes,
        in_specs=[pl.BlockSpec(memory_space=pltpu.VMEM)] * len(arrays),
        out_specs=[pl.BlockSpec(memory_space=pltpu.VMEM)] * len(arrays),
        scratch_shapes=[
            pltpu.SemaphoreType.DMA((len(arrays), n)),
            pltpu.SemaphoreType.DMA((len(arrays), n)),
        ]
        + landings,
        compiler_params=pltpu.CompilerParams(collective_id=collective_id, has_side_effects=True),
    )(*arrays)


def body(
    tokens,
    w_down,
    q_gain,
    kv_gain,
    w_q_up,
    w_kv_up,
    w_out,
    latent_cache,
    cache_len,
    new_len,
    page_table,
    home_slot,
):
    columns = lax.axis_size("col")
    column_id = lax.axis_index("col")
    row_id = lax.axis_index("row")
    lines = columns // PLANE_X
    line_id = column_id // PLANE_X
    lane_id = column_id % PLANE_X
    group_rows = tokens.shape[0]
    own_rows = group_rows // columns
    q_width = q_gain.shape[0]
    kv_width = kv_gain.shape[0]
    partial_sums = jnp.dot(tokens, w_down, preferred_element_type=jnp.float32)
    pieces, line_query_weight = exchange(
        [partial_sums.astype(jnp.bfloat16).reshape(columns, -1, 128), w_q_up.T],
        [("all", False, jnp.float32), ("y", True)],
        0,
    )
    pieces, line_query_weight, home_slot, cache_len, new_len = lax.optimization_barrier(
        (pieces, line_query_weight, home_slot, cache_len, new_len)
    )
    request_ids = jnp.arange(home_slot.shape[0], dtype=jnp.int32)
    slot_index = jnp.sum(jnp.where(request_ids == row_id, home_slot, 0))
    cached_count = jnp.sum(jnp.where(request_ids == slot_index, cache_len, 0))
    live_count = jnp.sum(jnp.where(request_ids == row_id, new_len, 0))
    combined = pieces.reshape(own_rows, -1)
    own_position = cached_count + column_id * own_rows + jnp.arange(own_rows, dtype=jnp.int32)
    own_cos, own_sin = angle_tables(own_position, ROPE)
    own_query = rms_scale(combined[:, :q_width], q_gain).astype(jnp.bfloat16)
    own_latent = rms_scale(combined[:, q_width : q_width + kv_width], kv_gain).astype(jnp.bfloat16)
    own_rope = rotary(combined[:, q_width + kv_width :], own_cos, own_sin).astype(jnp.bfloat16)
    own_rows_all = jnp.concatenate([own_query, own_latent, own_rope], 1)
    segment = lax.all_gather(latent_cache, "row", axis=0, tiled=True)
    own_cache = lax.dynamic_index_in_dim(segment, slot_index, axis=0, keepdims=False)
    chunk = own_cache.shape[0]
    cache_parts, all_rows = exchange(
        [own_cache.T, own_rows_all.reshape(-1, 128)], [("x", True), ("all", True)], 2
    )
    all_rows = all_rows.reshape(group_rows, -1)
    query_latent = all_rows[:, :q_width]
    fresh_latents = all_rows[:, q_width:]
    query_cos, query_sin = angle_tables(
        cached_count + jnp.arange(group_rows, dtype=jnp.int32), ROPE
    )
    projected = jnp.einsum(
        "qk,hdk->hqd", query_latent, line_query_weight, preferred_element_type=jnp.float32
    )
    head_queries = jnp.concatenate(
        [
            projected[:, :, :NOPE],
            rotary(projected[:, :, NOPE:], query_cos[None], query_sin[None]),
        ],
        2,
    ).astype(jnp.bfloat16)
    head_width = NOPE + VDIM
    heads = columns
    line_weight = lax.dynamic_slice_in_dim(
        w_kv_up.reshape(kv_width, lines, PLANE_X * head_width),
        lane_id * head_width,
        head_width,
        2,
    ).reshape(kv_width, lines * head_width)
    span = PLANE_X * chunk
    span_latents = cache_parts[:, :kv_width, :].transpose(0, 2, 1).reshape(span, kv_width)
    span_rope = cache_parts[:, kv_width:, :].transpose(0, 2, 1).reshape(span, ROPE)
    key_latents = jnp.concatenate([span_latents, fresh_latents[:, :kv_width]], 0)
    key_rope = jnp.concatenate([span_rope, fresh_latents[:, kv_width:]], 0)
    key_count = key_latents.shape[0]
    lifted = (
        jnp.dot(key_latents, line_weight, preferred_element_type=jnp.float32)
        .astype(jnp.bfloat16)
        .reshape(key_count, lines, head_width)
    )
    keys = jnp.concatenate(
        [
            lifted[:, :, :NOPE],
            jnp.broadcast_to(key_rope[:, None, :], (key_count, lines, ROPE)),
        ],
        2,
    )
    score_scale = 1.0 / math.sqrt(NOPE + ROPE)
    key_total = columns * chunk
    page_row = page_table[slot_index]
    page_count = page_row.shape[0]
    page_size = key_total // page_count
    offsets = jnp.arange(page_size, dtype=jnp.int32)
    page_ids = jnp.arange(page_count, dtype=jnp.int32)
    logical_page = jnp.sum(
        page_ids[:, None] * (page_row[:, None] == page_ids[None, :]).astype(jnp.int32), 0
    )
    cached_visible = (logical_page[:, None] * page_size + offsets[None, :]).reshape(
        key_total
    ) < cached_count
    span_visible = lax.dynamic_slice_in_dim(cached_visible, line_id * span, span, 0)
    share = group_rows // lines
    query_index = jnp.arange(group_rows, dtype=jnp.int32)[:, None]
    key_index = jnp.arange(group_rows, dtype=jnp.int32)[None, :]
    fresh_visible = (
        (key_index <= query_index) & (key_index < live_count) & (key_index // share == line_id)
    )
    visible = jnp.concatenate(
        [jnp.broadcast_to(span_visible[None, :], (group_rows, span)), fresh_visible], 1
    )
    scores = (
        jnp.einsum("hqd,khd->hqk", head_queries, keys, preferred_element_type=jnp.float32)
        * score_scale
    )
    scores = jnp.where(visible[None], scores, -jnp.inf)
    row_peak = jnp.max(scores, 2)
    safe_peak = jnp.where(row_peak == -jnp.inf, 0.0, row_peak)
    exponent = jnp.exp(scores - safe_peak[:, :, None])
    row_total = jnp.sum(exponent, 2)
    values = lifted[:, :, NOPE:]
    summed = jnp.einsum(
        "hqk,khd->hdq", exponent.astype(jnp.bfloat16), values, preferred_element_type=jnp.float32
    )
    stats = jnp.stack([row_peak, row_total], 1)
    attended, _ = exchange(
        [summed.astype(jnp.bfloat16), stats],
        [("y", False, "merge"), ("y", False, jnp.float32)],
        4,
    )
    live_rows = jnp.arange(group_rows, dtype=jnp.int32) < live_count
    attended = jnp.where(live_rows[None, :], attended, jnp.zeros_like(attended))
    out_parts = lax.dot_general(
        w_out, attended, (((0,), (0,)), ((), ())), preferred_element_type=jnp.float32
    ).astype(jnp.bfloat16)
    feature_block = out_parts.shape[0] // columns
    (lane_pieces,) = exchange(
        [out_parts.reshape(lines, PLANE_X, feature_block, group_rows)],
        [("x", False, jnp.bfloat16, 1)],
        3,
    )
    (summed_out,) = exchange([lane_pieces], [("y", False, jnp.bfloat16)], 5)
    result = summed_out.T
    return result


def solution(mesh):
    return jax.shard_map(
        body,
        mesh=mesh,
        in_specs=(
            P("row", "col"),
            P("col", None),
            P(),
            P(),
            P(None, "col"),
            P(),
            P("col", None),
            P("row", "col", None),
            P(),
            P(),
            P(),
            P(),
        ),
        out_specs=P("row", "col"),
        check_vma=False,
    )
```

```python
import functools
import math

import jax
import jax.numpy as jnp
from jax import lax
from jax.experimental import pallas as pl
from jax.experimental.pallas import tpu as pltpu
from jax.sharding import PartitionSpec as P

MESH = pl.DeviceIdType.MESH

NOPE = 64
ROPE = 32
VDIM = 64


epsilon = 1e-05


def rms_scale(values, gain):
    return values * lax.rsqrt(jnp.mean(values * values, axis=-1, keepdims=True) + epsilon) * gain


def angle_tables(positions, width):
    half_dim = width // 2
    frequency = 10000.0 ** (-2.0 * jnp.arange(half_dim, dtype=jnp.float32) / width)
    angles = positions.astype(jnp.float32)[:, None] * frequency[None, :]
    return (jnp.cos(angles), jnp.sin(angles))


def rotary(values, cosine, sine_table):
    half_dim = values.shape[-1] // 2
    first_half = values[..., :half_dim]
    second_half = values[..., half_dim:]
    return jnp.concatenate(
        [
            first_half * cosine - second_half * sine_table,
            second_half * cosine + first_half * sine_table,
        ],
        -1,
    )


PLANE_X = 4


def _group_size(group, n):
    return {"all": n, "x": PLANE_X, "y": n // PLANE_X}[group]


def _group_peer(group, n, me, k):
    if group == "x":
        return (me // PLANE_X) * PLANE_X + lax.rem(me % PLANE_X + k, PLANE_X)
    if group == "y":
        return lax.rem(me // PLANE_X + k, n // PLANE_X) * PLANE_X + me % PLANE_X
    return lax.rem(me + k, n)


def _group_slot(group, device):
    if group == "x":
        return device % PLANE_X
    if group == "y":
        return device // PLANE_X
    return device


def _exchange_kernel(n, plan, *refs):
    count = len(plan)
    sources, results = refs[:count], refs[count : 2 * count]
    send_sem, recv_sem = refs[2 * count : 2 * count + 2]
    landings = iter(refs[2 * count + 2 :])
    targets = [next(landings) if plan[a][2] else results[a] for a in range(count)]
    me = lax.axis_index("col")
    barrier = pltpu.get_barrier_semaphore()
    groups = sorted({entry[0] for entry in plan})
    if "all" in groups:
        groups = ["all"]
    greeted = 0
    for group in groups:
        for k in range(1, _group_size(group, n)):
            pl.semaphore_signal(
                barrier, inc=1, device_id={"col": _group_peer(group, n, me, k)},
                device_id_type=MESH,
            )
            greeted += 1
    pl.semaphore_wait(barrier, greeted)

    def remote(a, k, peer, landing):
        group, gather, _, axis = plan[a]
        x_ref = sources[a]
        slot = _group_slot(group, peer)
        return pltpu.make_async_remote_copy(
            src_ref=x_ref if gather else (x_ref.at[slot] if axis == 0 else x_ref.at[:, slot]),
            dst_ref=targets[a].at[landing],
            send_sem=send_sem.at[a, k],
            recv_sem=recv_sem.at[a, k],
            device_id={"col": peer},
            device_id_type=MESH,
        )

    sends = []
    for a, (group, gather, _, _) in enumerate(plan):
        for k in range(1, _group_size(group, n)):
            copy = remote(a, k, _group_peer(group, n, me, k), _group_slot(group, me))
            copy.start()
            sends.append(copy)
    for a, (group, gather, _, axis) in enumerate(plan):
        mine = _group_slot(group, me)
        if gather:
            targets[a][mine] = sources[a][...]
        elif axis == 0:
            targets[a][mine] = sources[a][mine]
        else:
            targets[a][mine] = sources[a][:, mine]
    for copy in sends:
        copy.wait_send()
    for a, (group, gather, summed, _) in enumerate(plan):
        size = _group_size(group, n)
        for k in range(1, size):
            source = _group_peer(group, n, me, size - k)
            remote(a, k, source, _group_slot(group, source)).wait_recv()
        if summed == "merge":
            continue
        if summed:
            total = targets[a][0].astype(jnp.float32)
            for j in range(1, size):
                total = total + targets[a][j].astype(jnp.float32)
            if summed == "flip":
                total = total.T
            results[a][...] = total.astype(results[a].dtype)
    if plan[0][2] == "merge":
        parts, stats = targets[0], targets[1]
        size = parts.shape[0]
        peak = stats[0][0:1, :]
        for j in range(1, size):
            peak = jnp.maximum(peak, stats[j][0:1, :])
        total = jnp.zeros_like(peak)
        merged = jnp.zeros(parts.shape[1:], jnp.float32)
        for j in range(size):
            factor = jnp.exp(stats[j][0:1, :] - peak)
            total = total + factor * stats[j][1:2, :]
            merged = merged + factor * parts[j].astype(jnp.float32)
        results[0][...] = (merged / total).astype(results[0].dtype)


def exchange(arrays, plan, collective_id):
    n = lax.axis_size("col")
    plan = tuple(tuple(entry) + (None, 0)[len(entry) - 2 :] for entry in plan)
    shapes = []
    landings = []
    for x, (group, gather, summed, axis) in zip(arrays, plan):
        if summed:
            chunk_shape = x.shape[:axis] + x.shape[axis + 1 :]
            size = x.shape[axis]
            shapes.append(
                jax.ShapeDtypeStruct(
                    chunk_shape[::-1] if summed == "flip" else chunk_shape,
                    jnp.bfloat16 if summed in ("merge", "flip") else summed,
                )
            )
            landings.append(pltpu.VMEM((size,) + chunk_shape, x.dtype))
        else:
            size = _group_size(group, n)
            shapes.append(
                jax.ShapeDtypeStruct(((size,) + x.shape) if gather else x.shape, x.dtype)
            )
    return pl.pallas_call(
        functools.partial(_exchange_kernel, n, plan),
        out_shape=shapes,
        in_specs=[pl.BlockSpec(memory_space=pltpu.VMEM)] * len(arrays),
        out_specs=[pl.BlockSpec(memory_space=pltpu.VMEM)] * len(arrays),
        scratch_shapes=[
            pltpu.SemaphoreType.DMA((len(arrays), n)),
            pltpu.SemaphoreType.DMA((len(arrays), n)),
        ]
        + landings,
        compiler_params=pltpu.CompilerParams(collective_id=collective_id, has_side_effects=True),
    )(*arrays)


def body(
    tokens,
    w_down,
    q_gain,
    kv_gain,
    w_q_up,
    w_kv_up,
    w_out,
    latent_cache,
    cache_len,
    new_len,
    page_table,
    home_slot,
):
    columns = lax.axis_size("col")
    column_id = lax.axis_index("col")
    row_id = lax.axis_index("row")
    lines = columns // PLANE_X
    line_id = column_id // PLANE_X
    lane_id = column_id % PLANE_X
    group_rows = tokens.shape[0]
    own_rows = group_rows // columns
    q_width = q_gain.shape[0]
    kv_width = kv_gain.shape[0]
    partial_sums = jnp.dot(tokens, w_down, preferred_element_type=jnp.float32)
    pieces, line_query_weight = exchange(
        [partial_sums.astype(jnp.bfloat16).reshape(columns, -1, 128), w_q_up.T],
        [("all", False, jnp.float32), ("y", True)],
        0,
    )
    pieces, line_query_weight, home_slot, cache_len, new_len = lax.optimization_barrier(
        (pieces, line_query_weight, home_slot, cache_len, new_len)
    )
    request_ids = jnp.arange(home_slot.shape[0], dtype=jnp.int32)
    slot_index = jnp.sum(jnp.where(request_ids == row_id, home_slot, 0))
    cached_count = jnp.sum(jnp.where(request_ids == slot_index, cache_len, 0))
    live_count = jnp.sum(jnp.where(request_ids == row_id, new_len, 0))
    combined = pieces.reshape(own_rows, -1)
    own_position = cached_count + column_id * own_rows + jnp.arange(own_rows, dtype=jnp.int32)
    own_cos, own_sin = angle_tables(own_position, ROPE)
    own_query = rms_scale(combined[:, :q_width], q_gain).astype(jnp.bfloat16)
    own_latent = rms_scale(combined[:, q_width : q_width + kv_width], kv_gain).astype(jnp.bfloat16)
    own_rope = rotary(combined[:, q_width + kv_width :], own_cos, own_sin).astype(jnp.bfloat16)
    own_rows_all = jnp.concatenate([own_query, own_latent, own_rope], 1)
    segment = lax.all_gather(latent_cache, "row", axis=0, tiled=True)
    own_cache = lax.dynamic_index_in_dim(segment, slot_index, axis=0, keepdims=False)
    chunk = own_cache.shape[0]
    cache_parts, all_rows = exchange(
        [own_cache.T, own_rows_all.reshape(-1, 128)], [("x", True), ("all", True)], 2
    )
    all_rows = all_rows.reshape(group_rows, -1)
    query_latent = all_rows[:, :q_width]
    fresh_latents = all_rows[:, q_width:]
    query_cos, query_sin = angle_tables(
        cached_count + jnp.arange(group_rows, dtype=jnp.int32), ROPE
    )
    projected = jnp.einsum(
        "qk,hdk->hqd", query_latent, line_query_weight, preferred_element_type=jnp.float32
    )
    head_queries = jnp.concatenate(
        [
            projected[:, :, :NOPE],
            rotary(projected[:, :, NOPE:], query_cos[None], query_sin[None]),
        ],
        2,
    ).astype(jnp.bfloat16)
    head_width = NOPE + VDIM
    heads = columns
    line_weight = lax.dynamic_slice_in_dim(
        w_kv_up.reshape(kv_width, lines, PLANE_X * head_width),
        lane_id * head_width,
        head_width,
        2,
    ).reshape(kv_width, lines * head_width)
    span = PLANE_X * chunk
    span_latents = cache_parts[:, :kv_width, :].transpose(0, 2, 1).reshape(span, kv_width)
    span_rope = cache_parts[:, kv_width:, :].transpose(0, 2, 1).reshape(span, ROPE)
    key_latents = jnp.concatenate([span_latents, fresh_latents[:, :kv_width]], 0)
    key_rope = jnp.concatenate([span_rope, fresh_latents[:, kv_width:]], 0)
    key_count = key_latents.shape[0]
    lifted = (
        jnp.dot(key_latents, line_weight, preferred_element_type=jnp.float32)
        .astype(jnp.bfloat16)
        .reshape(key_count, lines, head_width)
    )
    keys = jnp.concatenate(
        [
            lifted[:, :, :NOPE],
            jnp.broadcast_to(key_rope[:, None, :], (key_count, lines, ROPE)),
        ],
        2,
    )
    score_scale = 1.0 / math.sqrt(NOPE + ROPE)
    key_total = columns * chunk
    page_row = page_table[slot_index]
    page_count = page_row.shape[0]
    page_size = key_total // page_count
    offsets = jnp.arange(page_size, dtype=jnp.int32)
    page_ids = jnp.arange(page_count, dtype=jnp.int32)
    logical_page = jnp.sum(
        page_ids[:, None] * (page_row[:, None] == page_ids[None, :]).astype(jnp.int32), 0
    )
    cached_visible = (logical_page[:, None] * page_size + offsets[None, :]).reshape(
        key_total
    ) < cached_count
    span_visible = lax.dynamic_slice_in_dim(cached_visible, line_id * span, span, 0)
    share = group_rows // lines
    query_index = jnp.arange(group_rows, dtype=jnp.int32)[:, None]
    key_index = jnp.arange(group_rows, dtype=jnp.int32)[None, :]
    fresh_visible = (
        (key_index <= query_index) & (key_index < live_count) & (key_index // share == line_id)
    )
    visible = jnp.concatenate(
        [jnp.broadcast_to(span_visible[None, :], (group_rows, span)), fresh_visible], 1
    )
    scores = (
        jnp.einsum("hqd,khd->hqk", head_queries, keys, preferred_element_type=jnp.float32)
        * score_scale
    )
    scores = jnp.where(visible[None], scores, -jnp.inf)
    row_peak = jnp.max(scores, 2)
    safe_peak = jnp.where(row_peak == -jnp.inf, 0.0, row_peak)
    exponent = jnp.exp(scores - safe_peak[:, :, None])
    row_total = jnp.sum(exponent, 2)
    values = lifted[:, :, NOPE:]
    summed = jnp.einsum(
        "hqk,khd->hdq", exponent.astype(jnp.bfloat16), values, preferred_element_type=jnp.float32
    )
    stats = jnp.stack([row_peak, row_total], 1)
    attended, _ = exchange(
        [summed.astype(jnp.bfloat16), stats],
        [("y", False, "merge"), ("y", False, jnp.float32)],
        4,
    )
    live_rows = jnp.arange(group_rows, dtype=jnp.int32) < live_count
    attended = jnp.where(live_rows[None, :], attended, jnp.zeros_like(attended))
    out_parts = lax.dot_general(
        w_out, attended, (((0,), (0,)), ((), ())), preferred_element_type=jnp.float32
    ).astype(jnp.bfloat16)
    feature_block = out_parts.shape[0] // columns
    (lane_pieces,) = exchange(
        [out_parts.reshape(lines, PLANE_X, feature_block, group_rows)],
        [("x", False, jnp.bfloat16, 1)],
        3,
    )
    (result,) = exchange([lane_pieces], [("y", False, "flip")], 5)
    return result


def solution(mesh):
    return jax.shard_map(
        body,
        mesh=mesh,
        in_specs=(
            P("row", "col"),
            P("col", None),
            P(),
            P(),
            P(None, "col"),
            P(),
            P("col", None),
            P("row", "col", None),
            P(),
            P(),
            P(),
            P(),
        ),
        out_specs=P("row", "col"),
        check_vma=False,
    )
```
